512 devices in a mesh: grp: 16 (over x, z_lo, core), mem: 32 (over y, z_hi).
Axes of the slice: x: 4, y: 8, z: 8 (z_hi: 4, z_lo: 2; z = z_hi * 2 + z_lo), core: 2. Of those that a mesh axis runs over, the one named last changes fastest.
Arguments:
- images: bfloat16 [16, 2, 768, 16384], P('grp', None, None, 'mem'), may hold values from -6 to 6
- phantom: bfloat16 [16, 16384], P('grp', 'mem'), may hold values from -12 to 12
- inject_rows: int32 [16, 2, 64], P('grp'), may hold values from 0 to 767
- prior_blocks: int32 [16, 2, 768], P('grp'), may hold values from 0 to 127
- basis: bfloat16 [16384, 512], P('mem'), may hold values from -0.046875 to 0.046875
- refs: bfloat16 [512, 32768], P(None, 'mem'), may hold values from -24 to 24
Outputs:
- new_refs: float32 [512, 32768], P('grp', 'mem')
The draws below stay inside these ranges and needn't reach their ends.
Inputs may be any that keep to these rules, and one draw needn't show every extreme that they name: `inject_rows`: row numbers within a batch; repeats may occur. `prior_blocks`: orientation block numbers; block b holds orientations b * 256 to (b + 1) * 256 - 1.
All inputs are finite; a program needn't handle non-finite values.
Results may differ from the reference program's by a relative error of at most 0.0051.
Values sent between devices are 32-bit elements; how exact they have to be, the bound alone decides.
No kernel may reach another device: no remote copies, remote signals or barrier semaphores. Data moves between devices by JAX's collectives and lax.ppermute only.
A program may use at most 64 MiB of HBM per device.

```python
import math
import jax
import jax.numpy as jnp
import numpy as np
from jax import lax

PARTICLES = 768
BATCHES = 2
PIXELS = 16384
EIGEN = 512
ORIENT = 32768
OBLOCK = 256
INJECTED = 64
GROUPS = 16


def draw_refs(key, part):
    keys = jax.random.split(jax.random.fold_in(key, 11), 1)
    return jnp.clip(jax.random.normal(keys[0], (EIGEN, ORIENT), jnp.float32) * 0.13, -0.8, 0.8).astype(jnp.bfloat16)


def place_ends(result, key, low, largest):
    index_at = [jax.random.randint(jax.random.fold_in(key, axis), (), 0, length) for axis, length in enumerate(result.shape)]
    widest = result.shape.index(max(result.shape))
    beside = index_at[:widest] + [(index_at[widest] + 1) % result.shape[widest]] + index_at[widest + 1:]
    return result.at[tuple(index_at)].set(low).at[tuple(beside)].set(largest)


def block_levels(stream_key, shape, cuts, least, high):
    level, own = 1.0, jax.random.fold_in(stream_key, 6)
    for position, blocks in cuts:
        steps = jnp.exp(jax.random.uniform(jax.random.fold_in(own, position), (blocks,), jnp.float32, least / len(cuts), high / len(cuts)))
        level = level * jnp.repeat(steps, shape[position] // blocks).reshape([-1 if axis == position else 1 for axis in range(len(shape))])
    return level


def cumulative_ranks(amount, slope):
    loads = [(1 << 20) // math.isqrt(rank ** slope) + 1 for rank in range(1, amount + 1)]
    deviation = 1 + sum(loads) // (1 << 30)
    return np.cumsum(np.array([max(1, weight // deviation) for weight in loads]))


def skewed_ids(key, shape, amount, slope):
    grid = cumulative_ranks(amount, slope)
    lot = jax.random.randint(jax.random.fold_in(key, 1), shape, 0, int(grid[amount - 1]))
    rank = jnp.searchsorted(jnp.asarray(grid, jnp.int32), lot, side="right")
    return jax.random.permutation(jax.random.fold_in(key, 2), amount)[rank].astype(jnp.int32)


def centred(stream_key, shape, scale, limit, pieces=(), kind=jnp.bfloat16):
    values = jax.random.normal(stream_key, shape, jnp.float32) * scale
    if len(pieces) > 0:
        values = block_levels(stream_key, shape, pieces, -0.22, 0.18) * values
    return jnp.clip(values, min=-limit, max=limit).astype(kind)


def setup_inputs(seed: int = 0) -> dict:
    key_of = jax.random.split(jax.random.key(seed), 7)
    images = centred(key_of[0], (GROUPS, BATCHES, PARTICLES, PIXELS), 1.0, 6.0, ((0, 16), (3, 32)))
    phantom = centred(key_of[1], (GROUPS, PIXELS), 2.0, 12.0, ((0, 16), (1, 32)))
    inject_rows = place_ends(jax.random.randint(key_of[2], (GROUPS, BATCHES, INJECTED), 0, PARTICLES), jax.random.fold_in(key_of[2], 1), 0, PARTICLES - 1).astype(jnp.int32)
    prior_blocks = place_ends(skewed_ids(key_of[3], (GROUPS, BATCHES, PARTICLES), ORIENT // OBLOCK, 2), jax.random.fold_in(key_of[3], 3), 0, (ORIENT // OBLOCK) - 1).astype(jnp.int32)
    basis = centred(key_of[4], (PIXELS, EIGEN), PIXELS ** -0.5, 0.046875, ((0, 32),))
    refs = draw_refs(jax.random.fold_in(key_of[6], 71), 0)
    return {"images": images, "phantom": phantom, "inject_rows": inject_rows, "prior_blocks": prior_blocks, "basis": basis, "refs": refs}


PRIOR_INCREMENT = 3.0


def reference(images, phantom, inject_rows, prior_blocks, basis, refs):
    positions = jnp.arange(PARTICLES, dtype=jnp.int32)
    orient_block = (jnp.arange(ORIENT, dtype=jnp.int32) // OBLOCK).astype(jnp.int32)

    def per_group(running, inputs):
        totals, masses = running
        group_images, group_phantom, group_rows, group_blocks = inputs
        phantom_coef = jnp.dot(group_phantom, basis, preferred_element_type=jnp.float32)
        for batch_index in range(BATCHES):
            chosen = jnp.any(group_rows[batch_index][:, None] == positions[None, :], axis=0).astype(jnp.float32)
            plain = jnp.dot(group_images[batch_index], basis, preferred_element_type=jnp.float32)
            basis_coefficients = (plain + chosen[:, None] * phantom_coef[None, :]).astype(jnp.bfloat16)
            match_score = (group_blocks[batch_index][:, None] == orient_block[None, :]).astype(jnp.float32)
            score_rows = jnp.dot(basis_coefficients, refs, preferred_element_type=jnp.float32) + PRIOR_INCREMENT * match_score
            row_top = jnp.max(score_rows, axis=1, keepdims=True)
            powers = jnp.exp(score_rows - row_top)
            weights = (powers / jnp.sum(powers, axis=1, keepdims=True)).astype(jnp.bfloat16)
            totals = totals + lax.dot_general(basis_coefficients, weights, (((0,), (0,)), ((), ())), preferred_element_type=jnp.float32)
            masses = masses + jnp.sum(weights.astype(jnp.float32), axis=0)
        return (totals, masses), None

    start = (jnp.zeros((EIGEN, ORIENT), jnp.float32), jnp.zeros((ORIENT,), jnp.float32))
    (totals, masses), unused = lax.scan(per_group, start, (images, phantom, inject_rows, prior_blocks))
    return (totals + refs.astype(jnp.float32)) / (masses[None, :] + 1.0)
```

```python
import jax
import jax.numpy as jnp
from jax import lax
from jax.experimental import pallas as pl
from jax.experimental.pallas import tpu as pltpu
from jax.sharding import Mesh, PartitionSpec as P

OBLOCK = 256
PRIOR_INCREMENT = 3.0
GRP = ("x", "zl", "core")
MEM = ("y", "zh")
LANES = 128


def score_kernel(at, coefs, prior, refs_t, powers, rounded, stats):
    step = pl.program_id(0)
    rows = coefs.shape[1]
    orient = refs_t.shape[0]
    lines = stats.shape[1] // 2
    mine = coefs[...].astype(jnp.bfloat16)
    rounded[...] = mine
    scores = jnp.dot(refs_t[...], mine, preferred_element_type=jnp.float32)
    block = prior[...] - at[0] * (orient // OBLOCK)
    parts = [
        scores[k * OBLOCK : (k + 1) * OBLOCK] + jnp.where(block == k, PRIOR_INCREMENT, 0.0)
        for k in range(orient // OBLOCK)
    ]
    tops = [jnp.max(part, axis=0, keepdims=True) for part in parts]
    top = tops[0]
    for other in tops[1:]:
        top = jnp.maximum(top, other)
    total = jnp.zeros_like(top)
    for k, part in enumerate(parts):
        power = jnp.exp(part - top)
        powers[k * OBLOCK : (k + 1) * OBLOCK, :] = power
        total = total + jnp.sum(power, axis=0, keepdims=True)
    for h in range(rows // LANES):
        line = step * (rows // LANES) + h
        cut = slice(h * LANES, (h + 1) * LANES)
        shape = (stats.shape[0], 1, LANES)
        stats[:, pl.ds(line, 1), :] = jnp.broadcast_to(top[None, :, cut], shape)
        stats[:, pl.ds(lines + line, 1), :] = jnp.broadcast_to(total[None, :, cut], shape)


def scores_of(at, coefs, prior, refs_t, members):
    eigen, rows = coefs.shape
    orient = refs_t.shape[0]
    width = 256
    lines = 2 * rows // LANES
    return pl.pallas_call(
        score_kernel,
        grid_spec=pltpu.PrefetchScalarGridSpec(
            num_scalar_prefetch=1,
            grid=(rows // width,),
            in_specs=[
                pl.BlockSpec((eigen, width), lambda j, at: (0, j)),
                pl.BlockSpec((1, width), lambda j, at: (0, j)),
                pl.BlockSpec((orient, eigen), lambda j, at: (0, 0)),
            ],
            out_specs=[
                pl.BlockSpec((orient, width), lambda j, at: (0, j)),
                pl.BlockSpec((eigen, width), lambda j, at: (0, j)),
                pl.BlockSpec((members, lines, LANES), lambda j, at: (0, 0, 0)),
            ],
        ),
        out_shape=[
            jax.ShapeDtypeStruct((orient, rows), jnp.float32),
            jax.ShapeDtypeStruct((eigen, rows), jnp.bfloat16),
            jax.ShapeDtypeStruct((members, lines, LANES), jnp.float32),
        ],
        compiler_params=pltpu.CompilerParams(vmem_limit_bytes=40 << 20),
        name="scores",
    )(at, coefs, prior, refs_t)


def total_kernel(stats, own, powers, rounded, out, factor):
    step = pl.program_id(0)
    eigen, rows = rounded.shape
    width = powers.shape[0]
    owners = out.shape[0]
    share = eigen // owners
    lines = rows // LANES
    body = out.shape[1] - out.shape[1] % share

    @pl.when(step == 0)
    def _():
        tops = stats[:, :lines, :]
        top = jnp.max(tops, axis=0)
        total = jnp.sum(stats[:, lines:, :] * jnp.exp(tops - top[None]), axis=0)
        scale = jnp.exp(own[0, :lines, :] - top) / total
        for k in range(lines):
            factor[:, k * LANES : (k + 1) * LANES] = scale[k : k + 1, :]

    weights = (powers[...] * factor[...]).astype(jnp.bfloat16)
    contract = (((1,), (1,)), ((), ()))
    totals = lax.dot_general(rounded[...], weights, contract, preferred_element_type=jnp.float32)
    ones = jnp.ones((16, rows), jnp.bfloat16)
    masses = lax.dot_general(ones, weights, contract, preferred_element_type=jnp.float32)
    for h in range(width // LANES):
        column = step * (width // LANES) + h
        cut = slice(h * LANES, (h + 1) * LANES)
        for d in range(owners):
            out[d, pl.ds(pl.multiple_of(column * share, share), share), :] = totals[
                d * share : (d + 1) * share, cut
            ]
        out[:, pl.ds(body + column, 1), :] = jnp.broadcast_to(
            masses[None, 0:1, cut], (owners, 1, LANES)
        )


def totals_of(stats, sent, powers, rounded, owners):
    eigen, rows = rounded.shape
    orient = powers.shape[0]
    width = 256
    deep = (eigen // owners + 1) * (orient // LANES)
    return pl.pallas_call(
        total_kernel,
        grid=(orient // width,),
        in_specs=[
            pl.BlockSpec(stats.shape, lambda j: (0, 0, 0)),
            pl.BlockSpec((1, *sent.shape[1:]), lambda j: (0, 0, 0)),
            pl.BlockSpec((width, rows), lambda j: (j, 0)),
            pl.BlockSpec((eigen, rows), lambda j: (0, 0)),
        ],
        out_specs=pl.BlockSpec((owners, deep, LANES), lambda j: (0, 0, 0)),
        out_shape=jax.ShapeDtypeStruct((owners, deep, LANES), jnp.float32),
        scratch_shapes=[pltpu.VMEM((1, rows), jnp.float32)],
        compiler_params=pltpu.CompilerParams(vmem_limit_bytes=40 << 20),
        name="totals",
    )(stats, sent, powers, rounded)


def final_kernel(at, parts, refs, out):
    share, orient = out.shape
    both = parts[0]
    for d in range(1, parts.shape[0]):
        both = both + parts[d]
    body = share * (orient // LANES)
    for k in range(orient // LANES):
        cut = slice(k * LANES, (k + 1) * LANES)
        above = both[k * share : (k + 1) * share] + refs[:, cut].astype(jnp.float32)
        out[:, cut] = above / (both[body + k : body + k + 1] + 1.0)


def final_of(at, parts, refs):
    owners = parts.shape[0]
    eigen, orient = refs.shape
    share = eigen // owners
    return pl.pallas_call(
        final_kernel,
        grid_spec=pltpu.PrefetchScalarGridSpec(
            num_scalar_prefetch=1,
            grid=(1,),
            in_specs=[
                pl.BlockSpec(parts.shape, lambda j, at: (0, 0, 0)),
                pl.BlockSpec((share, orient), lambda j, at: (at[0], 0)),
            ],
            out_specs=pl.BlockSpec((share, orient), lambda j, at: (0, 0)),
        ),
        out_shape=jax.ShapeDtypeStruct((share, orient), jnp.float32),
        compiler_params=pltpu.CompilerParams(vmem_limit_bytes=40 << 20),
        name="final",
    )(at, parts, refs)


def shifted(x, axis, by):
    size = lax.axis_size(axis)
    return lax.ppermute(x, axis, [(i, (i + by) % size) for i in range(size)])


def sum_at_owner(x, axis):
    size, me = lax.axis_size(axis), lax.axis_index(axis)
    share = x.shape[0] // size
    total = lax.dynamic_slice_in_dim(x, me * share, share, 0)
    for by in range(1, size):
        block = lax.dynamic_slice_in_dim(x, ((me + by) % size) * share, share, 0)
        total = total + shifted(block, axis, by)
    return total


def gathered(x, axis):
    size, me = lax.axis_size(axis), lax.axis_index(axis)
    blocks = [x] + [shifted(x, axis, -by) for by in range(1, size)]
    around = jnp.concatenate(blocks + blocks[:-1])
    return lax.dynamic_slice_in_dim(around, ((size - me) % size) * x.shape[0], size * x.shape[0], 0)


def shards(images, phantom, inject_rows, prior_blocks, basis, refs):
    batches, particles = images.shape[1:3]
    rows = batches * particles
    positions = jnp.arange(particles, dtype=jnp.int32)
    chosen = jnp.any(inject_rows[0][:, :, None] == positions, axis=1)
    contract = (((0,), (1,)), ((), ()))
    plain = lax.dot_general(
        basis, images[0].reshape(rows, -1), contract, preferred_element_type=jnp.float32
    )
    extra = lax.dot_general(basis, phantom, contract, preferred_element_type=jnp.float32)
    partial = plain + extra * chosen.reshape(1, rows).astype(jnp.float32)
    owned = lax.psum_scatter(partial, "y", scatter_dimension=0, tiled=True)
    owned = gathered(sum_at_owner(owned, "zh"), "zh")
    coefs = lax.all_gather(owned, "y", axis=0, tiled=True)
    mem = lax.axis_index(MEM).astype(jnp.int32).reshape(1)
    grp = lax.axis_index(GRP).astype(jnp.int32).reshape(1)
    powers, rounded, sent = scores_of(
        mem, coefs, prior_blocks[0].reshape(1, rows), refs.T, lax.axis_size(MEM)
    )
    stats = lax.all_to_all(sent, MEM, 0, 0, tiled=True)
    parts = totals_of(stats, sent, powers, rounded, lax.axis_size(GRP))
    parts = lax.all_to_all(parts, GRP, 0, 0, tiled=True)
    return final_of(grp, parts, refs)


def solution(mesh):
    fine = Mesh(mesh.devices.reshape(4, 2, 2, 8, 4), GRP + MEM)
    placed = (
        P(GRP, None, None, MEM),
        P(GRP, MEM),
        P(GRP, None, None),
        P(GRP, None, None),
        P(MEM, None),
        P(None, MEM),
    )
    return jax.shard_map(
        shards, mesh=fine, in_specs=placed, out_specs=P(GRP, MEM), check_vma=False
    )
```

```python
import jax
import jax.numpy as jnp
from jax import lax
from jax.experimental import pallas as pl
from jax.experimental.pallas import tpu as pltpu
from jax.sharding import Mesh, PartitionSpec as P

OBLOCK = 256
PRIOR_INCREMENT = 3.0
GRP = ("x", "zl", "core")
MEM = ("yh", "yl", "zh")
RING = ("yh", "yl")
ALIKE = ("yh", "zh")
PEERS = ("x", "zl")
LANES = 128
BIG = pltpu.CompilerParams(vmem_limit_bytes=40 << 20)
LAST = (((1,), (1,)), ((), ()))


def project_kernel(inject, images, half, phantom, out_a, out_b):
    step = pl.program_id(0)
    width = images.shape[0]
    per_batch = 2
    injected = inject.shape[1]
    batch, part = step // per_batch, step % per_batch
    position = part * width + lax.broadcasted_iota(jnp.int32, (1, width), 1)
    hit = jnp.zeros((1, width), jnp.float32)
    for i in range(injected):
        hit = jnp.where(position == inject[batch, i], 1.0, hit)
    mine = half[...]
    plain = lax.dot_general(mine, images[...], LAST, preferred_element_type=jnp.float32)
    spread = jnp.broadcast_to(phantom[...], (LANES, phantom.shape[1]))
    extra = lax.dot_general(mine, spread, LAST, preferred_element_type=jnp.float32)
    middle = out_a.shape[0]
    for k in range(width // LANES):
        cut = slice(k * LANES, (k + 1) * LANES)
        value = plain[:, cut] + extra * hit[:, cut]
        out_a[:, cut] = value[:middle]
        out_b[:, cut] = value[middle:]


def projected(inject, images, half, phantom):
    rows, pixels = images.shape
    batches = inject.shape[0]
    width = rows // (2 * batches)
    count = half.shape[0]
    out = jax.ShapeDtypeStruct((count // 2, rows), jnp.float32)
    return pl.pallas_call(
        project_kernel,
        grid_spec=pltpu.PrefetchScalarGridSpec(
            num_scalar_prefetch=1,
            grid=(2 * batches,),
            in_specs=[
                pl.BlockSpec((width, pixels), lambda j, s: (j, 0)),
                pl.BlockSpec((count, pixels), lambda j, s: (0, 0)),
                pl.BlockSpec((1, pixels), lambda j, s: (0, 0)),
            ],
            out_specs=[pl.BlockSpec((count // 2, width), lambda j, s: (0, j))] * 2,
        ),
        out_shape=[out, out],
        compiler_params=BIG,
        name="project",
    )(inject, images, half, phantom)


def join_kernel(keep_a, keep_b, came_a, came_b, out):
    for q in range(out.shape[0]):
        cut = slice(q * 8, (q + 1) * 8)
        out[q, :8, :] = keep_a[cut, :] + came_a[cut, :]
        out[q, 8:, :] = keep_b[cut, :] + came_b[cut, :]


def joined(keep, came):
    high, rows = keep[0].shape
    steps = 4
    members = high // 8
    return pl.pallas_call(
        join_kernel,
        grid=(steps,),
        in_specs=[pl.BlockSpec((high // steps, rows), lambda j: (j, 0))] * 4,
        out_specs=pl.BlockSpec((members // steps, 16, rows), lambda j: (j, 0, 0)),
        out_shape=jax.ShapeDtypeStruct((members, 16, rows), jnp.float32),
        compiler_params=BIG,
        name="join",
    )(*keep, *came)


def spread_kernel(parts, out):
    total = parts[0]
    for k in range(1, parts.shape[0]):
        total = total + parts[k]
    for k in range(out.shape[0]):
        out[k] = total


def summed_copies(parts):
    members, high, rows = parts.shape
    steps = 4
    block = pl.BlockSpec((members, high, rows // steps), lambda j: (0, 0, j))
    return pl.pallas_call(
        spread_kernel,
        grid=(steps,),
        in_specs=[block],
        out_specs=block,
        out_shape=jax.ShapeDtypeStruct(parts.shape, jnp.float32),
        compiler_params=BIG,
        name="spread",
    )(parts)


def score_kernel(at, own_a, own_b, came_a, came_b, prior, refs_t, powers, rounded, stats):
    step = pl.program_id(0)
    rows = prior.shape[1]
    orient, eigen = refs_t.shape
    lines = stats.shape[1] // 2
    high = eigen // 4
    for base, held in ((0, (own_a, came_a)), (2 * high, (own_b, came_b))):
        for side, source in enumerate(held):
            place = base + high * (at[1] if side == 0 else 1 - at[1])
            rounded[pl.ds(pl.multiple_of(place, high), high), :] = (
                source[...].reshape(high, rows).astype(jnp.bfloat16)
            )
    scores = jnp.dot(refs_t[...], rounded[...], preferred_element_type=jnp.float32)
    block = prior[...] - at[0] * (orient // OBLOCK)
    parts = [
        scores[k * OBLOCK : (k + 1) * OBLOCK] + jnp.where(block == k, PRIOR_INCREMENT, 0.0)
        for k in range(orient // OBLOCK)
    ]
    tops = [jnp.max(part, axis=0, keepdims=True) for part in parts]
    top = tops[0]
    for other in tops[1:]:
        top = jnp.maximum(top, other)
    total = jnp.zeros_like(top)
    for k, part in enumerate(parts):
        power = jnp.exp(part - top)
        powers[k * OBLOCK : (k + 1) * OBLOCK, :] = power
        total = total + jnp.sum(power, axis=0, keepdims=True)
    for h in range(rows // LANES):
        line = step * (rows // LANES) + h
        cut = slice(h * LANES, (h + 1) * LANES)
        shape = (stats.shape[0], 1, LANES)
        stats[:, pl.ds(line, 1), :] = jnp.broadcast_to(top[None, :, cut], shape)
        stats[:, pl.ds(lines + line, 1), :] = jnp.broadcast_to(total[None, :, cut], shape)


def scores_of(at, own, came, prior, refs_t, members):
    rows = prior.shape[1]
    orient, eigen = refs_t.shape
    width = 256
    lines = 2 * rows // LANES
    group = own.shape[0]
    return pl.pallas_call(
        score_kernel,
        grid_spec=pltpu.PrefetchScalarGridSpec(
            num_scalar_prefetch=1,
            grid=(rows // width,),
            in_specs=[
                pl.BlockSpec((group, 8, width), lambda j, at: (0, 0, j)),
                pl.BlockSpec((group, 8, width), lambda j, at: (0, 1, j)),
                pl.BlockSpec((group, 8, width), lambda j, at: (0, 0, j)),
                pl.BlockSpec((group, 8, width), lambda j, at: (0, 0, j)),
                pl.BlockSpec((1, width), lambda j, at: (0, j)),
                pl.BlockSpec((orient, eigen), lambda j, at: (0, 0)),
            ],
            out_specs=[
                pl.BlockSpec((orient, width), lambda j, at: (0, j)),
                pl.BlockSpec((eigen, width), lambda j, at: (0, j)),
                pl.BlockSpec((members, lines, LANES), lambda j, at: (0, 0, 0)),
            ],
        ),
        out_shape=[
            jax.ShapeDtypeStruct((orient, rows), jnp.float32),
            jax.ShapeDtypeStruct((eigen, rows), jnp.bfloat16),
            jax.ShapeDtypeStruct((members, lines, LANES), jnp.float32),
        ],
        compiler_params=BIG,
        name="scores",
    )(at, own, own, *came, prior, refs_t)


def total_kernel(at, stats, own, powers, rounded, keep, send, factor):
    step = pl.program_id(0)
    eigen, rows = rounded.shape
    width = powers.shape[0]
    peers = keep.shape[0]
    share = eigen // (2 * peers)
    lines = rows // LANES
    body = keep.shape[1] - keep.shape[1] % share

    @pl.when(step == 0)
    def _():
        tops = stats[:, :lines, :]
        top = jnp.max(tops, axis=0)
        total = jnp.sum(stats[:, lines:, :] * jnp.exp(tops - top[None]), axis=0)
        scale = jnp.exp(own[0, :lines, :] - top) / total
        for k in range(lines):
            factor[:, k * LANES : (k + 1) * LANES] = scale[k : k + 1, :]

    weights = (powers[...] * factor[...]).astype(jnp.bfloat16)
    totals = lax.dot_general(rounded[...], weights, LAST, preferred_element_type=jnp.float32)
    ones = jnp.ones((16, rows), jnp.bfloat16)
    masses = lax.dot_general(ones, weights, LAST, preferred_element_type=jnp.float32)
    first = at[2] == 0
    for h in range(width // LANES):
        column = step * (width // LANES) + h
        cut = slice(h * LANES, (h + 1) * LANES)
        place = pl.ds(pl.multiple_of(column * share, share), share)
        for q in range(peers):
            even = totals[2 * q * share : (2 * q + 1) * share, cut]
            odd = totals[(2 * q + 1) * share : (2 * q + 2) * share, cut]
            keep[q, place, :] = jnp.where(first, even, odd)
            send[q, place, :] = jnp.where(first, odd, even)
        mass = jnp.broadcast_to(masses[None, 0:1, cut], (peers, 1, LANES))
        keep[:, pl.ds(body + column, 1), :] = mass
        send[:, pl.ds(body + column, 1), :] = mass


def totals_of(at, stats, sent, powers, rounded, peers):
    eigen, rows = rounded.shape
    orient = powers.shape[0]
    width = 256
    deep = (eigen // (2 * peers) + 1) * (orient // LANES)
    out = jax.ShapeDtypeStruct((peers, deep, LANES), jnp.float32)
    return pl.pallas_call(
        total_kernel,
        grid_spec=pltpu.PrefetchScalarGridSpec(
            num_scalar_prefetch=1,
            grid=(orient // width,),
            in_specs=[
                pl.BlockSpec(stats.shape, lambda j, at: (0, 0, 0)),
                pl.BlockSpec((1, *sent.shape[1:]), lambda j, at: (0, 0, 0)),
                pl.BlockSpec((width, rows), lambda j, at: (j, 0)),
                pl.BlockSpec((eigen, rows), lambda j, at: (0, 0)),
            ],
            out_specs=[pl.BlockSpec((peers, deep, LANES), lambda j, at: (0, 0, 0))] * 2,
            scratch_shapes=[pltpu.VMEM((1, rows), jnp.float32)],
        ),
        out_shape=[out, out],
        compiler_params=BIG,
        name="totals",
    )(at, stats, sent, powers, rounded)


def final_kernel(at, parts, refs, out):
    share, orient = out.shape
    both = parts[0]
    for d in range(1, parts.shape[0]):
        both = both + parts[d]
    body = share * (orient // LANES)
    for k in range(orient // LANES):
        cut = slice(k * LANES, (k + 1) * LANES)
        above = both[k * share : (k + 1) * share] + refs[:, cut].astype(jnp.float32)
        out[:, cut] = above / (both[body + k : body + k + 1] + 1.0)


def final_of(at, parts, refs):
    eigen, orient = refs.shape
    share = eigen // (2 * parts.shape[0])
    return pl.pallas_call(
        final_kernel,
        grid_spec=pltpu.PrefetchScalarGridSpec(
            num_scalar_prefetch=1,
            grid=(1,),
            in_specs=[
                pl.BlockSpec(parts.shape, lambda j, at: (0, 0, 0)),
                pl.BlockSpec((share, orient), lambda j, at: (at[3], 0)),
            ],
            out_specs=pl.BlockSpec((share, orient), lambda j, at: (0, 0)),
        ),
        out_shape=jax.ShapeDtypeStruct((share, orient), jnp.float32),
        compiler_params=BIG,
        name="final",
    )(at, parts, refs)


def swapped(pair):
    size = lax.axis_size(RING)
    with_a = [(i, i ^ 1) for i in range(size)]
    with_b = [(i, (i + (1 if i % 2 else -1)) % size) for i in range(size)]
    return tuple(lax.ppermute(x, RING, p) for x, p in zip(pair, (with_a, with_b)))


def shards(images, phantom, inject_rows, prior_blocks, basis, refs):
    rows = images.shape[1] * images.shape[2]
    pixels, eigen = basis.shape
    flat = images[0].reshape(rows, pixels)
    parity = lax.axis_index("yl").astype(jnp.int32)
    at = jnp.stack(
        [
            lax.axis_index(MEM).astype(jnp.int32),
            parity,
            lax.axis_index("core").astype(jnp.int32),
            lax.axis_index(GRP).astype(jnp.int32),
        ]
    )
    halves = basis.T.reshape(2, 2, eigen // 4, pixels)

    def half(side):
        chosen = lax.dynamic_index_in_dim(halves, side, 1, keepdims=False)
        return projected(inject_rows[0], flat, chosen.reshape(eigen // 2, pixels), phantom)

    came = swapped(half(1 - parity))
    parts = joined(half(parity), came)
    parts = lax.all_to_all(parts, ALIKE, 0, 0, tiled=True)
    own = lax.all_to_all(summed_copies(parts), ALIKE, 0, 0, tiled=True)
    came = swapped((own[:, :8], own[:, 8:]))
    powers, rounded, sent = scores_of(
        at, own, came, prior_blocks[0].reshape(1, rows), refs.T, lax.axis_size(MEM)
    )
    stats = lax.all_to_all(sent, MEM, 0, 0, tiled=True)
    keep, send = totals_of(at, stats, sent, powers, rounded, lax.axis_size(PEERS))
    parts = keep + lax.ppermute(send, "core", [(0, 1), (1, 0)])
    parts = lax.all_to_all(parts, PEERS, 0, 0, tiled=True)
    return final_of(at, parts, refs)


def solution(mesh):
    fine = Mesh(mesh.devices.reshape(4, 2, 2, 4, 2, 4), GRP + MEM)
    placed = (
        P(GRP, None, None, MEM),
        P(GRP, MEM),
        P(GRP, None, None),
        P(GRP, None, None),
        P(MEM, None),
        P(None, MEM),
    )
    return jax.shard_map(
        shards, mesh=fine, in_specs=placed, out_specs=P(GRP, MEM), check_vma=False
    )
```

```python
import jax
import jax.numpy as jnp
from jax import lax
from jax.experimental import pallas as pl
from jax.experimental.pallas import tpu as pltpu
from jax.sharding import Mesh, PartitionSpec as P

OBLOCK = 256
PRIOR_INCREMENT = 3.0
GRP = ("x", "zl", "core")
RING = ("yh", "yl")
TALL = ("zhh", "zhl")
MEM = RING + TALL
ALIKE = ("yh", "zhh")
PEERS = ("x", "zl")
LANES = 128
BIG = pltpu.CompilerParams(vmem_limit_bytes=40 << 20)
LAST = (((1,), (1,)), ((), ()))


def project_kernel(at, inject, images, basis, phantom, out_a, out_b):
    step = pl.program_id(0)
    width = images.shape[0]
    per_batch = pl.num_programs(0) // inject.shape[0]
    batch, part = step // per_batch, step % per_batch
    position = part * width + lax.broadcasted_iota(jnp.int32, (1, width), 1)
    hit = jnp.zeros((1, width), jnp.float32)
    for i in range(inject.shape[1]):
        hit = jnp.where(position == inject[batch, i], 1.0, hit)
    mine = basis[...].T
    plain = lax.dot_general(mine, images[...], LAST, preferred_element_type=jnp.float32)
    spread = jnp.broadcast_to(phantom[...], (LANES, phantom.shape[1]))
    extra = lax.dot_general(mine, spread, LAST, preferred_element_type=jnp.float32)
    middle = out_a.shape[0]
    for k in range(width // LANES):
        cut = slice(k * LANES, (k + 1) * LANES)
        value = plain[:, cut] + extra * hit[:, cut]
        out_a[:, cut] = value[:middle]
        out_b[:, cut] = value[middle:]


def projected(at, which, inject, images, basis, phantom):
    rows, pixels = images.shape
    batches = inject.shape[0]
    width = rows // (2 * batches)
    count = basis.shape[1] // 4
    out = jax.ShapeDtypeStruct((count // 2, rows), jnp.float32)
    return pl.pallas_call(
        project_kernel,
        grid_spec=pltpu.PrefetchScalarGridSpec(
            num_scalar_prefetch=2,
            grid=(2 * batches,),
            in_specs=[
                pl.BlockSpec((width, pixels), lambda j, at, s: (j, 0)),
                pl.BlockSpec((pixels, count), lambda j, at, s: (0, at[which])),
                pl.BlockSpec((1, pixels), lambda j, at, s: (0, 0)),
            ],
            out_specs=[pl.BlockSpec((count // 2, width), lambda j, at, s: (0, j))] * 2,
        ),
        out_shape=[out, out],
        compiler_params=BIG,
        name="project",
    )(at, inject, images, basis, phantom)


def relay_kernel(here_a, here_b, came_a, came_b, low, high):
    members = low.shape[0]
    for side, out in enumerate((low, high)):
        for q in range(members):
            cut = slice((side * members + q) * 8, (side * members + q + 1) * 8)
            out[q, :8, :] = here_a[cut, :] + came_a[cut, :]
            out[q, 8:, :] = here_b[cut, :] + came_b[cut, :]


def relayed(here, came):
    count, rows = here[0].shape
    width = rows // 3
    members = count // 8
    out = jax.ShapeDtypeStruct((members // 2, 16, rows), jnp.float32)
    return pl.pallas_call(
        relay_kernel,
        grid=(rows // width,),
        in_specs=[pl.BlockSpec((count, width), lambda j: (0, j))] * 4,
        out_specs=[pl.BlockSpec((members // 2, 16, width), lambda j: (0, 0, j))] * 2,
        out_shape=[out, out],
        compiler_params=BIG,
        name="relay",
    )(*here, *came)


def join_kernel(here_a, here_b, came_a, came_b, low, high, out):
    members = low.shape[0]
    for side, other in enumerate((low, high)):
        for q in range(members):
            m = side * members + q
            cut = slice(m * 8, (m + 1) * 8)
            out[m, :8, :] = here_a[cut, :] + came_a[cut, :] + other[q, :8, :]
            out[m, 8:, :] = here_b[cut, :] + came_b[cut, :] + other[q, 8:, :]


def joined(here, came, others):
    count, rows = here[0].shape
    width = rows // 3
    members = count // 8
    return pl.pallas_call(
        join_kernel,
        grid=(rows // width,),
        in_specs=[pl.BlockSpec((count, width), lambda j: (0, j))] * 4
        + [pl.BlockSpec((members // 2, 16, width), lambda j: (0, 0, j))] * 2,
        out_specs=pl.BlockSpec((members, 16, width), lambda j: (0, 0, j)),
        out_shape=jax.ShapeDtypeStruct((members, 16, rows), jnp.float32),
        compiler_params=BIG,
        name="join",
    )(*here, *came, *others)


def spread_kernel(parts, out):
    total = parts[0]
    for k in range(1, parts.shape[0]):
        total = total + parts[k]
    for k in range(out.shape[0]):
        out[k] = total


def summed_copies(parts):
    members, high, rows = parts.shape
    steps = 3
    block = pl.BlockSpec((members, high, rows // steps), lambda j: (0, 0, j))
    return pl.pallas_call(
        spread_kernel,
        grid=(steps,),
        in_specs=[block],
        out_specs=block,
        out_shape=jax.ShapeDtypeStruct(parts.shape, jnp.float32),
        compiler_params=BIG,
        name="spread",
    )(parts)


def peel_kernel(low, high, out_a, out_b):
    middle = low.shape[0]
    for offset, source in ((0, low), (middle, high)):
        out_a[offset : offset + middle] = source[:, :8, :]
        out_b[offset : offset + middle] = source[:, 8:, :]


def peeled(low, high):
    members, _, rows = low.shape
    width = rows // 3
    out = jax.ShapeDtypeStruct((2 * members, 8, rows), jnp.float32)
    return pl.pallas_call(
        peel_kernel,
        grid=(rows // width,),
        in_specs=[pl.BlockSpec((members, 16, width), lambda j: (0, 0, j))] * 2,
        out_specs=[pl.BlockSpec((2 * members, 8, width), lambda j: (0, 0, j))] * 2,
        out_shape=[out, out],
        compiler_params=BIG,
        name="peel",
    )(low, high)


def score_kernel(
    at, own, low, high, near_a, near_b, far_a, far_b, prior, refs_t, powers, rounded, stats
):
    step = pl.program_id(0)
    rows = prior.shape[1]
    orient, eigen = refs_t.shape
    lines = stats.shape[1] // 2
    half = eigen // 8
    quarter = half // 2

    def put(which, offset, block):
        count = block.shape[0] * block.shape[1]
        place = pl.multiple_of(at[which] * 2 * half + offset, quarter)
        rounded[pl.ds(place, count), :] = block.reshape(count, rows).astype(jnp.bfloat16)

    put(0, 0, far_a[...])
    put(0, half, far_b[...])
    put(1, 0, near_a[...])
    put(1, half, near_b[...])
    for offset, source in ((0, low), (quarter, high)):
        put(2, offset, source[:, :8, :])
        put(2, half + offset, source[:, 8:, :])
    put(3, 0, own[:, :8, :])
    put(3, half, own[:, 8:, :])
    scores = jnp.dot(refs_t[...], rounded[...], preferred_element_type=jnp.float32)
    block = prior[...] - at[4] * (orient // OBLOCK)
    parts = [
        scores[k * OBLOCK : (k + 1) * OBLOCK] + jnp.where(block == k, PRIOR_INCREMENT, 0.0)
        for k in range(orient // OBLOCK)
    ]
    tops = [jnp.max(part, axis=0, keepdims=True) for part in parts]
    top = tops[0]
    for other in tops[1:]:
        top = jnp.maximum(top, other)
    total = jnp.zeros_like(top)
    for k, part in enumerate(parts):
        power = jnp.exp(part - top)
        powers[k * OBLOCK : (k + 1) * OBLOCK, :] = power
        total = total + jnp.sum(power, axis=0, keepdims=True)
    for h in range(rows // LANES):
        line = step * (rows // LANES) + h
        cut = slice(h * LANES, (h + 1) * LANES)
        shape = (stats.shape[0], 1, LANES)
        stats[:, pl.ds(line, 1), :] = jnp.broadcast_to(top[None, :, cut], shape)
        stats[:, pl.ds(lines + line, 1), :] = jnp.broadcast_to(total[None, :, cut], shape)


def scores_of(at, held, prior, refs_t, members):
    rows = prior.shape[1]
    orient, eigen = refs_t.shape
    width = 256
    lines = 2 * rows // LANES
    return pl.pallas_call(
        score_kernel,
        grid_spec=pltpu.PrefetchScalarGridSpec(
            num_scalar_prefetch=1,
            grid=(rows // width,),
            in_specs=[pl.BlockSpec((*x.shape[:2], width), lambda j, at: (0, 0, j)) for x in held]
            + [
                pl.BlockSpec((1, width), lambda j, at: (0, j)),
                pl.BlockSpec((orient, eigen), lambda j, at: (0, 0)),
            ],
            out_specs=[
                pl.BlockSpec((orient, width), lambda j, at: (0, j)),
                pl.BlockSpec((eigen, width), lambda j, at: (0, j)),
                pl.BlockSpec((members, lines, LANES), lambda j, at: (0, 0, 0)),
            ],
        ),
        out_shape=[
            jax.ShapeDtypeStruct((orient, rows), jnp.float32),
            jax.ShapeDtypeStruct((eigen, rows), jnp.bfloat16),
            jax.ShapeDtypeStruct((members, lines, LANES), jnp.float32),
        ],
        compiler_params=BIG,
        name="scores",
    )(at, *held, prior, refs_t)


def total_kernel(at, stats, own, powers, rounded, keep, send, factor):
    step = pl.program_id(0)
    eigen, rows = rounded.shape
    width = powers.shape[0]
    peers = keep.shape[0]
    share = eigen // (2 * peers)
    lines = rows // LANES
    body = keep.shape[1] - keep.shape[1] % share

    @pl.when(step == 0)
    def _():
        tops = stats[:, :lines, :]
        top = jnp.max(tops, axis=0)
        total = jnp.sum(stats[:, lines:, :] * jnp.exp(tops - top[None]), axis=0)
        scale = jnp.exp(own[0, :lines, :] - top) / total
        for k in range(lines):
            factor[:, k * LANES : (k + 1) * LANES] = scale[k : k + 1, :]

    weights = (powers[...] * factor[...]).astype(jnp.bfloat16)
    totals = lax.dot_general(rounded[...], weights, LAST, preferred_element_type=jnp.float32)
    ones = jnp.ones((16, rows), jnp.bfloat16)
    masses = lax.dot_general(ones, weights, LAST, preferred_element_type=jnp.float32)
    first = at[5] == 0
    for h in range(width // LANES):
        column = step * (width // LANES) + h
        cut = slice(h * LANES, (h + 1) * LANES)
        place = pl.ds(pl.multiple_of(column * share, share), share)
        for q in range(peers):
            even = totals[2 * q * share : (2 * q + 1) * share, cut]
            odd = totals[(2 * q + 1) * share : (2 * q + 2) * share, cut]
            keep[q, place, :] = jnp.where(first, even, odd)
            send[q, place, :] = jnp.where(first, odd, even)
        mass = jnp.broadcast_to(masses[None, 0:1, cut], (peers, 1, LANES))
        keep[:, pl.ds(body + column, 1), :] = mass
        send[:, pl.ds(body + column, 1), :] = mass


def totals_of(at, stats, sent, powers, rounded, peers):
    eigen, rows = rounded.shape
    orient = powers.shape[0]
    width = 256
    deep = (eigen // (2 * peers) + 1) * (orient // LANES)
    out = jax.ShapeDtypeStruct((peers, deep, LANES), jnp.float32)
    return pl.pallas_call(
        total_kernel,
        grid_spec=pltpu.PrefetchScalarGridSpec(
            num_scalar_prefetch=1,
            grid=(orient // width,),
            in_specs=[
                pl.BlockSpec(stats.shape, lambda j, at: (0, 0, 0)),
                pl.BlockSpec((1, *sent.shape[1:]), lambda j, at: (0, 0, 0)),
                pl.BlockSpec((width, rows), lambda j, at: (j, 0)),
                pl.BlockSpec((eigen, rows), lambda j, at: (0, 0)),
            ],
            out_specs=[pl.BlockSpec((peers, deep, LANES), lambda j, at: (0, 0, 0))] * 2,
            scratch_shapes=[pltpu.VMEM((1, rows), jnp.float32)],
        ),
        out_shape=[out, out],
        compiler_params=BIG,
        name="totals",
    )(at, stats, sent, powers, rounded)


def final_kernel(at, parts, refs, out):
    share, orient = out.shape
    both = parts[0]
    for d in range(1, parts.shape[0]):
        both = both + parts[d]
    body = share * (orient // LANES)
    for k in range(orient // LANES):
        cut = slice(k * LANES, (k + 1) * LANES)
        above = both[k * share : (k + 1) * share] + refs[:, cut].astype(jnp.float32)
        out[:, cut] = above / (both[body + k : body + k + 1] + 1.0)


def final_of(at, parts, refs):
    eigen, orient = refs.shape
    share = eigen // (2 * parts.shape[0])
    return pl.pallas_call(
        final_kernel,
        grid_spec=pltpu.PrefetchScalarGridSpec(
            num_scalar_prefetch=1,
            grid=(1,),
            in_specs=[
                pl.BlockSpec(parts.shape, lambda j, at: (0, 0, 0)),
                pl.BlockSpec((share, orient), lambda j, at: (at[6], 0)),
            ],
            out_specs=pl.BlockSpec((share, orient), lambda j, at: (0, 0)),
        ),
        out_shape=jax.ShapeDtypeStruct((share, orient), jnp.float32),
        compiler_params=BIG,
        name="final",
    )(at, parts, refs)


def swapped(pair, axis):
    size = lax.axis_size(axis)
    with_a = [(i, i ^ 1) for i in range(size)]
    with_b = [(i, (i + (1 if i % 2 else -1)) % size) for i in range(size)]
    return tuple(lax.ppermute(x, axis, p) for x, p in zip(pair, (with_a, with_b)))


def shards(images, phantom, inject_rows, prior_blocks, basis, refs):
    rows = images.shape[1] * images.shape[2]
    flat = images[0].reshape(rows, basis.shape[0])
    p, q = lax.axis_index("yl"), lax.axis_index("zhl")
    at = jnp.stack(
        [
            (1 - p) * 2 + 1 - q,
            (1 - p) * 2 + q,
            p * 2 + 1 - q,
            p * 2 + q,
            lax.axis_index(MEM),
            lax.axis_index("core"),
            lax.axis_index(GRP),
        ]
    ).astype(jnp.int32)
    blocks = [projected(at, k, inject_rows[0], flat, basis, phantom) for k in range(4)]

    through = swapped(blocks[0], RING)
    came = swapped(blocks[1], RING)
    others = swapped(relayed(blocks[2], through), TALL)
    parts = joined(blocks[3], came, others)
    parts = lax.all_to_all(parts, ALIKE, 0, 0, tiled=True)
    own = lax.all_to_all(summed_copies(parts), ALIKE, 0, 0, tiled=True)
    middle = own.shape[0] // 2
    low, high = swapped((own[:middle], own[middle:]), TALL)
    near = swapped((own[:, :8], own[:, 8:]), RING)
    far = swapped(peeled(low, high), RING)
    powers, rounded, sent = scores_of(
        at,
        (own, low, high, *near, *far),
        prior_blocks[0].reshape(1, rows),
        refs.T,
        lax.axis_size(MEM),
    )
    stats = lax.all_to_all(sent, MEM, 0, 0, tiled=True)
    keep, send = totals_of(at, stats, sent, powers, rounded, lax.axis_size(PEERS))
    parts = keep + lax.ppermute(send, "core", [(0, 1), (1, 0)])
    parts = lax.all_to_all(parts, PEERS, 0, 0, tiled=True)
    return final_of(at, parts, refs)


def solution(mesh):
    fine = Mesh(mesh.devices.reshape(4, 2, 2, 4, 2, 2, 2), GRP + MEM)
    placed = (
        P(GRP, None, None, MEM),
        P(GRP, MEM),
        P(GRP, None, None),
        P(GRP, None, None),
        P(MEM, None),
        P(None, MEM),
    )
    return jax.shard_map(
        shards, mesh=fine, in_specs=placed, out_specs=P(GRP, MEM), check_vma=False
    )
```

```python
import jax
import jax.numpy as jnp
from jax import lax
from jax.experimental import pallas as pl
from jax.experimental.pallas import tpu as pltpu
from jax.sharding import Mesh, PartitionSpec as P

OBLOCK = 256
PRIOR_INCREMENT = 3.0
GRP = ("x", "zl", "core")
RING = ("yh", "yl")
TALL = ("zhh", "zhl")
MEM = RING + TALL
ALIKE = ("yh", "zhh")
PEERS = ("x", "zl")
LANES = 128
BIG = pltpu.CompilerParams(vmem_limit_bytes=28 << 20)
SMALL = pltpu.CompilerParams(vmem_limit_bytes=14 << 20)
LAST = (((1,), (1,)), ((), ()))


def project_kernel(at, inject, images, basis, phantom, *rest):
    outs, (pixels_in, columns, ghost, sems) = rest[:-4], rest[-4:]
    which = pixels_in.shape[0]
    width = pixels_in.shape[1]
    count = columns.shape[1]
    first = pl.multiple_of(at[0] * count, count)
    loads = [
        pltpu.make_async_copy(basis.at[:, pl.ds(first, count)], columns, sems.at[which]),
        pltpu.make_async_copy(phantom, ghost, sems.at[which + 1]),
    ] + [
        pltpu.make_async_copy(images.at[pl.ds(k * width, width), :], pixels_in.at[k], sems.at[k])
        for k in range(which)
    ]
    for load in loads:
        load.start()
    per_batch = which // inject.shape[0]
    hits = []
    for k in range(which):
        position = (k % per_batch) * width + lax.broadcasted_iota(jnp.int32, (1, width), 1)
        hit = jnp.zeros((1, width), jnp.float32)
        for i in range(inject.shape[1]):
            hit = jnp.where(position == inject[k // per_batch, i], 1.0, hit)
        hits.append(hit)
    loads[0].wait()
    loads[1].wait()
    mine = columns[...].T
    spread = jnp.broadcast_to(ghost[...], (LANES, ghost.shape[1]))
    extra = lax.dot_general(mine, spread, LAST, preferred_element_type=jnp.float32)
    share = count // len(outs)
    for k in range(which):
        loads[2 + k].wait()
        plain = lax.dot_general(mine, pixels_in[k], LAST, preferred_element_type=jnp.float32)
        for c in range(width // LANES):
            cut = slice(c * LANES, (c + 1) * LANES)
            value = plain[:, cut] + extra * hits[k][:, cut]
            for j, out in enumerate(outs):
                out[:, k * width + c * LANES : k * width + (c + 1) * LANES] = value[
                    j * share : (j + 1) * share
                ]


def projected(block, inject, images, basis, phantom, pieces):
    rows, pixels = images.shape
    steps = 2 * inject.shape[0]
    count = basis.shape[1] // 4
    out = jax.ShapeDtypeStruct((count // pieces, rows), jnp.float32)
    images, basis, phantom = (
        pltpu.with_memory_space_constraint(x, pltpu.HBM) for x in (images, basis, phantom)
    )
    found = pl.pallas_call(
        project_kernel,
        grid_spec=pltpu.PrefetchScalarGridSpec(
            num_scalar_prefetch=2,
            grid=(1,),
            in_specs=[pl.BlockSpec(memory_space=pltpu.HBM)] * 3,
            out_specs=[pl.BlockSpec(out.shape, lambda j, at, s: (0, 0))] * pieces,
            scratch_shapes=[
                pltpu.VMEM((steps, rows // steps, pixels), images.dtype),
                pltpu.VMEM((pixels, count), basis.dtype),
                pltpu.VMEM((1, pixels), phantom.dtype),
                pltpu.SemaphoreType.DMA((steps + 2,)),
            ],
        ),
        out_shape=[out] * pieces,
        compiler_params=SMALL,
        name="project",
    )(block, inject, images, basis, phantom)
    return tuple(found)


def relay_kernel(at, tall, wide, came_y, came_a, came_b, to_a, to_b, to_y, left, right):
    p, q = at[0], at[1]
    piece = to_a.shape[0]
    for s, (out, came) in enumerate(((to_a, came_a), (to_b, came_b))):
        base = 2 * s * piece
        here = pl.ds(pl.multiple_of(base + q * piece, piece), piece)
        there = pl.ds(pl.multiple_of(base + (1 - q) * piece, piece), piece)
        out[...] = tall[there, :] + came_y[there, :]
        left[s * piece : (s + 1) * piece, :] = tall[here, :] + came_y[here, :]
        for spot, side in ((right, p), (to_y, 1 - p)):
            inner = pl.multiple_of(side * piece, piece)
            spot[s * piece : (s + 1) * piece, :] = (
                wide[pl.ds(pl.multiple_of(base + side * piece, piece), piece), :]
                + came[pl.ds(inner, piece), :]
            )


def relayed(at, tall, wide, came_y, came_z):
    count, rows = tall.shape
    width = rows // 3

    def spec(high):
        return pl.BlockSpec((high, width), lambda j, at: (0, j))

    highs = (count // 4, count // 4, count // 2, count // 2, count // 2)
    return pl.pallas_call(
        relay_kernel,
        grid_spec=pltpu.PrefetchScalarGridSpec(
            num_scalar_prefetch=1,
            grid=(rows // width,),
            in_specs=[spec(x.shape[0]) for x in (tall, wide, came_y, *came_z)],
            out_specs=[spec(high) for high in highs],
        ),
        out_shape=[jax.ShapeDtypeStruct((high, rows), jnp.float32) for high in highs],
        compiler_params=SMALL,
        name="relay",
    )(at, tall, wide, came_y, *came_z)


def join_kernel(left, right, came_a, came_b, came_y, out):
    members = out.shape[0]
    for m in range(members):
        cut = slice(m * 8, (m + 1) * 8)
        source = (came_a, came_b)[m // (members // 2)]
        inner = (m % (members // 2)) * 8
        out[m, :8, :] = left[cut, :] + source[inner : inner + 8, :]
        out[m, 8:, :] = right[cut, :] + came_y[cut, :]


def joined(left, right, came_z, came_y):
    count, rows = left.shape
    width = rows // 3
    operands = (left, right, *came_z, came_y)
    return pl.pallas_call(
        join_kernel,
        grid=(rows // width,),
        in_specs=[pl.BlockSpec((x.shape[0], width), lambda j: (0, j)) for x in operands],
        out_specs=pl.BlockSpec((count // 8, 16, width), lambda j: (0, 0, j)),
        out_shape=jax.ShapeDtypeStruct((count // 8, 16, rows), jnp.float32),
        compiler_params=SMALL,
        name="join",
    )(*operands)


def spread_kernel(parts, out):
    total = parts[0]
    for k in range(1, parts.shape[0]):
        total = total + parts[k]
    for k in range(out.shape[0]):
        out[k] = total


def summed_copies(parts):
    members, high, rows = parts.shape
    steps = 3
    block = pl.BlockSpec((members, high, rows // steps), lambda j: (0, 0, j))
    return pl.pallas_call(
        spread_kernel,
        grid=(steps,),
        in_specs=[block],
        out_specs=block,
        out_shape=jax.ShapeDtypeStruct(parts.shape, jnp.float32),
        compiler_params=SMALL,
        name="spread",
    )(parts)


def part_kernel(own, to_a, to_b, to_y):
    middle = to_a.shape[0]
    to_a[...] = own[:middle, :8, :]
    to_b[...] = own[middle:, :8, :]
    to_y[...] = own[:, 8:, :]


def peel_kernel(own, came_a, came_b, came_y, to_y, to_a, to_b):
    members = own.shape[0]
    middle = members // 2
    to_y[:members] = own[:, :8, :]
    to_y[members : members + middle] = came_a[...]
    to_y[members + middle :] = came_b[...]
    for out, cut in ((to_a, slice(0, middle)), (to_b, slice(middle, members))):
        out[:middle] = own[cut, 8:, :]
        out[middle:] = came_y[cut]


def copied(kernel, name, operands, lengths):
    rows = operands[0].shape[2]
    width = rows // 3

    def spec(length, high):
        return pl.BlockSpec((length, high, width), lambda j: (0, 0, j))

    return pl.pallas_call(
        kernel,
        grid=(rows // width,),
        in_specs=[spec(*x.shape[:2]) for x in operands],
        out_specs=[spec(length, 8) for length in lengths],
        out_shape=[jax.ShapeDtypeStruct((length, 8, rows), jnp.float32) for length in lengths],
        compiler_params=SMALL,
        name=name,
    )(*operands)


def score_kernel(
    at, own, za0, zb0, yb1, ya0, za1, zb1, prior, refs_t, powers, rounded, stats
):
    step = pl.program_id(0)
    p, q = at[0], at[1]
    rows = prior.shape[1]
    orient, eigen = refs_t.shape
    lines = stats.shape[1] // 2
    piece = eigen // 16
    middle = own.shape[0] // 2

    def put(base, major, s, minor, block):
        place = base + major * (4 * piece) + s * (2 * piece) + minor * piece
        rounded[pl.ds(pl.multiple_of(place, piece), piece), :] = block.reshape(piece, rows).astype(
            jnp.bfloat16
        )

    wide = eigen // 2
    for s, (z0, z1) in enumerate(((za0, za1), (zb0, zb1))):
        cut = slice(s * middle, (s + 1) * middle)
        after = slice((2 + s) * middle, (3 + s) * middle)
        put(0, p, s, q, own[cut, :8, :])
        put(0, p, s, 1 - q, z0[...])
        put(0, 1 - p, s, q, ya0[cut])
        put(0, 1 - p, s, 1 - q, ya0[after])
        put(wide, q, s, p, own[cut, 8:, :])
        put(wide, q, s, 1 - p, yb1[cut])
        put(wide, 1 - q, s, p, z1[:middle])
        put(wide, 1 - q, s, 1 - p, z1[middle:])
    scores = jnp.dot(refs_t[...], rounded[...], preferred_element_type=jnp.float32)
    block = prior[...] - at[2] * (orient // OBLOCK)
    parts = [
        scores[k * OBLOCK : (k + 1) * OBLOCK] + jnp.where(block == k, PRIOR_INCREMENT, 0.0)
        for k in range(orient // OBLOCK)
    ]
    tops = [jnp.max(part, axis=0, keepdims=True) for part in parts]
    top = tops[0]
    for other in tops[1:]:
        top = jnp.maximum(top, other)
    total = jnp.zeros_like(top)
    for k, part in enumerate(parts):
        power = jnp.exp(part - top)
        powers[k * OBLOCK : (k + 1) * OBLOCK, :] = power
        total = total + jnp.sum(power, axis=0, keepdims=True)
    for h in range(rows // LANES):
        line = step * (rows // LANES) + h
        cut = slice(h * LANES, (h + 1) * LANES)
        shape = (stats.shape[0], 1, LANES)
        stats[:, pl.ds(line, 1), :] = jnp.broadcast_to(top[None, :, cut], shape)
        stats[:, pl.ds(lines + line, 1), :] = jnp.broadcast_to(total[None, :, cut], shape)


def scores_of(at, held, prior, refs_t, members):
    rows = prior.shape[1]
    orient, eigen = refs_t.shape
    width = 256
    lines = 2 * rows // LANES
    return pl.pallas_call(
        score_kernel,
        grid_spec=pltpu.PrefetchScalarGridSpec(
            num_scalar_prefetch=1,
            grid=(rows // width,),
            in_specs=[pl.BlockSpec((*x.shape[:2], width), lambda j, at: (0, 0, j)) for x in held]
            + [
                pl.BlockSpec((1, width), lambda j, at: (0, j)),
                pl.BlockSpec((orient, eigen), lambda j, at: (0, 0)),
            ],
            out_specs=[
                pl.BlockSpec((orient, width), lambda j, at: (0, j)),
                pl.BlockSpec((eigen, width), lambda j, at: (0, j)),
                pl.BlockSpec((members, lines, LANES), lambda j, at: (0, 0, 0)),
            ],
        ),
        out_shape=[
            jax.ShapeDtypeStruct((orient, rows), jnp.float32),
            jax.ShapeDtypeStruct((eigen, rows), jnp.bfloat16),
            jax.ShapeDtypeStruct((members, lines, LANES), jnp.float32),
        ],
        compiler_params=BIG,
        name="scores",
    )(at, *held, prior, refs_t)


def total_kernel(at, stats, own, powers, rounded, keep, send, factor):
    step = pl.program_id(0)
    eigen, rows = rounded.shape
    width = powers.shape[0]
    peers = keep.shape[0]
    share = eigen // (2 * peers)
    lines = rows // LANES
    body = keep.shape[1] - keep.shape[1] % share

    @pl.when(step == 0)
    def _():
        tops = stats[:, :lines, :]
        top = jnp.max(tops, axis=0)
        total = jnp.sum(stats[:, lines:, :] * jnp.exp(tops - top[None]), axis=0)
        scale = jnp.exp(own[0, :lines, :] - top) / total
        for k in range(lines):
            factor[:, k * LANES : (k + 1) * LANES] = scale[k : k + 1, :]

    weights = (powers[...] * factor[...]).astype(jnp.bfloat16)
    totals = lax.dot_general(rounded[...], weights, LAST, preferred_element_type=jnp.float32)
    ones = jnp.ones((16, rows), jnp.bfloat16)
    masses = lax.dot_general(ones, weights, LAST, preferred_element_type=jnp.float32)
    first = at[3] == 0
    for h in range(width // LANES):
        column = step * (width // LANES) + h
        cut = slice(h * LANES, (h + 1) * LANES)
        place = pl.ds(pl.multiple_of(column * share, share), share)
        for q in range(peers):
            even = totals[2 * q * share : (2 * q + 1) * share, cut]
            odd = totals[(2 * q + 1) * share : (2 * q + 2) * share, cut]
            keep[q, place, :] = jnp.where(first, even, odd)
            send[q, place, :] = jnp.where(first, odd, even)
        mass = jnp.broadcast_to(masses[None, 0:1, cut], (peers, 1, LANES))
        keep[:, pl.ds(body + column, 1), :] = mass
        send[:, pl.ds(body + column, 1), :] = mass


def totals_of(at, stats, sent, powers, rounded, peers):
    eigen, rows = rounded.shape
    orient = powers.shape[0]
    width = 256
    deep = (eigen // (2 * peers) + 1) * (orient // LANES)
    out = jax.ShapeDtypeStruct((peers, deep, LANES), jnp.float32)
    return pl.pallas_call(
        total_kernel,
        grid_spec=pltpu.PrefetchScalarGridSpec(
            num_scalar_prefetch=1,
            grid=(orient // width,),
            in_specs=[
                pl.BlockSpec(stats.shape, lambda j, at: (0, 0, 0)),
                pl.BlockSpec((1, *sent.shape[1:]), lambda j, at: (0, 0, 0)),
                pl.BlockSpec((width, rows), lambda j, at: (j, 0)),
                pl.BlockSpec((eigen, rows), lambda j, at: (0, 0)),
            ],
            out_specs=[pl.BlockSpec((peers, deep, LANES), lambda j, at: (0, 0, 0))] * 2,
            scratch_shapes=[pltpu.VMEM((1, rows), jnp.float32)],
        ),
        out_shape=[out, out],
        compiler_params=BIG,
        name="totals",
    )(at, stats, sent, powers, rounded)


def final_kernel(at, parts, refs, out):
    share, orient = out.shape
    both = parts[0]
    for d in range(1, parts.shape[0]):
        both = both + parts[d]
    body = share * (orient // LANES)
    for k in range(orient // LANES):
        cut = slice(k * LANES, (k + 1) * LANES)
        above = both[k * share : (k + 1) * share] + refs[:, cut].astype(jnp.float32)
        out[:, cut] = above / (both[body + k : body + k + 1] + 1.0)


def final_of(at, parts, refs):
    eigen, orient = refs.shape
    share = eigen // (2 * parts.shape[0])
    return pl.pallas_call(
        final_kernel,
        grid_spec=pltpu.PrefetchScalarGridSpec(
            num_scalar_prefetch=1,
            grid=(1,),
            in_specs=[
                pl.BlockSpec(parts.shape, lambda j, at: (0, 0, 0)),
                pl.BlockSpec((share, orient), lambda j, at: (at[4], 0)),
            ],
            out_specs=pl.BlockSpec((share, orient), lambda j, at: (0, 0)),
        ),
        out_shape=jax.ShapeDtypeStruct((share, orient), jnp.float32),
        compiler_params=SMALL,
        name="final",
    )(at, parts, refs)


def with_a(x, axis):
    return lax.ppermute(x, axis, [(i, i ^ 1) for i in range(lax.axis_size(axis))])


def with_b(x, axis):
    size = lax.axis_size(axis)
    return lax.ppermute(x, axis, [(i, (i + (1 if i % 2 else -1)) % size) for i in range(size)])


def shards(images, phantom, inject_rows, prior_blocks, basis, refs):
    rows = images.shape[1] * images.shape[2]
    flat = images[0].reshape(rows, basis.shape[0])
    p, q = lax.axis_index("yl"), lax.axis_index("zhl")
    at = jnp.stack(
        [p, q, lax.axis_index(MEM), lax.axis_index("core"), lax.axis_index(GRP)]
    ).astype(jnp.int32)

    def block(which, pieces):
        column = jnp.int32(which).reshape(1)
        return projected(column, inject_rows[0], flat, basis, phantom, pieces)

    to_a, to_b = block(3 - q, 2)
    (to_y,) = block(1 - p, 1)
    came_z = with_a(to_a, TALL), with_b(to_b, TALL)
    came_y = with_a(to_y, RING)
    to_a, to_b, to_y, left, right = relayed(at, *block(p, 1), *block(2 + q, 1), came_y, came_z)
    came_z = with_a(to_a, TALL), with_b(to_b, TALL)
    parts = joined(left, right, came_z, with_b(to_y, RING))
    parts = lax.all_to_all(parts, ALIKE, 0, 0, tiled=True)
    own = lax.all_to_all(summed_copies(parts), ALIKE, 0, 0, tiled=True)
    members = own.shape[0]
    to_a, to_b, to_y = copied(
        part_kernel, "part", (own,), (members // 2, members // 2, members)
    )
    first = with_a(to_a, TALL), with_b(to_b, TALL), with_b(to_y, RING)
    to_y, to_a, to_b = copied(
        peel_kernel, "peel", (own, *first), (2 * members, members, members)
    )
    second = with_a(to_y, RING), with_a(to_a, TALL), with_b(to_b, TALL)
    powers, rounded, sent = scores_of(
        at,
        (own, *first, *second),
        prior_blocks[0].reshape(1, rows),
        refs.T,
        lax.axis_size(MEM),
    )
    stats = lax.all_to_all(sent, MEM, 0, 0, tiled=True)
    keep, send = totals_of(at, stats, sent, powers, rounded, lax.axis_size(PEERS))
    parts = keep + lax.ppermute(send, "core", [(0, 1), (1, 0)])
    parts = lax.all_to_all(parts, PEERS, 0, 0, tiled=True)
    return final_of(at, parts, refs)


def solution(mesh):
    fine = Mesh(mesh.devices.reshape(4, 2, 2, 4, 2, 2, 2), GRP + MEM)
    placed = (
        P(GRP, None, None, MEM),
        P(GRP, MEM),
        P(GRP, None, None),
        P(GRP, None, None),
        P(MEM, None),
        P(None, MEM),
    )
    return jax.shard_map(
        shards, mesh=fine, in_specs=placed, out_specs=P(GRP, MEM), check_vma=False
    )
```

```python
import functools

import jax
import jax.numpy as jnp
from jax import lax
from jax.experimental import pallas as pl
from jax.experimental.pallas import tpu as pltpu
from jax.sharding import Mesh, PartitionSpec as P

OBLOCK = 256
PRIOR_INCREMENT = 3.0
GRP = ("x", "zl", "core")
RING = ("yh", "yl")
MEM = RING + ("zh",)
ALIKE = ("yh", "zh")
PEERS = ("x", "zl")
LANES = 128
BIG = pltpu.CompilerParams(vmem_limit_bytes=28 << 20)
SMALL = pltpu.CompilerParams(vmem_limit_bytes=14 << 20)
LAST = (((1,), (1,)), ((), ()))


def project_kernel(batch, at, inject, images, basis, phantom, *rest):
    outs, (pixels_in, columns, ghost, sems) = rest[:-4], rest[-4:]
    steps, width = pixels_in.shape[:2]
    count = columns.shape[2]
    start = batch * steps * width
    loads = [
        pltpu.make_async_copy(
            basis.at[:, pl.ds(pl.multiple_of(at[j] * count, count), count)],
            columns.at[j],
            sems.at[j],
        )
        for j in range(2)
    ]
    loads.append(pltpu.make_async_copy(phantom, ghost, sems.at[2]))
    for k in range(steps):
        source = images.at[pl.ds(start + k * width, width), :]
        loads.append(pltpu.make_async_copy(source, pixels_in.at[k], sems.at[3 + k]))
    for load in loads:
        load.start()
    hits = []
    for k in range(steps):
        position = k * width + lax.broadcasted_iota(jnp.int32, (1, width), 1)
        hit = jnp.zeros((1, width), jnp.float32)
        for i in range(inject.shape[1]):
            hit = jnp.where(position == inject[batch, i], 1.0, hit)
        hits.append(hit)
    for load in loads[:3]:
        load.wait()
    spread = jnp.broadcast_to(ghost[...], (LANES, ghost.shape[1]))
    mine = [columns[j].T for j in range(2)]
    extra = [
        lax.dot_general(m, spread, LAST, preferred_element_type=jnp.float32) for m in mine
    ]
    for k in range(steps):
        loads[3 + k].wait()
        for j, out in enumerate(outs):
            plain = lax.dot_general(
                mine[j], pixels_in[k], LAST, preferred_element_type=jnp.float32
            )
            for c in range(width // LANES):
                cut = slice(c * LANES, (c + 1) * LANES)
                out[:, k * width + c * LANES : k * width + (c + 1) * LANES] = (
                    plain[:, cut] + extra[j] * hits[k][:, cut]
                )


def projected(at, batch, inject, images, basis, phantom):
    pixels = images.shape[1]
    rows = images.shape[0] // inject.shape[0]
    steps = 2
    count = basis.shape[1] // 4
    out = jax.ShapeDtypeStruct((count, rows), jnp.float32)
    images, basis, phantom = (
        pltpu.with_memory_space_constraint(x, pltpu.HBM) for x in (images, basis, phantom)
    )
    found = pl.pallas_call(
        functools.partial(project_kernel, batch),
        grid_spec=pltpu.PrefetchScalarGridSpec(
            num_scalar_prefetch=2,
            grid=(1,),
            in_specs=[pl.BlockSpec(memory_space=pltpu.HBM)] * 3,
            out_specs=[pl.BlockSpec(out.shape, lambda j, at, s: (0, 0))] * 2,
            scratch_shapes=[
                pltpu.VMEM((steps, rows // steps, pixels), images.dtype),
                pltpu.VMEM((2, pixels, count), basis.dtype),
                pltpu.VMEM((1, pixels), phantom.dtype),
                pltpu.SemaphoreType.DMA((steps + 3,)),
            ],
        ),
        out_shape=[out, out],
        compiler_params=SMALL,
        name="project",
    )(at, inject, images, basis, phantom)
    return tuple(found)


def by_columns(kernel, name, operands, shapes):
    rows = operands[0].shape[-1]
    width = rows // 3

    def spec(shape):
        head = tuple(shape[:-1])
        zeros = (0,) * len(head)
        return pl.BlockSpec((*head, width), lambda j: (*zeros, j))

    shapes = [(*shape, rows) for shape in shapes]
    return pl.pallas_call(
        kernel,
        grid=(rows // width,),
        in_specs=[spec(x.shape) for x in operands],
        out_specs=[spec(shape) for shape in shapes],
        out_shape=[jax.ShapeDtypeStruct(shape, jnp.float32) for shape in shapes],
        compiler_params=SMALL,
        name=name,
    )(*operands)


def join_kernel(keep_a, keep_b, came_a, came_b, out):
    for m in range(out.shape[0]):
        cut = slice(m * 8, (m + 1) * 8)
        out[m, :8, :] = keep_a[cut, :] + came_a[cut, :]
        out[m, 8:, :] = keep_b[cut, :] + came_b[cut, :]


def total_of(parts):
    total = parts[0]
    for part in parts[1:]:
        total = total + part
    return total


def middle_kernel(parts, keep_a, keep_b, came_a, came_b, out):
    total = total_of([parts[m] for m in range(parts.shape[0])])
    for m in range(out.shape[0]):
        cut = slice(m * 8, (m + 1) * 8)
        out[m, 0] = total
        out[m, 1, :8, :] = keep_a[cut, :] + came_a[cut, :]
        out[m, 1, 8:, :] = keep_b[cut, :] + came_b[cut, :]


def turn_kernel(both, copies, out_a, out_b):
    total = total_of([both[m, 1] for m in range(both.shape[0])])
    for m in range(both.shape[0]):
        copies[m] = total
        out_a[m] = both[m, 0, :8, :]
        out_b[m] = both[m, 0, 8:, :]


def part_kernel(own, out_a, out_b):
    for m in range(own.shape[0]):
        out_a[m] = own[m, :8, :]
        out_b[m] = own[m, 8:, :]


def score_kernel(at, own_a, own_b, came_a, came_b, prior, refs_t, past, powers, rounded, stats):
    step = pl.program_id(0)
    rows = prior.shape[1]
    orient, eigen = refs_t.shape
    high = eigen // 4
    before = stats.shape[1] - 2 * pl.num_programs(0) * (rows // LANES)
    lines = (stats.shape[1] - before) // 2

    if before:

        @pl.when(step == 0)
        def _():
            stats[:, :before, :] = past[:, :before, :]

    for base, held in ((0, (own_a, came_a)), (2 * high, (own_b, came_b))):
        for side, source in zip((at[0], 1 - at[0]), held):
            place = pl.multiple_of(base + high * side, high)
            rounded[pl.ds(place, high), :] = source[...].reshape(high, rows).astype(jnp.bfloat16)
    scores = jnp.dot(refs_t[...], rounded[...], preferred_element_type=jnp.float32)
    block = prior[...] - at[1] * (orient // OBLOCK)
    parts = [
        scores[k * OBLOCK : (k + 1) * OBLOCK] + jnp.where(block == k, PRIOR_INCREMENT, 0.0)
        for k in range(orient // OBLOCK)
    ]
    tops = [jnp.max(part, axis=0, keepdims=True) for part in parts]
    top = tops[0]
    for other in tops[1:]:
        top = jnp.maximum(top, other)
    total = jnp.zeros_like(top)
    for k, part in enumerate(parts):
        power = jnp.exp(part - top)
        powers[k * OBLOCK : (k + 1) * OBLOCK, :] = power
        total = total + jnp.sum(power, axis=0, keepdims=True)
    for h in range(rows // LANES):
        line = before + step * (rows // LANES) + h
        cut = slice(h * LANES, (h + 1) * LANES)
        shape = (stats.shape[0], 1, LANES)
        stats[:, pl.ds(line, 1), :] = jnp.broadcast_to(top[None, :, cut], shape)
        stats[:, pl.ds(lines + line, 1), :] = jnp.broadcast_to(total[None, :, cut], shape)


def scores_of(at, own, came, prior, refs_t, past, members):
    rows = prior.shape[1]
    orient, eigen = refs_t.shape
    width = 256
    group = own[0].shape[0]
    lines = 2 * rows // LANES
    if past is None:
        past = jnp.zeros((1, 1, LANES), jnp.float32)
    else:
        lines += past.shape[1]
    piece = pl.BlockSpec((group, 8, width), lambda j, at: (0, 0, j))
    return pl.pallas_call(
        score_kernel,
        grid_spec=pltpu.PrefetchScalarGridSpec(
            num_scalar_prefetch=1,
            grid=(rows // width,),
            in_specs=[piece] * 4
            + [
                pl.BlockSpec((1, width), lambda j, at: (0, j)),
                pl.BlockSpec((orient, eigen), lambda j, at: (0, 0)),
                pl.BlockSpec(past.shape, lambda j, at: (0, 0, 0)),
            ],
            out_specs=[
                pl.BlockSpec((orient, width), lambda j, at: (0, j)),
                pl.BlockSpec((eigen, width), lambda j, at: (0, j)),
                pl.BlockSpec((members, lines, LANES), lambda j, at: (0, 0, 0)),
            ],
        ),
        out_shape=[
            jax.ShapeDtypeStruct((orient, rows), jnp.float32),
            jax.ShapeDtypeStruct((eigen, rows), jnp.bfloat16),
            jax.ShapeDtypeStruct((members, lines, LANES), jnp.float32),
        ],
        compiler_params=BIG,
        name="scores",
    )(at, *own, *came, prior, refs_t, past)


def total_kernel(at, stats, own, powers_0, powers_1, rounded_0, rounded_1, keep, send, factor):
    step = pl.program_id(0)
    eigen, rows = rounded_0.shape
    width = powers_0.shape[0]
    peers = keep.shape[0]
    share = eigen // (2 * peers)
    lines = rows // LANES
    body = keep.shape[1] - keep.shape[1] % share

    @pl.when(step == 0)
    def _():
        for b in range(2):
            low, high = 2 * b * lines, (2 * b + 1) * lines
            tops = stats[:, low:high, :]
            top = jnp.max(tops, axis=0)
            total = jnp.sum(stats[:, high : high + lines, :] * jnp.exp(tops - top[None]), axis=0)
            scale = jnp.exp(own[0, low:high, :] - top) / total
            for k in range(lines):
                factor[b : b + 1, k * LANES : (k + 1) * LANES] = scale[k : k + 1, :]

    totals, masses = 0.0, 0.0
    ones = jnp.ones((16, rows), jnp.bfloat16)
    for b, (powers, rounded) in enumerate(((powers_0, rounded_0), (powers_1, rounded_1))):
        weights = (powers[...] * factor[b : b + 1, :]).astype(jnp.bfloat16)
        totals += lax.dot_general(rounded[...], weights, LAST, preferred_element_type=jnp.float32)
        masses += lax.dot_general(ones, weights, LAST, preferred_element_type=jnp.float32)
    first = at[2] == 0
    for h in range(width // LANES):
        column = step * (width // LANES) + h
        cut = slice(h * LANES, (h + 1) * LANES)
        place = pl.ds(pl.multiple_of(column * share, share), share)
        for q in range(peers):
            even = totals[2 * q * share : (2 * q + 1) * share, cut]
            odd = totals[(2 * q + 1) * share : (2 * q + 2) * share, cut]
            keep[q, place, :] = jnp.where(first, even, odd)
            send[q, place, :] = jnp.where(first, odd, even)
        mass = jnp.broadcast_to(masses[None, 0:1, cut], (peers, 1, LANES))
        keep[:, pl.ds(body + column, 1), :] = mass
        send[:, pl.ds(body + column, 1), :] = mass


def totals_of(at, stats, sent, powers, rounded, peers):
    eigen, rows = rounded[0].shape
    orient = powers[0].shape[0]
    width = 256
    deep = (eigen // (2 * peers) + 1) * (orient // LANES)
    out = jax.ShapeDtypeStruct((peers, deep, LANES), jnp.float32)
    return pl.pallas_call(
        total_kernel,
        grid_spec=pltpu.PrefetchScalarGridSpec(
            num_scalar_prefetch=1,
            grid=(orient // width,),
            in_specs=[
                pl.BlockSpec(stats.shape, lambda j, at: (0, 0, 0)),
                pl.BlockSpec((1, *sent.shape[1:]), lambda j, at: (0, 0, 0)),
            ]
            + [pl.BlockSpec((width, rows), lambda j, at: (j, 0))] * 2
            + [pl.BlockSpec((eigen, rows), lambda j, at: (0, 0))] * 2,
            out_specs=[pl.BlockSpec((peers, deep, LANES), lambda j, at: (0, 0, 0))] * 2,
            scratch_shapes=[pltpu.VMEM((2, rows), jnp.float32)],
        ),
        out_shape=[out, out],
        compiler_params=BIG,
        name="totals",
    )(at, stats, sent, *powers, *rounded)


def final_kernel(at, parts, refs, out):
    share, orient = out.shape
    both = parts[0]
    for d in range(1, parts.shape[0]):
        both = both + parts[d]
    body = share * (orient // LANES)
    for k in range(orient // LANES):
        cut = slice(k * LANES, (k + 1) * LANES)
        above = both[k * share : (k + 1) * share] + refs[:, cut].astype(jnp.float32)
        out[:, cut] = above / (both[body + k : body + k + 1] + 1.0)


def final_of(at, parts, refs):
    eigen, orient = refs.shape
    share = eigen // (2 * parts.shape[0])
    return pl.pallas_call(
        final_kernel,
        grid_spec=pltpu.PrefetchScalarGridSpec(
            num_scalar_prefetch=1,
            grid=(1,),
            in_specs=[
                pl.BlockSpec(parts.shape, lambda j, at: (0, 0, 0)),
                pl.BlockSpec((share, orient), lambda j, at: (at[3], 0)),
            ],
            out_specs=pl.BlockSpec((share, orient), lambda j, at: (0, 0)),
        ),
        out_shape=jax.ShapeDtypeStruct((share, orient), jnp.float32),
        compiler_params=SMALL,
        name="final",
    )(at, parts, refs)


def swapped(pair, axis):
    size = lax.axis_size(axis)
    with_a = [(i, i ^ 1) for i in range(size)]
    with_b = [(i, (i + (1 if i % 2 else -1)) % size) for i in range(size)]
    return tuple(lax.ppermute(x, axis, p) for x, p in zip(pair, (with_a, with_b)))


def shards(images, phantom, inject_rows, prior_blocks, basis, refs):
    batches, particles = images.shape[1:3]
    flat = images[0].reshape(batches * particles, basis.shape[0])
    p = lax.axis_index("yl").astype(jnp.int32)
    at = jnp.stack(
        [p]
        + [lax.axis_index(axis).astype(jnp.int32) for axis in (MEM, "core", GRP)]
    )

    def block(side, batch):
        columns = jnp.stack([side, 2 + side])
        return projected(columns, batch, inject_rows[0], flat, basis, phantom)

    def exchange(x):
        return lax.all_to_all(x, ALIKE, 0, 0, tiled=True)

    size = lax.axis_size(ALIKE)
    came_0 = swapped(block(1 - p, 0), RING)
    (parts,) = by_columns(join_kernel, "join", (*block(p, 0), *came_0), [(size, 16)])
    came_1 = swapped(block(1 - p, 1), RING)
    (both,) = by_columns(
        middle_kernel, "middle", (exchange(parts), *block(p, 1), *came_1), [(size, 2, 16)]
    )
    copies, *own_0 = by_columns(
        turn_kernel, "turn", (exchange(both),), [(size, 16), (size, 8), (size, 8)]
    )
    far_0 = swapped(own_0, RING)
    own_1 = by_columns(part_kernel, "part", (exchange(copies),), [(size, 8)] * 2)
    far_1 = swapped(own_1, RING)
    refs_t = refs.T
    members = lax.axis_size(MEM)
    powers_0, rounded_0, sent = scores_of(
        at, own_0, far_0, prior_blocks[0, :1], refs_t, None, members
    )
    powers_1, rounded_1, sent = scores_of(
        at, own_1, far_1, prior_blocks[0, 1:], refs_t, sent, members
    )
    stats = lax.all_to_all(sent, MEM, 0, 0, tiled=True)
    keep, send = totals_of(
        at, stats, sent, (powers_0, powers_1), (rounded_0, rounded_1), lax.axis_size(PEERS)
    )
    parts = keep + lax.ppermute(send, "core", [(0, 1), (1, 0)])
    parts = lax.all_to_all(parts, PEERS, 0, 0, tiled=True)
    return final_of(at, parts, refs)


def solution(mesh):
    fine = Mesh(mesh.devices.reshape(4, 2, 2, 4, 2, 4), GRP + MEM)
    placed = (
        P(GRP, None, None, MEM),
        P(GRP, MEM),
        P(GRP, None, None),
        P(GRP, None, None),
        P(MEM, None),
        P(None, MEM),
    )
    return jax.shard_map(
        shards, mesh=fine, in_specs=placed, out_specs=P(GRP, MEM), check_vma=False
    )
```

```python
import jax
import jax.numpy as jnp
from jax import lax
from jax.experimental import pallas as pl
from jax.experimental.pallas import tpu as pltpu
from jax.sharding import Mesh, PartitionSpec as P

OBLOCK = 256
PRIOR_INCREMENT = 3.0
GRP = ("x", "zl", "core")
RING = ("yh", "yl")
TALL = ("zhh", "zhl")
MEM = RING + TALL
ALIKE = ("yh", "zhh")
PEERS = ("x", "zl")
LANES = 128
BIG = pltpu.CompilerParams(vmem_limit_bytes=16 << 20)
SMALL = pltpu.CompilerParams(vmem_limit_bytes=8 << 20)
LAST = (((1,), (1,)), ((), ()))


def project_kernel(at, inject, images, basis, phantom, *rest):
    outs, (pixels_in, columns, ghost, sems) = rest[:-4], rest[-4:]
    which = pixels_in.shape[0]
    width = pixels_in.shape[1]
    count = columns.shape[1]
    first = pl.multiple_of(at[0] * count, count)
    loads = [
        pltpu.make_async_copy(basis.at[:, pl.ds(first, count)], columns, sems.at[which]),
        pltpu.make_async_copy(phantom, ghost, sems.at[which + 1]),
    ] + [
        pltpu.make_async_copy(images.at[pl.ds(k * width, width), :], pixels_in.at[k], sems.at[k])
        for k in range(which)
    ]
    for load in loads:
        load.start()
    per_batch = which // inject.shape[0]
    hits = []
    for k in range(which):
        position = (k % per_batch) * width + lax.broadcasted_iota(jnp.int32, (1, width), 1)
        hit = jnp.zeros((1, width), jnp.float32)
        for i in range(inject.shape[1]):
            hit = jnp.where(position == inject[k // per_batch, i], 1.0, hit)
        hits.append(hit)
    loads[0].wait()
    loads[1].wait()
    mine = columns[...].T
    spread = jnp.broadcast_to(ghost[...], (LANES, ghost.shape[1]))
    extra = lax.dot_general(mine, spread, LAST, preferred_element_type=jnp.float32)
    share = count // len(outs)
    for k in range(which):
        loads[2 + k].wait()
        plain = lax.dot_general(mine, pixels_in[k], LAST, preferred_element_type=jnp.float32)
        for c in range(width // LANES):
            cut = slice(c * LANES, (c + 1) * LANES)
            value = plain[:, cut] + extra * hits[k][:, cut]
            for j, out in enumerate(outs):
                out[:, k * width + c * LANES : k * width + (c + 1) * LANES] = value[
                    j * share : (j + 1) * share
                ]


def projected(block, inject, images, basis, phantom, pieces):
    rows, pixels = images.shape
    steps = 2 * inject.shape[0]
    count = basis.shape[1] // 4
    out = jax.ShapeDtypeStruct((count // pieces, rows), jnp.float32)
    images, basis, phantom = (
        pltpu.with_memory_space_constraint(x, pltpu.HBM) for x in (images, basis, phantom)
    )
    found = pl.pallas_call(
        project_kernel,
        grid_spec=pltpu.PrefetchScalarGridSpec(
            num_scalar_prefetch=2,
            grid=(1,),
            in_specs=[pl.BlockSpec(memory_space=pltpu.HBM)] * 3,
            out_specs=[pl.BlockSpec(out.shape, lambda j, at, s: (0, 0))] * pieces,
            scratch_shapes=[
                pltpu.VMEM((steps, rows // steps, pixels), images.dtype),
                pltpu.VMEM((pixels, count), basis.dtype),
                pltpu.VMEM((1, pixels), phantom.dtype),
                pltpu.SemaphoreType.DMA((steps + 2,)),
            ],
        ),
        out_shape=[out] * pieces,
        compiler_params=SMALL,
        name="project",
    )(block, inject, images, basis, phantom)
    return tuple(found)


def whole(kernel, name, operands, shapes, at=None, scratch=(), params=SMALL):
    lead = [] if at is None else [at]
    return pl.pallas_call(
        kernel,
        in_specs=[pl.BlockSpec(memory_space=pltpu.SMEM)] * len(lead)
        + [pl.BlockSpec(memory_space=pltpu.VMEM)] * len(operands),
        out_specs=[pl.BlockSpec(memory_space=pltpu.VMEM)] * len(shapes),
        out_shape=[jax.ShapeDtypeStruct(shape, dtype) for shape, dtype in shapes],
        scratch_shapes=list(scratch),
        compiler_params=params,
        name=name,
    )(*lead, *operands)


def relay_kernel(here_a, here_b, came_a, came_b, low, high):
    members = low.shape[0]
    for side, out in enumerate((low, high)):
        for q in range(members):
            cut = slice((side * members + q) * 8, (side * members + q + 1) * 8)
            out[q, :8, :] = here_a[cut, :] + came_a[cut, :]
            out[q, 8:, :] = here_b[cut, :] + came_b[cut, :]


def relayed(here, came):
    count, rows = here[0].shape
    shape = ((count // 16, 16, rows), jnp.float32)
    return whole(relay_kernel, "relay", (*here, *came), [shape, shape])


def join_kernel(here_a, here_b, came_a, came_b, low, high, out):
    members = low.shape[0]
    for side, other in enumerate((low, high)):
        for q in range(members):
            m = side * members + q
            cut = slice(m * 8, (m + 1) * 8)
            out[m, :8, :] = here_a[cut, :] + came_a[cut, :] + other[q, :8, :]
            out[m, 8:, :] = here_b[cut, :] + came_b[cut, :] + other[q, 8:, :]


def joined(here, came, others):
    count, rows = here[0].shape
    shape = ((count // 8, 16, rows), jnp.float32)
    return whole(join_kernel, "join", (*here, *came, *others), [shape])[0]


def spread_kernel(parts, out):
    width = 256

    def column(j, carry):
        cut = pl.ds(pl.multiple_of(j * width, width), width)
        total = parts[0, :, cut]
        for k in range(1, parts.shape[0]):
            total = total + parts[k, :, cut]
        for k in range(out.shape[0]):
            out[k, :, cut] = total
        return carry

    lax.fori_loop(0, parts.shape[2] // width, column, 0)


def summed_copies(parts):
    return whole(spread_kernel, "spread", (parts,), [(parts.shape, jnp.float32)])[0]


def peel_kernel(low, high, out_a, out_b):
    middle = low.shape[0]
    for offset, source in ((0, low), (middle, high)):
        out_a[offset : offset + middle] = source[:, :8, :]
        out_b[offset : offset + middle] = source[:, 8:, :]


def peeled(low, high):
    members, _, rows = low.shape
    shape = ((2 * members, 8, rows), jnp.float32)
    return whole(peel_kernel, "peel", (low, high), [shape, shape])


def score_kernel(
    at, own, low, high, near_a, near_b, far_a, far_b, prior, refs_t, powers, rounded, stats
):
    width = 256
    orient, eigen = refs_t.shape
    lines = stats.shape[1] // 2
    half = eigen // 8
    quarter = half // 2

    def column(step, carry):
        cut = pl.ds(pl.multiple_of(step * width, width), width)

        def put(which, offset, block):
            count = block.shape[0] * block.shape[1]
            place = pl.multiple_of(at[which] * 2 * half + offset, quarter)
            rounded[pl.ds(place, count), cut] = block.reshape(count, width).astype(jnp.bfloat16)

        put(0, 0, far_a[:, :, cut])
        put(0, half, far_b[:, :, cut])
        put(1, 0, near_a[:, :, cut])
        put(1, half, near_b[:, :, cut])
        for offset, source in ((0, low), (quarter, high)):
            put(2, offset, source[:, :8, cut])
            put(2, half + offset, source[:, 8:, cut])
        put(3, 0, own[:, :8, cut])
        put(3, half, own[:, 8:, cut])
        scores = jnp.dot(refs_t[...], rounded[:, cut], preferred_element_type=jnp.float32)
        block = prior[:, cut] - at[4] * (orient // OBLOCK)
        parts = [
            scores[k * OBLOCK : (k + 1) * OBLOCK] + jnp.where(block == k, PRIOR_INCREMENT, 0.0)
            for k in range(orient // OBLOCK)
        ]
        tops = [jnp.max(part, axis=0, keepdims=True) for part in parts]
        top = tops[0]
        for other in tops[1:]:
            top = jnp.maximum(top, other)
        total = jnp.zeros_like(top)
        for k, part in enumerate(parts):
            power = jnp.exp(part - top)
            powers[k * OBLOCK : (k + 1) * OBLOCK, cut] = power
            total = total + jnp.sum(power, axis=0, keepdims=True)
        for h in range(width // LANES):
            line = step * (width // LANES) + h
            side = slice(h * LANES, (h + 1) * LANES)
            shape = (stats.shape[0], 1, LANES)
            stats[:, pl.ds(line, 1), :] = jnp.broadcast_to(top[None, :, side], shape)
            stats[:, pl.ds(lines + line, 1), :] = jnp.broadcast_to(total[None, :, side], shape)
        return carry

    lax.fori_loop(0, powers.shape[1] // width, column, 0)


def scores_of(at, held, prior, refs_t, members):
    rows = prior.shape[1]
    orient, eigen = refs_t.shape
    shapes = [
        ((orient, rows), jnp.float32),
        ((eigen, rows), jnp.bfloat16),
        ((members, 2 * rows // LANES, LANES), jnp.float32),
    ]
    return whole(score_kernel, "scores", (*held, prior, refs_t), shapes, at=at, params=BIG)


def total_kernel(at, stats, own, powers, rounded, keep, send, factor):
    width = 256
    eigen, rows = rounded.shape
    peers = keep.shape[0]
    share = eigen // (2 * peers)
    lines = rows // LANES
    body = keep.shape[1] - keep.shape[1] % share
    tops = stats[:, :lines, :]
    top = jnp.max(tops, axis=0)
    total = jnp.sum(stats[:, lines:, :] * jnp.exp(tops - top[None]), axis=0)
    scale = jnp.exp(own[0, :lines, :] - top) / total
    for k in range(lines):
        factor[:, k * LANES : (k + 1) * LANES] = scale[k : k + 1, :]
    first = at[5] == 0
    ones = jnp.ones((16, rows), jnp.bfloat16)

    def orients(step, carry):
        block = powers[pl.ds(pl.multiple_of(step * width, width), width), :]
        weights = (block * factor[...]).astype(jnp.bfloat16)
        totals = lax.dot_general(rounded[...], weights, LAST, preferred_element_type=jnp.float32)
        masses = lax.dot_general(ones, weights, LAST, preferred_element_type=jnp.float32)
        for h in range(width // LANES):
            column = step * (width // LANES) + h
            cut = slice(h * LANES, (h + 1) * LANES)
            place = pl.ds(pl.multiple_of(column * share, share), share)
            for q in range(peers):
                even = totals[2 * q * share : (2 * q + 1) * share, cut]
                odd = totals[(2 * q + 1) * share : (2 * q + 2) * share, cut]
                keep[q, place, :] = jnp.where(first, even, odd)
                send[q, place, :] = jnp.where(first, odd, even)
            mass = jnp.broadcast_to(masses[None, 0:1, cut], (peers, 1, LANES))
            keep[:, pl.ds(body + column, 1), :] = mass
            send[:, pl.ds(body + column, 1), :] = mass
        return carry

    lax.fori_loop(0, powers.shape[0] // width, orients, 0)


def totals_of(at, stats, sent, powers, rounded, peers):
    eigen, rows = rounded.shape
    orient = powers.shape[0]
    deep = (eigen // (2 * peers) + 1) * (orient // LANES)
    shape = ((peers, deep, LANES), jnp.float32)
    return whole(
        total_kernel,
        "totals",
        (stats, sent, powers, rounded),
        [shape, shape],
        at=at,
        scratch=[pltpu.VMEM((1, rows), jnp.float32)],
        params=BIG,
    )


def final_kernel(at, parts, refs, out):
    share, orient = out.shape
    both = parts[0]
    for d in range(1, parts.shape[0]):
        both = both + parts[d]
    body = share * (orient // LANES)
    for k in range(orient // LANES):
        cut = slice(k * LANES, (k + 1) * LANES)
        above = both[k * share : (k + 1) * share] + refs[:, cut].astype(jnp.float32)
        out[:, cut] = above / (both[body + k : body + k + 1] + 1.0)


def final_of(at, parts, refs):
    eigen, orient = refs.shape
    share = eigen // (2 * parts.shape[0])
    return pl.pallas_call(
        final_kernel,
        grid_spec=pltpu.PrefetchScalarGridSpec(
            num_scalar_prefetch=1,
            grid=(1,),
            in_specs=[
                pl.BlockSpec(parts.shape, lambda j, at: (0, 0, 0)),
                pl.BlockSpec((share, orient), lambda j, at: (at[6], 0)),
            ],
            out_specs=pl.BlockSpec((share, orient), lambda j, at: (0, 0)),
        ),
        out_shape=jax.ShapeDtypeStruct((share, orient), jnp.float32),
        compiler_params=SMALL,
        name="final",
    )(at, parts, refs)


def swapped(pair, axis):
    size = lax.axis_size(axis)
    with_a = [(i, i ^ 1) for i in range(size)]
    with_b = [(i, (i + (1 if i % 2 else -1)) % size) for i in range(size)]
    return tuple(lax.ppermute(x, axis, p) for x, p in zip(pair, (with_a, with_b)))


def shards(images, phantom, inject_rows, prior_blocks, basis, refs):
    rows = images.shape[1] * images.shape[2]
    flat = images[0].reshape(rows, basis.shape[0])
    p, q = lax.axis_index("yl"), lax.axis_index("zhl")
    at = jnp.stack(
        [
            (1 - p) * 2 + 1 - q,
            (1 - p) * 2 + q,
            p * 2 + 1 - q,
            p * 2 + q,
            lax.axis_index(MEM),
            lax.axis_index("core"),
            lax.axis_index(GRP),
        ]
    ).astype(jnp.int32)
    blocks = [
        projected(at[k : k + 1], inject_rows[0], flat, basis, phantom, 2) for k in range(4)
    ]

    through = swapped(blocks[0], RING)
    came = swapped(blocks[1], RING)
    others = swapped(relayed(blocks[2], through), TALL)
    parts = joined(blocks[3], came, others)
    parts = lax.all_to_all(parts, ALIKE, 0, 0, tiled=True)
    own = lax.all_to_all(summed_copies(parts), ALIKE, 0, 0, tiled=True)
    middle = own.shape[0] // 2
    low, high = swapped((own[:middle], own[middle:]), TALL)
    near = swapped((own[:, :8], own[:, 8:]), RING)
    far = swapped(peeled(low, high), RING)
    powers, rounded, sent = scores_of(
        at,
        (own, low, high, *near, *far),
        prior_blocks[0].reshape(1, rows),
        refs.T,
        lax.axis_size(MEM),
    )
    stats = lax.all_to_all(sent, MEM, 0, 0, tiled=True)
    keep, send = totals_of(at, stats, sent, powers, rounded, lax.axis_size(PEERS))
    parts = keep + lax.ppermute(send, "core", [(0, 1), (1, 0)])
    parts = lax.all_to_all(parts, PEERS, 0, 0, tiled=True)
    return final_of(at, parts, refs)


def solution(mesh):
    fine = Mesh(mesh.devices.reshape(4, 2, 2, 4, 2, 2, 2), GRP + MEM)
    placed = (
        P(GRP, None, None, MEM),
        P(GRP, MEM),
        P(GRP, None, None),
        P(GRP, None, None),
        P(MEM, None),
        P(None, MEM),
    )
    return jax.shard_map(
        shards, mesh=fine, in_specs=placed, out_specs=P(GRP, MEM), check_vma=False
    )
```

```python
import functools

import jax
import jax.numpy as jnp
from jax import lax
from jax.experimental import pallas as pl
from jax.experimental.pallas import tpu as pltpu
from jax.sharding import Mesh, PartitionSpec as P

OBLOCK = 256
PRIOR_INCREMENT = 3.0
GRP = ("x", "zl", "core")
RING = ("yh", "yl")
TALL = ("zhh", "zhl")
MEM = RING + TALL
ALIKE = ("yh", "zhh")
PEERS = ("x", "zl")
LANES = 128
BIG = pltpu.CompilerParams(vmem_limit_bytes=16 << 20)
SMALL = pltpu.CompilerParams(vmem_limit_bytes=8 << 20)
LAST = (((1,), (1,)), ((), ()))


def project_kernel(at, inject, images, basis, phantom, *rest):
    outs, (pixels_in, columns, ghost, sems) = rest[:-4], rest[-4:]
    which = pixels_in.shape[0]
    width = pixels_in.shape[1]
    count = columns.shape[1]
    first = pl.multiple_of(at[0] * count, count)
    loads = [
        pltpu.make_async_copy(basis.at[:, pl.ds(first, count)], columns, sems.at[which]),
        pltpu.make_async_copy(phantom, ghost, sems.at[which + 1]),
    ] + [
        pltpu.make_async_copy(images.at[pl.ds(k * width, width), :], pixels_in.at[k], sems.at[k])
        for k in range(which)
    ]
    for load in loads:
        load.start()
    per_batch = which // inject.shape[0]
    hits = []
    for k in range(which):
        position = (k % per_batch) * width + lax.broadcasted_iota(jnp.int32, (1, width), 1)
        hit = jnp.zeros((1, width), jnp.float32)
        for i in range(inject.shape[1]):
            hit = jnp.where(position == inject[k // per_batch, i], 1.0, hit)
        hits.append(hit)
    loads[0].wait()
    loads[1].wait()
    mine = columns[...].T
    spread = jnp.broadcast_to(ghost[...], (LANES, ghost.shape[1]))
    extra = lax.dot_general(mine, spread, LAST, preferred_element_type=jnp.float32)
    share = count // len(outs)
    for k in range(which):
        loads[2 + k].wait()
        plain = lax.dot_general(mine, pixels_in[k], LAST, preferred_element_type=jnp.float32)
        for c in range(width // LANES):
            cut = slice(c * LANES, (c + 1) * LANES)
            value = plain[:, cut] + extra * hits[k][:, cut]
            for j, out in enumerate(outs):
                out[:, k * width + c * LANES : k * width + (c + 1) * LANES] = value[
                    j * share : (j + 1) * share
                ]


def projected(block, inject, images, basis, phantom, pieces):
    rows, pixels = images.shape
    steps = 2 * inject.shape[0]
    count = basis.shape[1] // 4
    out = jax.ShapeDtypeStruct((count // pieces, rows), jnp.float32)
    images, basis, phantom = (
        pltpu.with_memory_space_constraint(x, pltpu.HBM) for x in (images, basis, phantom)
    )
    found = pl.pallas_call(
        project_kernel,
        grid_spec=pltpu.PrefetchScalarGridSpec(
            num_scalar_prefetch=2,
            grid=(1,),
            in_specs=[pl.BlockSpec(memory_space=pltpu.HBM)] * 3,
            out_specs=[pl.BlockSpec(out.shape, lambda j, at, s: (0, 0))] * pieces,
            scratch_shapes=[
                pltpu.VMEM((steps, rows // steps, pixels), images.dtype),
                pltpu.VMEM((pixels, count), basis.dtype),
                pltpu.VMEM((1, pixels), phantom.dtype),
                pltpu.SemaphoreType.DMA((steps + 2,)),
            ],
        ),
        out_shape=[out] * pieces,
        compiler_params=SMALL,
        name="project",
    )(block, inject, images, basis, phantom)
    return tuple(found)


def whole(kernel, name, operands, shapes, at=None, scratch=(), params=SMALL):
    lead = [] if at is None else [at]
    return pl.pallas_call(
        kernel,
        in_specs=[pl.BlockSpec(memory_space=pltpu.SMEM)] * len(lead)
        + [pl.BlockSpec(memory_space=pltpu.VMEM)] * len(operands),
        out_specs=[pl.BlockSpec(memory_space=pltpu.VMEM)] * len(shapes),
        out_shape=[jax.ShapeDtypeStruct(shape, dtype) for shape, dtype in shapes],
        scratch_shapes=list(scratch),
        compiler_params=params,
        name=name,
    )(*lead, *operands)


def relay_kernel(here_a, here_b, came_a, came_b, low, high):
    members = low.shape[0]
    for side, out in enumerate((low, high)):
        for q in range(members):
            cut = slice((side * members + q) * 8, (side * members + q + 1) * 8)
            out[q, :8, :] = here_a[cut, :] + came_a[cut, :]
            out[q, 8:, :] = here_b[cut, :] + came_b[cut, :]


def relayed(here, came):
    count, rows = here[0].shape
    shape = ((count // 16, 16, rows), jnp.float32)
    return whole(relay_kernel, "relay", (*here, *came), [shape, shape])


def join_kernel(here_a, here_b, came_a, came_b, low, high, out):
    members = low.shape[0]
    for side, other in enumerate((low, high)):
        for q in range(members):
            m = side * members + q
            cut = slice(m * 8, (m + 1) * 8)
            out[m, :8, :] = here_a[cut, :] + came_a[cut, :] + other[q, :8, :]
            out[m, 8:, :] = here_b[cut, :] + came_b[cut, :] + other[q, 8:, :]


def joined(here, came, others):
    count, rows = here[0].shape
    shape = ((count // 8, 16, rows), jnp.float32)
    return whole(join_kernel, "join", (*here, *came, *others), [shape])[0]


def spread_kernel(parts, out):
    width = 256

    def column(j, carry):
        cut = pl.ds(pl.multiple_of(j * width, width), width)
        total = parts[0, :, cut]
        for k in range(1, parts.shape[0]):
            total = total + parts[k, :, cut]
        for k in range(out.shape[0]):
            out[k, :, cut] = total
        return carry

    lax.fori_loop(0, parts.shape[2] // width, column, 0)


def summed_copies(parts):
    return whole(spread_kernel, "spread", (parts,), [(parts.shape, jnp.float32)])[0]


def peel_kernel(low, high, out_a, out_b):
    middle = low.shape[0]
    for offset, source in ((0, low), (middle, high)):
        out_a[offset : offset + middle] = source[:, :8, :]
        out_b[offset : offset + middle] = source[:, 8:, :]


def peeled(low, high):
    members, _, rows = low.shape
    shape = ((2 * members, 8, rows), jnp.float32)
    return whole(peel_kernel, "peel", (low, high), [shape, shape])


def put_block(at, rounded, cut, which, offset, block):
    count = block.shape[0] * block.shape[1]
    place = at[which] * (rounded.shape[0] // 4) + offset
    place = pl.multiple_of(place, rounded.shape[0] // 16)
    rounded[pl.ds(place, count), cut] = block.reshape(count, -1).astype(jnp.bfloat16)


def stage_kernel(at, own, low, high, near_a, near_b, staged):
    width = 256
    half = staged.shape[0] // 8
    quarter = half // 2

    def column(step, carry):
        cut = pl.ds(pl.multiple_of(step * width, width), width)
        put = functools.partial(put_block, at, staged, cut)
        put(0, 0, jnp.zeros((16, 8, width), jnp.float32))
        put(1, 0, near_a[:, :, cut])
        put(1, half, near_b[:, :, cut])
        for offset, source in ((0, low), (quarter, high)):
            put(2, offset, source[:, :8, cut])
            put(2, half + offset, source[:, 8:, cut])
        put(3, 0, own[:, :8, cut])
        put(3, half, own[:, 8:, cut])
        return carry

    lax.fori_loop(0, staged.shape[1] // width, column, 0)


def staged_of(at, held):
    members, high, rows = held[0].shape
    shape = ((members * high * 4, rows), jnp.bfloat16)
    return whole(stage_kernel, "stage", held, [shape], at=at)[0]


def score_kernel(at, staged, far_a, far_b, prior, refs_t, powers, rounded, stats):
    width = 256
    orient, eigen = refs_t.shape
    lines = stats.shape[1] // 2

    def column(step, carry):
        cut = pl.ds(pl.multiple_of(step * width, width), width)
        rounded[:, cut] = staged[:, cut]
        put_block(at, rounded, cut, 0, 0, far_a[:, :, cut])
        put_block(at, rounded, cut, 0, eigen // 8, far_b[:, :, cut])
        scores = jnp.dot(refs_t[...], rounded[:, cut], preferred_element_type=jnp.float32)
        block = prior[:, cut] - at[4] * (orient // OBLOCK)
        parts = [
            scores[k * OBLOCK : (k + 1) * OBLOCK] + jnp.where(block == k, PRIOR_INCREMENT, 0.0)
            for k in range(orient // OBLOCK)
        ]
        tops = [jnp.max(part, axis=0, keepdims=True) for part in parts]
        top = tops[0]
        for other in tops[1:]:
            top = jnp.maximum(top, other)
        total = jnp.zeros_like(top)
        for k, part in enumerate(parts):
            power = jnp.exp(part - top)
            powers[k * OBLOCK : (k + 1) * OBLOCK, cut] = power
            total = total + jnp.sum(power, axis=0, keepdims=True)
        for h in range(width // LANES):
            line = step * (width // LANES) + h
            side = slice(h * LANES, (h + 1) * LANES)
            shape = (stats.shape[0], 1, LANES)
            stats[:, pl.ds(line, 1), :] = jnp.broadcast_to(top[None, :, side], shape)
            stats[:, pl.ds(lines + line, 1), :] = jnp.broadcast_to(total[None, :, side], shape)
        return carry

    lax.fori_loop(0, powers.shape[1] // width, column, 0)


def scores_of(at, held, prior, refs_t, members):
    rows = prior.shape[1]
    orient, eigen = refs_t.shape
    shapes = [
        ((orient, rows), jnp.float32),
        ((eigen, rows), jnp.bfloat16),
        ((members, 2 * rows // LANES, LANES), jnp.float32),
    ]
    return whole(score_kernel, "scores", (*held, prior, refs_t), shapes, at=at, params=BIG)


def total_kernel(at, stats, own, powers, rounded, keep, send, factor):
    width = 256
    eigen, rows = rounded.shape
    peers = keep.shape[0]
    share = eigen // (2 * peers)
    lines = rows // LANES
    body = keep.shape[1] - keep.shape[1] % share
    tops = stats[:, :lines, :]
    top = jnp.max(tops, axis=0)
    total = jnp.sum(stats[:, lines:, :] * jnp.exp(tops - top[None]), axis=0)
    scale = jnp.exp(own[0, :lines, :] - top) / total
    for k in range(lines):
        factor[:, k * LANES : (k + 1) * LANES] = scale[k : k + 1, :]
    first = at[5] == 0
    ones = jnp.ones((16, rows), jnp.bfloat16)

    def orients(step, carry):
        block = powers[pl.ds(pl.multiple_of(step * width, width), width), :]
        weights = (block * factor[...]).astype(jnp.bfloat16)
        totals = lax.dot_general(rounded[...], weights, LAST, preferred_element_type=jnp.float32)
        masses = lax.dot_general(ones, weights, LAST, preferred_element_type=jnp.float32)
        for h in range(width // LANES):
            column = step * (width // LANES) + h
            cut = slice(h * LANES, (h + 1) * LANES)
            place = pl.ds(pl.multiple_of(column * share, share), share)
            for q in range(peers):
                even = totals[2 * q * share : (2 * q + 1) * share, cut]
                odd = totals[(2 * q + 1) * share : (2 * q + 2) * share, cut]
                keep[q, place, :] = jnp.where(first, even, odd)
                send[q, place, :] = jnp.where(first, odd, even)
            mass = jnp.broadcast_to(masses[None, 0:1, cut], (peers, 1, LANES))
            keep[:, pl.ds(body + column, 1), :] = mass
            send[:, pl.ds(body + column, 1), :] = mass
        return carry

    lax.fori_loop(0, powers.shape[0] // width, orients, 0)


def totals_of(at, stats, sent, powers, rounded, peers):
    eigen, rows = rounded.shape
    orient = powers.shape[0]
    deep = (eigen // (2 * peers) + 1) * (orient // LANES)
    shape = ((peers, deep, LANES), jnp.float32)
    return whole(
        total_kernel,
        "totals",
        (stats, sent, powers, rounded),
        [shape, shape],
        at=at,
        scratch=[pltpu.VMEM((1, rows), jnp.float32)],
        params=BIG,
    )


def final_kernel(at, parts, refs, out):
    share, orient = out.shape
    both = parts[0]
    for d in range(1, parts.shape[0]):
        both = both + parts[d]
    body = share * (orient // LANES)
    for k in range(orient // LANES):
        cut = slice(k * LANES, (k + 1) * LANES)
        above = both[k * share : (k + 1) * share] + refs[:, cut].astype(jnp.float32)
        out[:, cut] = above / (both[body + k : body + k + 1] + 1.0)


def final_of(at, parts, refs):
    eigen, orient = refs.shape
    share = eigen // (2 * parts.shape[0])
    return pl.pallas_call(
        final_kernel,
        grid_spec=pltpu.PrefetchScalarGridSpec(
            num_scalar_prefetch=1,
            grid=(1,),
            in_specs=[
                pl.BlockSpec(parts.shape, lambda j, at: (0, 0, 0)),
                pl.BlockSpec((share, orient), lambda j, at: (at[6], 0)),
            ],
            out_specs=pl.BlockSpec((share, orient), lambda j, at: (0, 0)),
        ),
        out_shape=jax.ShapeDtypeStruct((share, orient), jnp.float32),
        compiler_params=SMALL,
        name="final",
    )(at, parts, refs)


def swapped(pair, axis):
    size = lax.axis_size(axis)
    with_a = [(i, i ^ 1) for i in range(size)]
    with_b = [(i, (i + (1 if i % 2 else -1)) % size) for i in range(size)]
    return tuple(lax.ppermute(x, axis, p) for x, p in zip(pair, (with_a, with_b)))


def shards(images, phantom, inject_rows, prior_blocks, basis, refs):
    rows = images.shape[1] * images.shape[2]
    flat = images[0].reshape(rows, basis.shape[0])
    p, q = lax.axis_index("yl"), lax.axis_index("zhl")
    at = jnp.stack(
        [
            (1 - p) * 2 + 1 - q,
            (1 - p) * 2 + q,
            p * 2 + 1 - q,
            p * 2 + q,
            lax.axis_index(MEM),
            lax.axis_index("core"),
            lax.axis_index(GRP),
        ]
    ).astype(jnp.int32)
    def block(which):
        return projected(which, inject_rows[0], flat, basis, phantom, 2)

    through = swapped(block(at[0:1]), RING)
    turned = relayed(block(at[2:3]), through)
    kept = block(at[3:4])
    low, high, after = lax.optimization_barrier((*turned, at[1:2]))
    others = swapped((low, high), TALL)
    came = swapped(block(after), RING)
    parts = joined(kept, came, others)
    parts = lax.all_to_all(parts, ALIKE, 0, 0, tiled=True)
    own = lax.all_to_all(summed_copies(parts), ALIKE, 0, 0, tiled=True)
    middle = own.shape[0] // 2
    low, high = swapped((own[:middle], own[middle:]), TALL)
    near = swapped((own[:, :8], own[:, 8:]), RING)
    far = swapped(peeled(low, high), RING)
    powers, rounded, sent = scores_of(
        at,
        (staged_of(at, (own, low, high, *near)), *far),
        prior_blocks[0].reshape(1, rows),
        refs.T,
        lax.axis_size(MEM),
    )
    stats = lax.all_to_all(sent, MEM, 0, 0, tiled=True)
    keep, send = totals_of(at, stats, sent, powers, rounded, lax.axis_size(PEERS))
    parts = keep + lax.ppermute(send, "core", [(0, 1), (1, 0)])
    parts = lax.all_to_all(parts, PEERS, 0, 0, tiled=True)
    return final_of(at, parts, refs)


def solution(mesh):
    fine = Mesh(mesh.devices.reshape(4, 2, 2, 4, 2, 2, 2), GRP + MEM)
    placed = (
        P(GRP, None, None, MEM),
        P(GRP, MEM),
        P(GRP, None, None),
        P(GRP, None, None),
        P(MEM, None),
        P(None, MEM),
    )
    return jax.shard_map(
        shards, mesh=fine, in_specs=placed, out_specs=P(GRP, MEM), check_vma=False
    )
```

```python
import functools

import jax
import jax.numpy as jnp
from jax import lax
from jax.experimental import pallas as pl
from jax.experimental.pallas import tpu as pltpu
from jax.sharding import Mesh, PartitionSpec as P

OBLOCK = 256
PRIOR_INCREMENT = 3.0
GRP = ("x", "zl", "core")
RING = ("yh", "yl")
TALL = ("zhh", "zhl")
MEM = RING + TALL
ALIKE = ("yh", "zhh")
PEERS = ("x", "zl")
LANES = 128
BIG = pltpu.CompilerParams(vmem_limit_bytes=16 << 20)
SMALL = pltpu.CompilerParams(vmem_limit_bytes=8 << 20)
LAST = (((1,), (1,)), ((), ()))


def project_kernel(at, inject, images, basis, phantom, *rest):
    outs, (pixels_in, columns, ghost, sems) = rest[:-4], rest[-4:]
    which = pixels_in.shape[0]
    width = pixels_in.shape[1]
    count = columns.shape[1]
    first = pl.multiple_of(at[0] * count, count)
    loads = [
        pltpu.make_async_copy(basis.at[:, pl.ds(first, count)], columns, sems.at[which]),
        pltpu.make_async_copy(phantom, ghost, sems.at[which + 1]),
    ] + [
        pltpu.make_async_copy(images.at[pl.ds(k * width, width), :], pixels_in.at[k], sems.at[k])
        for k in range(which)
    ]
    for load in loads:
        load.start()
    per_batch = which // inject.shape[0]
    hits = []
    for k in range(which):
        position = (k % per_batch) * width + lax.broadcasted_iota(jnp.int32, (1, width), 1)
        hit = jnp.zeros((1, width), jnp.float32)
        for i in range(inject.shape[1]):
            hit = jnp.where(position == inject[k // per_batch, i], 1.0, hit)
        hits.append(hit)
    loads[0].wait()
    loads[1].wait()
    mine = columns[...].T
    spread = jnp.broadcast_to(ghost[...], (LANES, ghost.shape[1]))
    extra = lax.dot_general(mine, spread, LAST, preferred_element_type=jnp.float32)
    share = count // len(outs)
    for k in range(which):
        loads[2 + k].wait()
        plain = lax.dot_general(mine, pixels_in[k], LAST, preferred_element_type=jnp.float32)
        for c in range(width // LANES):
            cut = slice(c * LANES, (c + 1) * LANES)
            value = plain[:, cut] + extra * hits[k][:, cut]
            for j, out in enumerate(outs):
                out[:, k * width + c * LANES : k * width + (c + 1) * LANES] = value[
                    j * share : (j + 1) * share
                ]


def projected(block, inject, images, basis, phantom, pieces):
    rows, pixels = images.shape
    steps = 2 * inject.shape[0]
    count = basis.shape[1] // 4
    out = jax.ShapeDtypeStruct((count // pieces, rows), jnp.float32)
    images, basis, phantom = (
        pltpu.with_memory_space_constraint(x, pltpu.HBM) for x in (images, basis, phantom)
    )
    found = pl.pallas_call(
        project_kernel,
        grid_spec=pltpu.PrefetchScalarGridSpec(
            num_scalar_prefetch=2,
            grid=(1,),
            in_specs=[pl.BlockSpec(memory_space=pltpu.HBM)] * 3,
            out_specs=[pl.BlockSpec(out.shape, lambda j, at, s: (0, 0))] * pieces,
            scratch_shapes=[
                pltpu.VMEM((steps, rows // steps, pixels), images.dtype),
                pltpu.VMEM((pixels, count), basis.dtype),
                pltpu.VMEM((1, pixels), phantom.dtype),
                pltpu.SemaphoreType.DMA((steps + 2,)),
            ],
        ),
        out_shape=[out] * pieces,
        compiler_params=SMALL,
        name="project",
    )(block, inject, images, basis, phantom)
    return tuple(found)


def whole(kernel, name, operands, shapes, at=None, scratch=(), params=SMALL):
    lead = [] if at is None else [at]
    return pl.pallas_call(
        kernel,
        in_specs=[pl.BlockSpec(memory_space=pltpu.SMEM)] * len(lead)
        + [pl.BlockSpec(memory_space=pltpu.VMEM)] * len(operands),
        out_specs=[pl.BlockSpec(memory_space=pltpu.VMEM)] * len(shapes),
        out_shape=[jax.ShapeDtypeStruct(shape, dtype) for shape, dtype in shapes],
        scratch_shapes=list(scratch),
        compiler_params=params,
        name=name,
    )(*lead, *operands)


def relay_kernel(here_a, here_b, came_a, came_b, low, high):
    members = low.shape[0]
    for side, out in enumerate((low, high)):
        for q in range(members):
            cut = slice((side * members + q) * 8, (side * members + q + 1) * 8)
            out[q, :8, :] = here_a[cut, :] + came_a[cut, :]
            out[q, 8:, :] = here_b[cut, :] + came_b[cut, :]


def relayed(here, came):
    count, rows = here[0].shape
    shape = ((count // 16, 16, rows), jnp.float32)
    return whole(relay_kernel, "relay", (*here, *came), [shape, shape])


def join_kernel(here_a, here_b, came_a, came_b, low, high, out):
    members = low.shape[0]
    for side, other in enumerate((low, high)):
        for q in range(members):
            m = side * members + q
            cut = slice(m * 8, (m + 1) * 8)
            out[m, :8, :] = here_a[cut, :] + came_a[cut, :] + other[q, :8, :]
            out[m, 8:, :] = here_b[cut, :] + came_b[cut, :] + other[q, 8:, :]


def joined(here, came, others):
    count, rows = here[0].shape
    shape = ((count // 8, 16, rows), jnp.float32)
    return whole(join_kernel, "join", (*here, *came, *others), [shape])[0]


def spread_kernel(parts, out):
    width = 256

    def column(j, carry):
        cut = pl.ds(pl.multiple_of(j * width, width), width)
        total = parts[0, :, cut]
        for k in range(1, parts.shape[0]):
            total = total + parts[k, :, cut]
        for k in range(out.shape[0]):
            out[k, :, cut] = total
        return carry

    lax.fori_loop(0, parts.shape[2] // width, column, 0)


def summed_copies(parts):
    return whole(spread_kernel, "spread", (parts,), [(parts.shape, jnp.float32)])[0]


def peel_kernel(low, high, out_a, out_b):
    middle = low.shape[0]
    for offset, source in ((0, low), (middle, high)):
        out_a[offset : offset + middle] = source[:, :8, :]
        out_b[offset : offset + middle] = source[:, 8:, :]


def peeled(low, high):
    members, _, rows = low.shape
    shape = ((2 * members, 8, rows), jnp.float32)
    return whole(peel_kernel, "peel", (low, high), [shape, shape])


def put_block(at, rounded, cut, which, offset, block):
    count = block.shape[0] * block.shape[1]
    place = at[which] * (rounded.shape[0] // 4) + offset
    place = pl.multiple_of(place, rounded.shape[0] // 16)
    rounded[pl.ds(place, count), cut] = block.reshape(count, -1).astype(jnp.bfloat16)


def stage_kernel(at, own, low, high, near_a, near_b, staged):
    width = 256
    half = staged.shape[0] // 8
    quarter = half // 2

    def column(step, carry):
        cut = pl.ds(pl.multiple_of(step * width, width), width)
        put = functools.partial(put_block, at, staged, cut)
        put(0, 0, jnp.zeros((16, 8, width), jnp.float32))
        put(1, 0, near_a[:, :, cut])
        put(1, half, near_b[:, :, cut])
        for offset, source in ((0, low), (quarter, high)):
            put(2, offset, source[:, :8, cut])
            put(2, half + offset, source[:, 8:, cut])
        put(3, 0, own[:, :8, cut])
        put(3, half, own[:, 8:, cut])
        return carry

    lax.fori_loop(0, staged.shape[1] // width, column, 0)


def staged_of(at, held):
    members, high, rows = held[0].shape
    shape = ((members * high * 4, rows), jnp.bfloat16)
    return whole(stage_kernel, "stage", held, [shape], at=at)[0]


def score_kernel(at, staged, far_a, far_b, prior, refs_t, powers, rounded, stats):
    width = 256
    orient, eigen = refs_t.shape
    lines = stats.shape[1] // 2

    def column(step, carry):
        cut = pl.ds(pl.multiple_of(step * width, width), width)
        rounded[:, cut] = staged[:, cut]
        put_block(at, rounded, cut, 0, 0, far_a[:, :, cut])
        put_block(at, rounded, cut, 0, eigen // 8, far_b[:, :, cut])
        scores = jnp.dot(refs_t[...], rounded[:, cut], preferred_element_type=jnp.float32)
        block = prior[:, cut] - at[4] * (orient // OBLOCK)
        parts = [
            (scores[k * OBLOCK : (k + 1) * OBLOCK], jnp.where(block == k, PRIOR_INCREMENT, 0.0))
            for k in range(orient // OBLOCK)
        ]
        tops = [jnp.max(part, axis=0, keepdims=True) + bonus for part, bonus in parts]
        top = tops[0]
        for other in tops[1:]:
            top = jnp.maximum(top, other)
        total = jnp.zeros_like(top)
        for k, (part, bonus) in enumerate(parts):
            power = jnp.exp(part - (top - bonus))
            powers[k * OBLOCK : (k + 1) * OBLOCK, cut] = power
            total = total + jnp.sum(power, axis=0, keepdims=True)
        for h in range(width // LANES):
            line = step * (width // LANES) + h
            side = slice(h * LANES, (h + 1) * LANES)
            shape = (stats.shape[0], 1, LANES)
            stats[:, pl.ds(line, 1), :] = jnp.broadcast_to(top[None, :, side], shape)
            stats[:, pl.ds(lines + line, 1), :] = jnp.broadcast_to(total[None, :, side], shape)
        return carry

    lax.fori_loop(0, powers.shape[1] // width, column, 0)


def scores_of(at, held, prior, refs_t, members):
    rows = prior.shape[1]
    orient, eigen = refs_t.shape
    shapes = [
        ((orient, rows), jnp.float32),
        ((eigen, rows), jnp.bfloat16),
        ((members, 2 * rows // LANES, LANES), jnp.float32),
    ]
    return whole(score_kernel, "scores", (*held, prior, refs_t), shapes, at=at, params=BIG)


def total_kernel(other, at, stats, own, powers, rounded, out, factor, mine):
    width = 256
    eigen, rows = rounded.shape
    peers = out.shape[0]
    share = eigen // (2 * peers)
    lines = rows // LANES
    body = out.shape[1] - out.shape[1] % share
    tops = stats[:, :lines, :]
    top = jnp.max(tops, axis=0)
    total = jnp.sum(stats[:, lines:, :] * jnp.exp(tops - top[None]), axis=0)
    scale = jnp.exp(own[0, :lines, :] - top) / total
    for k in range(lines):
        factor[:, k * LANES : (k + 1) * LANES] = scale[k : k + 1, :]
    core = 1 - at[5] if other else at[5]
    for q in range(peers):
        place = pl.multiple_of((2 * q + core) * share, share)
        mine[q * share : (q + 1) * share, :] = rounded[pl.ds(place, share), :]
    ones = jnp.ones((16, rows), jnp.bfloat16)

    def orients(step, carry):
        block = powers[pl.ds(pl.multiple_of(step * width, width), width), :]
        weights = (block * factor[...]).astype(jnp.bfloat16)
        totals = lax.dot_general(mine[...], weights, LAST, preferred_element_type=jnp.float32)
        masses = lax.dot_general(ones, weights, LAST, preferred_element_type=jnp.float32)
        for h in range(width // LANES):
            column = step * (width // LANES) + h
            cut = slice(h * LANES, (h + 1) * LANES)
            place = pl.ds(pl.multiple_of(column * share, share), share)
            for q in range(peers):
                out[q, place, :] = totals[q * share : (q + 1) * share, cut]
            mass = jnp.broadcast_to(masses[None, 0:1, cut], (peers, 1, LANES))
            out[:, pl.ds(body + column, 1), :] = mass
        return carry

    lax.fori_loop(0, powers.shape[0] // width, orients, 0)


def totals_of(other, at, stats, sent, powers, rounded, peers):
    eigen, rows = rounded.shape
    orient = powers.shape[0]
    deep = (eigen // (2 * peers) + 1) * (orient // LANES)
    return whole(
        functools.partial(total_kernel, other),
        "totals",
        (stats, sent, powers, rounded),
        [((peers, deep, LANES), jnp.float32)],
        at=at,
        scratch=[pltpu.VMEM((1, rows), jnp.float32), pltpu.VMEM((eigen // 2, rows), jnp.bfloat16)],
        params=BIG,
    )[0]


def final_kernel(at, parts, refs, out):
    share, orient = out.shape
    both = parts[0]
    for d in range(1, parts.shape[0]):
        both = both + parts[d]
    body = share * (orient // LANES)
    for k in range(orient // LANES):
        cut = slice(k * LANES, (k + 1) * LANES)
        above = both[k * share : (k + 1) * share] + refs[:, cut].astype(jnp.float32)
        out[:, cut] = above / (both[body + k : body + k + 1] + 1.0)


def final_of(at, parts, refs):
    eigen, orient = refs.shape
    share = eigen // (2 * parts.shape[0])
    return pl.pallas_call(
        final_kernel,
        grid_spec=pltpu.PrefetchScalarGridSpec(
            num_scalar_prefetch=1,
            grid=(1,),
            in_specs=[
                pl.BlockSpec(parts.shape, lambda j, at: (0, 0, 0)),
                pl.BlockSpec((share, orient), lambda j, at: (at[6], 0)),
            ],
            out_specs=pl.BlockSpec((share, orient), lambda j, at: (0, 0)),
        ),
        out_shape=jax.ShapeDtypeStruct((share, orient), jnp.float32),
        compiler_params=SMALL,
        name="final",
    )(at, parts, refs)


def swapped(pair, axis):
    size = lax.axis_size(axis)
    with_a = [(i, i ^ 1) for i in range(size)]
    with_b = [(i, (i + (1 if i % 2 else -1)) % size) for i in range(size)]
    return tuple(lax.ppermute(x, axis, p) for x, p in zip(pair, (with_a, with_b)))


def shards(images, phantom, inject_rows, prior_blocks, basis, refs):
    rows = images.shape[1] * images.shape[2]
    flat = images[0].reshape(rows, basis.shape[0])
    p, q = lax.axis_index("yl"), lax.axis_index("zhl")
    at = jnp.stack(
        [
            (1 - p) * 2 + 1 - q,
            (1 - p) * 2 + q,
            p * 2 + 1 - q,
            p * 2 + q,
            lax.axis_index(MEM),
            lax.axis_index("core"),
            lax.axis_index(GRP),
        ]
    ).astype(jnp.int32)
    def block(which):
        return projected(which, inject_rows[0], flat, basis, phantom, 2)

    through = swapped(block(at[0:1]), RING)
    turned = relayed(block(at[2:3]), through)
    kept = block(at[3:4])
    low, high, after = lax.optimization_barrier((*turned, at[1:2]))
    others = swapped((low, high), TALL)
    came = swapped(block(after), RING)
    parts = joined(kept, came, others)
    parts = lax.all_to_all(parts, ALIKE, 0, 0, tiled=True)
    own = lax.all_to_all(summed_copies(parts), ALIKE, 0, 0, tiled=True)
    middle = own.shape[0] // 2
    low, high = swapped((own[:middle], own[middle:]), TALL)
    near = swapped((own[:, :8], own[:, 8:]), RING)
    far = swapped(peeled(low, high), RING)
    powers, rounded, sent = scores_of(
        at,
        (staged_of(at, (own, low, high, *near)), *far),
        prior_blocks[0].reshape(1, rows),
        refs.T,
        lax.axis_size(MEM),
    )
    stats = lax.all_to_all(sent, MEM, 0, 0, tiled=True)
    sums = (stats, sent, powers, rounded, lax.axis_size(PEERS))
    came = lax.ppermute(totals_of(True, at, *sums), "core", [(0, 1), (1, 0)])
    parts = totals_of(False, at, *sums) + came
    parts = lax.all_to_all(parts, PEERS, 0, 0, tiled=True)
    return final_of(at, parts, refs)


def solution(mesh):
    fine = Mesh(mesh.devices.reshape(4, 2, 2, 4, 2, 2, 2), GRP + MEM)
    placed = (
        P(GRP, None, None, MEM),
        P(GRP, MEM),
        P(GRP, None, None),
        P(GRP, None, None),
        P(MEM, None),
        P(None, MEM),
    )
    return jax.shard_map(
        shards, mesh=fine, in_specs=placed, out_specs=P(GRP, MEM), check_vma=False
    )
```

```python
import functools

import jax
import jax.numpy as jnp
from jax import lax
from jax.experimental import pallas as pl
from jax.experimental.pallas import tpu as pltpu
from jax.sharding import Mesh, PartitionSpec as P

OBLOCK = 256
PRIOR_INCREMENT = 3.0
GRP = ("x", "zl", "core")
RING = ("yh", "yl")
TALL = ("zhh", "zhl")
MEM = RING + TALL
ALIKE = ("zhh", "yh")
EVERY = ("zhl", "zhh", "yl", "yh")
PEERS = ("zl", "x")
LANES = 128
BIG = pltpu.CompilerParams(vmem_limit_bytes=16 << 20)
SMALL = pltpu.CompilerParams(vmem_limit_bytes=8 << 20)
LAST = (((1,), (1,)), ((), ()))


def project_kernel(at, inject, images, basis, phantom, *rest):
    outs, (pixels_in, columns, ghost, sems) = rest[:-4], rest[-4:]
    which = pixels_in.shape[0]
    width = pixels_in.shape[1]
    count = columns.shape[1]
    first = pl.multiple_of(at[0] * count, count)
    loads = [
        pltpu.make_async_copy(basis.at[:, pl.ds(first, count)], columns, sems.at[which]),
        pltpu.make_async_copy(phantom, ghost, sems.at[which + 1]),
    ] + [
        pltpu.make_async_copy(images.at[pl.ds(k * width, width), :], pixels_in.at[k], sems.at[k])
        for k in range(which)
    ]
    for load in loads:
        load.start()
    per_batch = which // inject.shape[0]
    hits = []
    for k in range(which):
        position = (k % per_batch) * width + lax.broadcasted_iota(jnp.int32, (1, width), 1)
        hit = jnp.zeros((1, width), jnp.float32)
        for i in range(inject.shape[1]):
            hit = jnp.where(position == inject[k // per_batch, i], 1.0, hit)
        hits.append(hit)
    loads[0].wait()
    loads[1].wait()
    mine = columns[...].T
    spread = jnp.broadcast_to(ghost[...], (LANES, ghost.shape[1]))
    extra = lax.dot_general(mine, spread, LAST, preferred_element_type=jnp.float32)
    share = count // len(outs)
    for k in range(which):
        loads[2 + k].wait()
        plain = lax.dot_general(mine, pixels_in[k], LAST, preferred_element_type=jnp.float32)
        for c in range(width // LANES):
            cut = slice(c * LANES, (c + 1) * LANES)
            value = plain[:, cut] + extra * hits[k][:, cut]
            for j, out in enumerate(outs):
                out[:, k * width + c * LANES : k * width + (c + 1) * LANES] = value[
                    j * share : (j + 1) * share
                ]


def projected(block, inject, images, basis, phantom, pieces):
    rows, pixels = images.shape
    steps = 2 * inject.shape[0]
    count = basis.shape[1] // 4
    out = jax.ShapeDtypeStruct((count // pieces, rows), jnp.float32)
    images, basis, phantom = (
        pltpu.with_memory_space_constraint(x, pltpu.HBM) for x in (images, basis, phantom)
    )
    found = pl.pallas_call(
        project_kernel,
        grid_spec=pltpu.PrefetchScalarGridSpec(
            num_scalar_prefetch=2,
            grid=(1,),
            in_specs=[pl.BlockSpec(memory_space=pltpu.HBM)] * 3,
            out_specs=[pl.BlockSpec(out.shape, lambda j, at, s: (0, 0))] * pieces,
            scratch_shapes=[
                pltpu.VMEM((steps, rows // steps, pixels), images.dtype),
                pltpu.VMEM((pixels, count), basis.dtype),
                pltpu.VMEM((1, pixels), phantom.dtype),
                pltpu.SemaphoreType.DMA((steps + 2,)),
            ],
        ),
        out_shape=[out] * pieces,
        compiler_params=SMALL,
        name="project",
    )(block, inject, images, basis, phantom)
    return tuple(found)


def whole(kernel, name, operands, shapes, at=None, scratch=(), params=SMALL):
    lead = [] if at is None else [at]
    return pl.pallas_call(
        kernel,
        in_specs=[pl.BlockSpec(memory_space=pltpu.SMEM)] * len(lead)
        + [pl.BlockSpec(memory_space=pltpu.VMEM)] * len(operands),
        out_specs=[pl.BlockSpec(memory_space=pltpu.VMEM)] * len(shapes),
        out_shape=[jax.ShapeDtypeStruct(shape, dtype) for shape, dtype in shapes],
        scratch_shapes=list(scratch),
        compiler_params=params,
        name=name,
    )(*lead, *operands)


def relay_kernel(here_a, here_b, came_a, came_b, low, high):
    members = low.shape[0]
    for side, out in enumerate((low, high)):
        for q in range(members):
            cut = slice((side * members + q) * 8, (side * members + q + 1) * 8)
            out[q, :8, :] = here_a[cut, :] + came_a[cut, :]
            out[q, 8:, :] = here_b[cut, :] + came_b[cut, :]


def relayed(here, came):
    count, rows = here[0].shape
    shape = ((count // 16, 16, rows), jnp.float32)
    return whole(relay_kernel, "relay", (*here, *came), [shape, shape])


def join_kernel(here_a, here_b, came_a, came_b, low, high, out):
    members = low.shape[0]
    for side, other in enumerate((low, high)):
        for q in range(members):
            m = side * members + q
            cut = slice(m * 8, (m + 1) * 8)
            out[m, :8, :] = here_a[cut, :] + came_a[cut, :] + other[q, :8, :]
            out[m, 8:, :] = here_b[cut, :] + came_b[cut, :] + other[q, 8:, :]


def joined(here, came, others):
    count, rows = here[0].shape
    shape = ((count // 8, 16, rows), jnp.float32)
    return whole(join_kernel, "join", (*here, *came, *others), [shape])[0]


def spread_kernel(parts, out):
    width = 256

    def column(j, carry):
        cut = pl.ds(pl.multiple_of(j * width, width), width)
        total = parts[0, :, cut]
        for k in range(1, parts.shape[0]):
            total = total + parts[k, :, cut]
        for k in range(out.shape[0]):
            out[k, :, cut] = total
        return carry

    lax.fori_loop(0, parts.shape[2] // width, column, 0)


def summed_copies(parts):
    return whole(spread_kernel, "spread", (parts,), [(parts.shape, jnp.float32)])[0]


def peel_kernel(low, high, out_a, out_b):
    middle = low.shape[0]
    for offset, source in ((0, low), (middle, high)):
        out_a[offset : offset + middle] = source[:, :8, :]
        out_b[offset : offset + middle] = source[:, 8:, :]


def peeled(low, high):
    members, _, rows = low.shape
    shape = ((2 * members, 8, rows), jnp.float32)
    return whole(peel_kernel, "peel", (low, high), [shape, shape])


def put_block(at, rounded, cut, which, offset, block):
    count = block.shape[0] * block.shape[1]
    place = at[which] * (rounded.shape[0] // 4) + offset
    place = pl.multiple_of(place, rounded.shape[0] // 16)
    rounded[pl.ds(place, count), cut] = block.reshape(count, -1).astype(jnp.bfloat16)


def stage_kernel(at, own, low, high, near_a, near_b, staged):
    width = 256
    half = staged.shape[0] // 8
    quarter = half // 2

    def column(step, carry):
        cut = pl.ds(pl.multiple_of(step * width, width), width)
        put = functools.partial(put_block, at, staged, cut)
        put(0, 0, jnp.zeros((16, 8, width), jnp.float32))
        put(1, 0, near_a[:, :, cut])
        put(1, half, near_b[:, :, cut])
        for offset, source in ((0, low), (quarter, high)):
            put(2, offset, source[:, :8, cut])
            put(2, half + offset, source[:, 8:, cut])
        put(3, 0, own[:, :8, cut])
        put(3, half, own[:, 8:, cut])
        return carry

    lax.fori_loop(0, staged.shape[1] // width, column, 0)


def staged_of(at, held):
    members, high, rows = held[0].shape
    shape = ((members * high * 4, rows), jnp.bfloat16)
    return whole(stage_kernel, "stage", held, [shape], at=at)[0]


def score_kernel(at, staged, far_a, far_b, prior, refs_t, powers, rounded, stats):
    width = 256
    orient, eigen = refs_t.shape
    lines = stats.shape[1] // 2

    def column(step, carry):
        cut = pl.ds(pl.multiple_of(step * width, width), width)
        rounded[:, cut] = staged[:, cut]
        put_block(at, rounded, cut, 0, 0, far_a[:, :, cut])
        put_block(at, rounded, cut, 0, eigen // 8, far_b[:, :, cut])
        scores = jnp.dot(refs_t[...], rounded[:, cut], preferred_element_type=jnp.float32)
        block = prior[:, cut] - at[4] * (orient // OBLOCK)
        parts = [
            (scores[k * OBLOCK : (k + 1) * OBLOCK], jnp.where(block == k, PRIOR_INCREMENT, 0.0))
            for k in range(orient // OBLOCK)
        ]
        tops = [jnp.max(part, axis=0, keepdims=True) + bonus for part, bonus in parts]
        top = tops[0]
        for other in tops[1:]:
            top = jnp.maximum(top, other)
        total = jnp.zeros_like(top)
        for k, (part, bonus) in enumerate(parts):
            power = jnp.exp(part - (top - bonus))
            powers[k * OBLOCK : (k + 1) * OBLOCK, cut] = power
            total = total + jnp.sum(power, axis=0, keepdims=True)
        for h in range(width // LANES):
            line = step * (width // LANES) + h
            side = slice(h * LANES, (h + 1) * LANES)
            shape = (stats.shape[0], 1, LANES)
            stats[:, pl.ds(line, 1), :] = jnp.broadcast_to(top[None, :, side], shape)
            stats[:, pl.ds(lines + line, 1), :] = jnp.broadcast_to(total[None, :, side], shape)
        return carry

    lax.fori_loop(0, powers.shape[1] // width, column, 0)


def scores_of(at, held, prior, refs_t, members):
    rows = prior.shape[1]
    orient, eigen = refs_t.shape
    shapes = [
        ((orient, rows), jnp.float32),
        ((eigen, rows), jnp.bfloat16),
        ((members, 2 * rows // LANES, LANES), jnp.float32),
    ]
    return whole(score_kernel, "scores", (*held, prior, refs_t), shapes, at=at, params=BIG)


def total_kernel(other, outer, at, stats, own, powers, rounded, out, factor, mine):
    width = 256
    eigen, rows = rounded.shape
    peers = out.shape[0]
    share = eigen // (2 * peers)
    lines = rows // LANES
    body = out.shape[1] - out.shape[1] % share
    tops = stats[:, :lines, :]
    top = jnp.max(tops, axis=0)
    total = jnp.sum(stats[:, lines:, :] * jnp.exp(tops - top[None]), axis=0)
    scale = jnp.exp(own[0, :lines, :] - top) / total
    for k in range(lines):
        factor[:, k * LANES : (k + 1) * LANES] = scale[k : k + 1, :]
    core = 1 - at[5] if other else at[5]
    for q in range(peers):
        owner = q % (peers // outer) * outer + q // (peers // outer)
        place = pl.multiple_of((2 * owner + core) * share, share)
        mine[q * share : (q + 1) * share, :] = rounded[pl.ds(place, share), :]
    ones = jnp.ones((16, rows), jnp.bfloat16)

    def orients(step, carry):
        block = powers[pl.ds(pl.multiple_of(step * width, width), width), :]
        weights = (block * factor[...]).astype(jnp.bfloat16)
        totals = lax.dot_general(mine[...], weights, LAST, preferred_element_type=jnp.float32)
        masses = lax.dot_general(ones, weights, LAST, preferred_element_type=jnp.float32)
        for h in range(width // LANES):
            column = step * (width // LANES) + h
            cut = slice(h * LANES, (h + 1) * LANES)
            place = pl.ds(pl.multiple_of(column * share, share), share)
            for q in range(peers):
                out[q, place, :] = totals[q * share : (q + 1) * share, cut]
            mass = jnp.broadcast_to(masses[None, 0:1, cut], (peers, 1, LANES))
            out[:, pl.ds(body + column, 1), :] = mass
        return carry

    lax.fori_loop(0, powers.shape[0] // width, orients, 0)


def totals_of(other, at, stats, sent, powers, rounded, peers):
    eigen, rows = rounded.shape
    orient = powers.shape[0]
    deep = (eigen // (2 * peers) + 1) * (orient // LANES)
    return whole(
        functools.partial(total_kernel, other, lax.axis_size(PEERS[0])),
        "totals",
        (stats, sent, powers, rounded),
        [((peers, deep, LANES), jnp.float32)],
        at=at,
        scratch=[pltpu.VMEM((1, rows), jnp.float32), pltpu.VMEM((eigen // 2, rows), jnp.bfloat16)],
        params=BIG,
    )[0]


def final_kernel(at, parts, refs, out):
    share, orient = out.shape
    both = parts[0]
    for d in range(1, parts.shape[0]):
        both = both + parts[d]
    body = share * (orient // LANES)
    for k in range(orient // LANES):
        cut = slice(k * LANES, (k + 1) * LANES)
        above = both[k * share : (k + 1) * share] + refs[:, cut].astype(jnp.float32)
        out[:, cut] = above / (both[body + k : body + k + 1] + 1.0)


def final_of(at, parts, refs):
    eigen, orient = refs.shape
    share = eigen // (2 * parts.shape[0])
    return pl.pallas_call(
        final_kernel,
        grid_spec=pltpu.PrefetchScalarGridSpec(
            num_scalar_prefetch=1,
            grid=(1,),
            in_specs=[
                pl.BlockSpec(parts.shape, lambda j, at: (0, 0, 0)),
                pl.BlockSpec((share, orient), lambda j, at: (at[6], 0)),
            ],
            out_specs=pl.BlockSpec((share, orient), lambda j, at: (0, 0)),
        ),
        out_shape=jax.ShapeDtypeStruct((share, orient), jnp.float32),
        compiler_params=SMALL,
        name="final",
    )(at, parts, refs)


def swapped(pair, axis):
    size = lax.axis_size(axis)
    with_a = [(i, i ^ 1) for i in range(size)]
    with_b = [(i, (i + (1 if i % 2 else -1)) % size) for i in range(size)]
    return tuple(lax.ppermute(x, axis, p) for x, p in zip(pair, (with_a, with_b)))


def shards(images, phantom, inject_rows, prior_blocks, basis, refs):
    rows = images.shape[1] * images.shape[2]
    flat = images[0].reshape(rows, basis.shape[0])
    p, q = lax.axis_index("yl"), lax.axis_index("zhl")
    at = jnp.stack(
        [
            (1 - p) * 2 + 1 - q,
            (1 - p) * 2 + q,
            p * 2 + 1 - q,
            p * 2 + q,
            lax.axis_index(MEM),
            lax.axis_index("core"),
            lax.axis_index(GRP),
        ]
    ).astype(jnp.int32)
    def block(which):
        return projected(which, inject_rows[0], flat, basis, phantom, 2)

    through = swapped(block(at[0:1]), RING)
    turned = relayed(block(at[2:3]), through)
    kept = block(at[3:4])
    low, high, after = lax.optimization_barrier((*turned, at[1:2]))
    others = swapped((low, high), TALL)
    came = swapped(block(after), RING)
    parts = joined(kept, came, others)
    parts = lax.all_to_all(parts, ALIKE, 0, 0, tiled=True)
    own = lax.all_to_all(summed_copies(parts), ALIKE, 0, 0, tiled=True)
    middle = own.shape[0] // 2
    low, high = swapped((own[:middle], own[middle:]), TALL)
    near = swapped((own[:, :8], own[:, 8:]), RING)
    far = swapped(peeled(low, high), RING)
    powers, rounded, sent = scores_of(
        at,
        (staged_of(at, (own, low, high, *near)), *far),
        prior_blocks[0].reshape(1, rows),
        refs.T,
        lax.axis_size(MEM),
    )
    stats = lax.all_to_all(sent, EVERY, 0, 0, tiled=True)
    sums = (stats, sent, powers, rounded, lax.axis_size(PEERS))
    came = lax.ppermute(totals_of(True, at, *sums), "core", [(0, 1), (1, 0)])
    parts = totals_of(False, at, *sums) + came
    parts = lax.all_to_all(parts, PEERS, 0, 0, tiled=True)
    return final_of(at, parts, refs)


def solution(mesh):
    fine = Mesh(mesh.devices.reshape(4, 2, 2, 4, 2, 2, 2), GRP + MEM)
    placed = (
        P(GRP, None, None, MEM),
        P(GRP, MEM),
        P(GRP, None, None),
        P(GRP, None, None),
        P(MEM, None),
        P(None, MEM),
    )
    return jax.shard_map(
        shards, mesh=fine, in_specs=placed, out_specs=P(GRP, MEM), check_vma=False
    )
```

```python
import functools

import jax
import jax.numpy as jnp
from jax import lax
from jax.experimental import pallas as pl
from jax.experimental.pallas import tpu as pltpu
from jax.sharding import Mesh, PartitionSpec as P

OBLOCK = 256
PRIOR_INCREMENT = 3.0
GRP = ("x", "zl", "core")
RING = ("yh", "yl")
TALL = ("zhh", "zhl")
MEM = RING + TALL
ALIKE = ("yh", "zhh")
EVERY = ("zhl", "zhh", "yl", "yh")
PEERS = ("zl", "x")
LANES = 128
BIG = pltpu.CompilerParams(vmem_limit_bytes=16 << 20)
SMALL = pltpu.CompilerParams(vmem_limit_bytes=8 << 20)
LAST = (((1,), (1,)), ((), ()))


def project_kernel(at, inject, images, basis, phantom, *rest):
    outs, (pixels_in, columns, ghost, sems) = rest[:-4], rest[-4:]
    which = pixels_in.shape[0]
    width = pixels_in.shape[1]
    count = columns.shape[1]
    first = pl.multiple_of(at[0] * count, count)
    loads = [
        pltpu.make_async_copy(basis.at[:, pl.ds(first, count)], columns, sems.at[which]),
        pltpu.make_async_copy(phantom, ghost, sems.at[which + 1]),
    ] + [
        pltpu.make_async_copy(images.at[pl.ds(k * width, width), :], pixels_in.at[k], sems.at[k])
        for k in range(which)
    ]
    for load in loads:
        load.start()
    per_batch = which // inject.shape[0]
    hits = []
    for k in range(which):
        position = (k % per_batch) * width + lax.broadcasted_iota(jnp.int32, (1, width), 1)
        hit = jnp.zeros((1, width), jnp.float32)
        for i in range(inject.shape[1]):
            hit = jnp.where(position == inject[k // per_batch, i], 1.0, hit)
        hits.append(hit)
    loads[0].wait()
    loads[1].wait()
    mine = columns[...].T
    spread = jnp.broadcast_to(ghost[...], (LANES, ghost.shape[1]))
    extra = lax.dot_general(mine, spread, LAST, preferred_element_type=jnp.float32)
    share = count // len(outs)
    for k in range(which):
        loads[2 + k].wait()
        plain = lax.dot_general(mine, pixels_in[k], LAST, preferred_element_type=jnp.float32)
        for c in range(width // LANES):
            cut = slice(c * LANES, (c + 1) * LANES)
            value = plain[:, cut] + extra * hits[k][:, cut]
            for j, out in enumerate(outs):
                out[:, k * width + c * LANES : k * width + (c + 1) * LANES] = value[
                    j * share : (j + 1) * share
                ]


def projected(block, inject, images, basis, phantom, pieces):
    rows, pixels = images.shape
    steps = 2 * inject.shape[0]
    count = basis.shape[1] // 4
    out = jax.ShapeDtypeStruct((count // pieces, rows), jnp.float32)
    inject, images, basis, phantom = (
        pltpu.with_memory_space_constraint(x, pltpu.HBM) for x in (inject, images, basis, phantom)
    )
    found = pl.pallas_call(
        project_kernel,
        grid_spec=pltpu.PrefetchScalarGridSpec(
            num_scalar_prefetch=2,
            grid=(1,),
            in_specs=[pl.BlockSpec(memory_space=pltpu.HBM)] * 3,
            out_specs=[pl.BlockSpec(out.shape, lambda j, at, s: (0, 0))] * pieces,
            scratch_shapes=[
                pltpu.VMEM((steps, rows // steps, pixels), images.dtype),
                pltpu.VMEM((pixels, count), basis.dtype),
                pltpu.VMEM((1, pixels), phantom.dtype),
                pltpu.SemaphoreType.DMA((steps + 2,)),
            ],
        ),
        out_shape=[out] * pieces,
        compiler_params=SMALL,
        name="project",
    )(block, inject, images, basis, phantom)
    return tuple(found)


def whole(kernel, name, operands, shapes, at=None, scratch=(), params=SMALL):
    lead = [] if at is None else [at]
    return pl.pallas_call(
        kernel,
        in_specs=[pl.BlockSpec(memory_space=pltpu.SMEM)] * len(lead)
        + [pl.BlockSpec(memory_space=pltpu.VMEM)] * len(operands),
        out_specs=[pl.BlockSpec(memory_space=pltpu.VMEM)] * len(shapes),
        out_shape=[jax.ShapeDtypeStruct(shape, dtype) for shape, dtype in shapes],
        scratch_shapes=list(scratch),
        compiler_params=params,
        name=name,
    )(*lead, *operands)


def relay_kernel(here_a, here_b, came_a, came_b, low, high):
    members = low.shape[0]
    for side, out in enumerate((low, high)):
        for q in range(members):
            cut = slice((side * members + q) * 8, (side * members + q + 1) * 8)
            out[q, :8, :] = here_a[cut, :] + came_a[cut, :]
            out[q, 8:, :] = here_b[cut, :] + came_b[cut, :]


def relayed(here, came):
    count, rows = here[0].shape
    shape = ((count // 16, 16, rows), jnp.float32)
    return whole(relay_kernel, "relay", (*here, *came), [shape, shape])


def join_kernel(here_a, here_b, came_a, came_b, low, high, out):
    members = low.shape[0]
    for side, other in enumerate((low, high)):
        for q in range(members):
            m = side * members + q
            cut = slice(m * 8, (m + 1) * 8)
            out[m, :8, :] = here_a[cut, :] + came_a[cut, :] + other[q, :8, :]
            out[m, 8:, :] = here_b[cut, :] + came_b[cut, :] + other[q, 8:, :]


def joined(here, came, others):
    count, rows = here[0].shape
    shape = ((count // 8, 16, rows), jnp.float32)
    return whole(join_kernel, "join", (*here, *came, *others), [shape])[0]


def spread_kernel(parts, out):
    width = 256

    def column(j, carry):
        cut = pl.ds(pl.multiple_of(j * width, width), width)
        total = parts[0, :, cut]
        for k in range(1, parts.shape[0]):
            total = total + parts[k, :, cut]
        for k in range(out.shape[0]):
            out[k, :, cut] = total
        return carry

    lax.fori_loop(0, parts.shape[2] // width, column, 0)


def summed_copies(parts):
    return whole(spread_kernel, "spread", (parts,), [(parts.shape, jnp.float32)])[0]


def peel_kernel(low, high, out_a, out_b):
    middle = low.shape[0]
    for offset, source in ((0, low), (middle, high)):
        out_a[offset : offset + middle] = source[:, :8, :]
        out_b[offset : offset + middle] = source[:, 8:, :]


def peeled(low, high):
    members, _, rows = low.shape
    shape = ((2 * members, 8, rows), jnp.float32)
    return whole(peel_kernel, "peel", (low, high), [shape, shape])


def put_block(at, rounded, cut, which, offset, block):
    count = block.shape[0] * block.shape[1]
    place = at[which] * (rounded.shape[0] // 4) + offset
    place = pl.multiple_of(place, rounded.shape[0] // 16)
    rounded[pl.ds(place, count), cut] = block.reshape(count, -1).astype(jnp.bfloat16)


def stage_kernel(at, own, low, high, near_a, near_b, staged):
    width = 256
    half = staged.shape[0] // 8
    quarter = half // 2

    def column(step, carry):
        cut = pl.ds(pl.multiple_of(step * width, width), width)
        put = functools.partial(put_block, at, staged, cut)
        put(0, 0, jnp.zeros((16, 8, width), jnp.float32))
        put(1, 0, near_a[:, :, cut])
        put(1, half, near_b[:, :, cut])
        for offset, source in ((0, low), (quarter, high)):
            put(2, offset, source[:, :8, cut])
            put(2, half + offset, source[:, 8:, cut])
        put(3, 0, own[:, :8, cut])
        put(3, half, own[:, 8:, cut])
        return carry

    lax.fori_loop(0, staged.shape[1] // width, column, 0)


def staged_of(at, held):
    members, high, rows = held[0].shape
    shape = ((members * high * 4, rows), jnp.bfloat16)
    return whole(stage_kernel, "stage", held, [shape], at=at)[0]


def score_kernel(at, staged, far_a, far_b, prior, refs_t, powers, rounded, stats):
    width = 256
    orient, eigen = refs_t.shape
    lines = stats.shape[1] // 2

    def column(step, carry):
        cut = pl.ds(pl.multiple_of(step * width, width), width)
        rounded[:, cut] = staged[:, cut]
        put_block(at, rounded, cut, 0, 0, far_a[:, :, cut])
        put_block(at, rounded, cut, 0, eigen // 8, far_b[:, :, cut])
        scores = jnp.dot(refs_t[...], rounded[:, cut], preferred_element_type=jnp.float32)
        block = prior[:, cut] - at[4] * (orient // OBLOCK)
        parts = [
            (scores[k * OBLOCK : (k + 1) * OBLOCK], jnp.where(block == k, PRIOR_INCREMENT, 0.0))
            for k in range(orient // OBLOCK)
        ]
        tops = [jnp.max(part, axis=0, keepdims=True) + bonus for part, bonus in parts]
        top = tops[0]
        for other in tops[1:]:
            top = jnp.maximum(top, other)
        total = jnp.zeros_like(top)
        for k, (part, bonus) in enumerate(parts):
            power = jnp.exp(part - (top - bonus))
            powers[k * OBLOCK : (k + 1) * OBLOCK, cut] = power
            total = total + jnp.sum(power, axis=0, keepdims=True)
        for h in range(width // LANES):
            line = step * (width // LANES) + h
            side = slice(h * LANES, (h + 1) * LANES)
            shape = (stats.shape[0], 1, LANES)
            stats[:, pl.ds(line, 1), :] = jnp.broadcast_to(top[None, :, side], shape)
            stats[:, pl.ds(lines + line, 1), :] = jnp.broadcast_to(total[None, :, side], shape)
        return carry

    lax.fori_loop(0, powers.shape[1] // width, column, 0)


def scores_of(at, held, prior, refs_t, members):
    rows = prior.shape[1]
    orient, eigen = refs_t.shape
    shapes = [
        ((orient, rows), jnp.float32),
        ((eigen, rows), jnp.bfloat16),
        ((members, 2 * rows // LANES, LANES), jnp.float32),
    ]
    return whole(score_kernel, "scores", (*held, prior, refs_t), shapes, at=at, params=BIG)


def total_kernel(other, outer, at, stats, own, powers, rounded, out, factor, mine):
    width = 256
    eigen, rows = rounded.shape
    peers = out.shape[0]
    share = eigen // (2 * peers)
    lines = rows // LANES
    body = out.shape[1] - out.shape[1] % share
    tops = stats[:, :lines, :]
    top = jnp.max(tops, axis=0)
    total = jnp.sum(stats[:, lines:, :] * jnp.exp(tops - top[None]), axis=0)
    scale = jnp.exp(own[0, :lines, :] - top) / total
    for k in range(lines):
        factor[:, k * LANES : (k + 1) * LANES] = scale[k : k + 1, :]
    core = 1 - at[5] if other else at[5]
    for q in range(peers):
        owner = q % (peers // outer) * outer + q // (peers // outer)
        place = pl.multiple_of((2 * owner + core) * share, share)
        mine[q * share : (q + 1) * share, :] = rounded[pl.ds(place, share), :]
    ones = jnp.ones((16, rows), jnp.bfloat16)

    def orients(step, carry):
        block = powers[pl.ds(pl.multiple_of(step * width, width), width), :]
        weights = (block * factor[...]).astype(jnp.bfloat16)
        totals = lax.dot_general(mine[...], weights, LAST, preferred_element_type=jnp.float32)
        masses = lax.dot_general(ones, weights, LAST, preferred_element_type=jnp.float32)
        for h in range(width // LANES):
            column = step * (width // LANES) + h
            cut = slice(h * LANES, (h + 1) * LANES)
            place = pl.ds(pl.multiple_of(column * share, share), share)
            for q in range(peers):
                out[q, place, :] = totals[q * share : (q + 1) * share, cut]
            mass = jnp.broadcast_to(masses[None, 0:1, cut], (peers, 1, LANES))
            out[:, pl.ds(body + column, 1), :] = mass
        return carry

    lax.fori_loop(0, powers.shape[0] // width, orients, 0)


def totals_of(other, at, stats, sent, powers, rounded, peers):
    eigen, rows = rounded.shape
    orient = powers.shape[0]
    deep = (eigen // (2 * peers) + 1) * (orient // LANES)
    return whole(
        functools.partial(total_kernel, other, lax.axis_size(PEERS[0])),
        "totals",
        (stats, sent, powers, rounded),
        [((peers, deep, LANES), jnp.float32)],
        at=at,
        scratch=[pltpu.VMEM((1, rows), jnp.float32), pltpu.VMEM((eigen // 2, rows), jnp.bfloat16)],
        params=BIG,
    )[0]


def final_kernel(at, parts, refs, out):
    share, orient = out.shape
    both = parts[0]
    for d in range(1, parts.shape[0]):
        both = both + parts[d]
    body = share * (orient // LANES)
    for k in range(orient // LANES):
        cut = slice(k * LANES, (k + 1) * LANES)
        above = both[k * share : (k + 1) * share] + refs[:, cut].astype(jnp.float32)
        out[:, cut] = above / (both[body + k : body + k + 1] + 1.0)


def final_of(at, parts, refs):
    eigen, orient = refs.shape
    share = eigen // (2 * parts.shape[0])
    return pl.pallas_call(
        final_kernel,
        grid_spec=pltpu.PrefetchScalarGridSpec(
            num_scalar_prefetch=1,
            grid=(1,),
            in_specs=[
                pl.BlockSpec(parts.shape, lambda j, at: (0, 0, 0)),
                pl.BlockSpec((share, orient), lambda j, at: (at[6], 0)),
            ],
            out_specs=pl.BlockSpec((share, orient), lambda j, at: (0, 0)),
        ),
        out_shape=jax.ShapeDtypeStruct((share, orient), jnp.float32),
        compiler_params=SMALL,
        name="final",
    )(at, parts, refs)


def swapped(pair, axis):
    size = lax.axis_size(axis)
    with_a = [(i, i ^ 1) for i in range(size)]
    with_b = [(i, (i + (1 if i % 2 else -1)) % size) for i in range(size)]
    return tuple(lax.ppermute(x, axis, p) for x, p in zip(pair, (with_a, with_b)))


def shards(images, phantom, inject_rows, prior_blocks, basis, refs):
    rows = images.shape[1] * images.shape[2]
    flat = images[0].reshape(rows, basis.shape[0])
    p, q = lax.axis_index("yl"), lax.axis_index("zhl")
    at = jnp.stack(
        [
            (1 - p) * 2 + 1 - q,
            (1 - p) * 2 + q,
            p * 2 + 1 - q,
            p * 2 + q,
            lax.axis_index(MEM),
            lax.axis_index("core"),
            lax.axis_index(GRP),
        ]
    ).astype(jnp.int32)
    def block(which):
        return projected(which, inject_rows[0], flat, basis, phantom, 2)

    through = swapped(block(at[0:1]), RING)
    turned = relayed(block(at[2:3]), through)
    kept = block(at[3:4])
    low, high, after = lax.optimization_barrier((*turned, at[1:2]))
    others = swapped((low, high), TALL)
    came = swapped(block(after), RING)
    parts = joined(kept, came, others)
    parts = lax.all_to_all(parts, ALIKE, 0, 0, tiled=True)
    own = lax.all_to_all(summed_copies(parts), ALIKE, 0, 0, tiled=True)
    middle = own.shape[0] // 2
    low, high = swapped((own[:middle], own[middle:]), TALL)
    near = swapped((own[:, :8], own[:, 8:]), RING)
    far = swapped(peeled(low, high), RING)
    powers, rounded, sent = scores_of(
        at,
        (staged_of(at, (own, low, high, *near)), *far),
        prior_blocks[0].reshape(1, rows),
        refs.T,
        lax.axis_size(MEM),
    )
    stats = lax.all_to_all(sent, EVERY, 0, 0, tiled=True)
    sums = (stats, sent, powers, rounded, lax.axis_size(PEERS))
    came = lax.ppermute(totals_of(True, at, *sums), "core", [(0, 1), (1, 0)])
    parts = totals_of(False, at, *sums) + came
    parts = lax.all_to_all(parts, PEERS, 0, 0, tiled=True)
    return final_of(at, parts, refs)


def solution(mesh):
    fine = Mesh(mesh.devices.reshape(4, 2, 2, 4, 2, 2, 2), GRP + MEM)
    placed = (
        P(GRP, None, None, MEM),
        P(GRP, MEM),
        P(GRP, None, None),
        P(GRP, None, None),
        P(MEM, None),
        P(None, MEM),
    )
    return jax.shard_map(
        shards, mesh=fine, in_specs=placed, out_specs=P(GRP, MEM), check_vma=False
    )
```

```python
import functools

import jax
import jax.numpy as jnp
from jax import lax
from jax.experimental import pallas as pl
from jax.experimental.pallas import tpu as pltpu
from jax.sharding import Mesh, PartitionSpec as P

OBLOCK = 256
PRIOR_INCREMENT = 3.0
GRP = ("x", "zl", "core")
RING = ("yh", "yl")
TALL = ("zhh", "zhl")
MEM = RING + TALL
ALIKE = ("yh", "zhh")
EVERY = ("zhl", "zhh", "yl", "yh")
PEERS = ("zl", "x")
LANES = 128
BIG = pltpu.CompilerParams(vmem_limit_bytes=16 << 20)
SMALL = pltpu.CompilerParams(vmem_limit_bytes=8 << 20)
LAST = (((1,), (1,)), ((), ()))


def project_kernel(at, inject, images, basis, phantom, *rest):
    outs, (pixels_in, columns, ghost, sems) = rest[:-4], rest[-4:]
    which = pixels_in.shape[0]
    width = pixels_in.shape[1]
    count = columns.shape[1]
    first = pl.multiple_of(at[0] * count, count)
    loads = [
        pltpu.make_async_copy(basis.at[:, pl.ds(first, count)], columns, sems.at[which]),
        pltpu.make_async_copy(phantom, ghost, sems.at[which + 1]),
    ] + [
        pltpu.make_async_copy(images.at[pl.ds(k * width, width), :], pixels_in.at[k], sems.at[k])
        for k in range(which)
    ]
    for load in loads:
        load.start()
    per_batch = which // inject.shape[0]
    hits = []
    for k in range(which):
        position = (k % per_batch) * width + lax.broadcasted_iota(jnp.int32, (1, width), 1)
        hit = jnp.zeros((1, width), jnp.float32)
        for i in range(inject.shape[1]):
            hit = jnp.where(position == inject[k // per_batch, i], 1.0, hit)
        hits.append(hit)
    loads[0].wait()
    loads[1].wait()
    mine = columns[...].T
    spread = jnp.broadcast_to(ghost[...], (LANES, ghost.shape[1]))
    extra = lax.dot_general(mine, spread, LAST, preferred_element_type=jnp.float32)
    share = count // len(outs)
    for k in range(which):
        loads[2 + k].wait()
        plain = lax.dot_general(mine, pixels_in[k], LAST, preferred_element_type=jnp.float32)
        for c in range(width // LANES):
            cut = slice(c * LANES, (c + 1) * LANES)
            value = plain[:, cut] + extra * hits[k][:, cut]
            for j, out in enumerate(outs):
                out[:, k * width + c * LANES : k * width + (c + 1) * LANES] = value[
                    j * share : (j + 1) * share
                ]


def projected(block, inject, images, basis, phantom, pieces):
    rows, pixels = images.shape
    steps = 2 * inject.shape[0]
    count = basis.shape[1] // 4
    out = jax.ShapeDtypeStruct((count // pieces, rows), jnp.float32)
    inject, images, basis, phantom = (
        pltpu.with_memory_space_constraint(x, pltpu.HBM) for x in (inject, images, basis, phantom)
    )
    found = pl.pallas_call(
        project_kernel,
        grid_spec=pltpu.PrefetchScalarGridSpec(
            num_scalar_prefetch=2,
            grid=(1,),
            in_specs=[pl.BlockSpec(memory_space=pltpu.HBM)] * 3,
            out_specs=[pl.BlockSpec(out.shape, lambda j, at, s: (0, 0))] * pieces,
            scratch_shapes=[
                pltpu.VMEM((steps, rows // steps, pixels), images.dtype),
                pltpu.VMEM((pixels, count), basis.dtype),
                pltpu.VMEM((1, pixels), phantom.dtype),
                pltpu.SemaphoreType.DMA((steps + 2,)),
            ],
        ),
        out_shape=[out] * pieces,
        compiler_params=SMALL,
        name="project",
    )(block, inject, images, basis, phantom)
    return tuple(found)


def whole(kernel, name, operands, shapes, at=None, scratch=(), params=SMALL):
    lead = [] if at is None else [at]
    return pl.pallas_call(
        kernel,
        in_specs=[pl.BlockSpec(memory_space=pltpu.SMEM)] * len(lead)
        + [pl.BlockSpec(memory_space=pltpu.VMEM)] * len(operands),
        out_specs=[pl.BlockSpec(memory_space=pltpu.VMEM)] * len(shapes),
        out_shape=[jax.ShapeDtypeStruct(shape, dtype) for shape, dtype in shapes],
        scratch_shapes=list(scratch),
        compiler_params=params,
        name=name,
    )(*lead, *operands)


def relay_kernel(here_a, here_b, came_a, came_b, low, high):
    members = low.shape[0]
    for side, out in enumerate((low, high)):
        for q in range(members):
            cut = slice((side * members + q) * 8, (side * members + q + 1) * 8)
            out[q, :8, :] = here_a[cut, :] + came_a[cut, :]
            out[q, 8:, :] = here_b[cut, :] + came_b[cut, :]


def relayed(here, came):
    count, rows = here[0].shape
    shape = ((count // 16, 16, rows), jnp.float32)
    return whole(relay_kernel, "relay", (*here, *came), [shape, shape])


def join_kernel(here_a, here_b, came_a, came_b, low, high, out):
    members = low.shape[0]
    for side, other in enumerate((low, high)):
        for q in range(members):
            m = side * members + q
            cut = slice(m * 8, (m + 1) * 8)
            out[m, :8, :] = here_a[cut, :] + came_a[cut, :] + other[q, :8, :]
            out[m, 8:, :] = here_b[cut, :] + came_b[cut, :] + other[q, 8:, :]


def joined(here, came, others):
    count, rows = here[0].shape
    shape = ((count // 8, 16, rows), jnp.float32)
    return whole(join_kernel, "join", (*here, *came, *others), [shape])[0]


def spread_kernel(parts, out):
    width = 256

    def column(j, carry):
        cut = pl.ds(pl.multiple_of(j * width, width), width)
        total = parts[0, :, cut]
        for k in range(1, parts.shape[0]):
            total = total + parts[k, :, cut]
        for k in range(out.shape[0]):
            out[k, :, cut] = total
        return carry

    lax.fori_loop(0, parts.shape[2] // width, column, 0)


def summed_copies(parts):
    return whole(spread_kernel, "spread", (parts,), [(parts.shape, jnp.float32)])[0]


def peel_kernel(low, high, out_a, out_b):
    middle = low.shape[0]
    for offset, source in ((0, low), (middle, high)):
        out_a[offset : offset + middle] = source[:, :8, :]
        out_b[offset : offset + middle] = source[:, 8:, :]


def peeled(low, high):
    members, _, rows = low.shape
    shape = ((2 * members, 8, rows), jnp.float32)
    return whole(peel_kernel, "peel", (low, high), [shape, shape])


def put_block(at, rounded, cut, which, offset, block):
    count = block.shape[0] * block.shape[1]
    place = at[which] * (rounded.shape[0] // 4) + offset
    place = pl.multiple_of(place, rounded.shape[0] // 16)
    rounded[pl.ds(place, count), cut] = block.reshape(count, -1).astype(jnp.bfloat16)


def stage_kernel(at, own, low, high, near_a, near_b, staged):
    width = 256
    half = staged.shape[0] // 8
    quarter = half // 2

    def column(step, carry):
        cut = pl.ds(pl.multiple_of(step * width, width), width)
        put = functools.partial(put_block, at, staged, cut)
        put(0, 0, jnp.zeros((16, 8, width), jnp.float32))
        put(1, 0, near_a[:, :, cut])
        put(1, half, near_b[:, :, cut])
        for offset, source in ((0, low), (quarter, high)):
            put(2, offset, source[:, :8, cut])
            put(2, half + offset, source[:, 8:, cut])
        put(3, 0, own[:, :8, cut])
        put(3, half, own[:, 8:, cut])
        return carry

    lax.fori_loop(0, staged.shape[1] // width, column, 0)


def staged_of(at, held):
    members, high, rows = held[0].shape
    shape = ((members * high * 4, rows), jnp.bfloat16)
    return whole(stage_kernel, "stage", held, [shape], at=at)[0]


def score_kernel(at, staged, far_a, far_b, prior, refs_t, powers, rounded, stats):
    width = 256
    orient, eigen = refs_t.shape
    lines = stats.shape[1] // 2

    def column(step, carry):
        cut = pl.ds(pl.multiple_of(step * width, width), width)
        rounded[:, cut] = staged[:, cut]
        put_block(at, rounded, cut, 0, 0, far_a[:, :, cut])
        put_block(at, rounded, cut, 0, eigen // 8, far_b[:, :, cut])
        scores = jnp.dot(refs_t[...], rounded[:, cut], preferred_element_type=jnp.float32)
        block = prior[:, cut] - at[4] * (orient // OBLOCK)
        parts = [
            (scores[k * OBLOCK : (k + 1) * OBLOCK], jnp.where(block == k, PRIOR_INCREMENT, 0.0))
            for k in range(orient // OBLOCK)
        ]
        tops = [jnp.max(part, axis=0, keepdims=True) + bonus for part, bonus in parts]
        top = tops[0]
        for other in tops[1:]:
            top = jnp.maximum(top, other)
        total = jnp.zeros_like(top)
        for k, (part, bonus) in enumerate(parts):
            power = jnp.exp(part - (top - bonus))
            powers[k * OBLOCK : (k + 1) * OBLOCK, cut] = power.astype(jnp.bfloat16)
            total = total + jnp.sum(power, axis=0, keepdims=True)
        for h in range(width // LANES):
            line = step * (width // LANES) + h
            side = slice(h * LANES, (h + 1) * LANES)
            shape = (stats.shape[0], 1, LANES)
            stats[:, pl.ds(line, 1), :] = jnp.broadcast_to(top[None, :, side], shape)
            stats[:, pl.ds(lines + line, 1), :] = jnp.broadcast_to(total[None, :, side], shape)
        return carry

    lax.fori_loop(0, powers.shape[1] // width, column, 0)


def scores_of(at, held, prior, refs_t, members):
    rows = prior.shape[1]
    orient, eigen = refs_t.shape
    shapes = [
        ((orient, rows), jnp.bfloat16),
        ((eigen, rows), jnp.bfloat16),
        ((members, 2 * rows // LANES, LANES), jnp.float32),
    ]
    return whole(score_kernel, "scores", (*held, prior, refs_t), shapes, at=at, params=BIG)


def total_kernel(other, outer, at, stats, own, powers, rounded, out, factor, mine):
    width = 256
    eigen, rows = rounded.shape
    peers = out.shape[0]
    share = eigen // (2 * peers)
    lines = rows // LANES
    body = out.shape[1] - out.shape[1] % share
    tops = stats[:, :lines, :]
    top = jnp.max(tops, axis=0)
    total = jnp.sum(stats[:, lines:, :] * jnp.exp(tops - top[None]), axis=0)
    scale = jnp.exp(own[0, :lines, :] - top) / total
    for k in range(lines):
        factor[:, k * LANES : (k + 1) * LANES] = scale[k : k + 1, :]
    core = 1 - at[5] if other else at[5]
    for q in range(peers):
        owner = q % (peers // outer) * outer + q // (peers // outer)
        place = pl.multiple_of((2 * owner + core) * share, share)
        mine[q * share : (q + 1) * share, :] = rounded[pl.ds(place, share), :]
    ones = jnp.ones((16, rows), jnp.bfloat16)

    def orients(step, carry):
        block = powers[pl.ds(pl.multiple_of(step * width, width), width), :]
        weights = (block.astype(jnp.float32) * factor[...]).astype(jnp.bfloat16)
        totals = lax.dot_general(mine[...], weights, LAST, preferred_element_type=jnp.float32)
        masses = lax.dot_general(ones, weights, LAST, preferred_element_type=jnp.float32)
        for h in range(width // LANES):
            column = step * (width // LANES) + h
            cut = slice(h * LANES, (h + 1) * LANES)
            place = pl.ds(pl.multiple_of(column * share, share), share)
            for q in range(peers):
                out[q, place, :] = totals[q * share : (q + 1) * share, cut]
            mass = jnp.broadcast_to(masses[None, 0:1, cut], (peers, 1, LANES))
            out[:, pl.ds(body + column, 1), :] = mass
        return carry

    lax.fori_loop(0, powers.shape[0] // width, orients, 0)


def totals_of(other, at, stats, sent, powers, rounded, peers):
    eigen, rows = rounded.shape
    orient = powers.shape[0]
    deep = (eigen // (2 * peers) + 1) * (orient // LANES)
    return whole(
        functools.partial(total_kernel, other, lax.axis_size(PEERS[0])),
        "totals",
        (stats, sent, powers, rounded),
        [((peers, deep, LANES), jnp.float32)],
        at=at,
        scratch=[pltpu.VMEM((1, rows), jnp.float32), pltpu.VMEM((eigen // 2, rows), jnp.bfloat16)],
        params=BIG,
    )[0]


def final_kernel(at, parts, refs, out):
    share, orient = out.shape
    both = parts[0]
    for d in range(1, parts.shape[0]):
        both = both + parts[d]
    body = share * (orient // LANES)
    for k in range(orient // LANES):
        cut = slice(k * LANES, (k + 1) * LANES)
        above = both[k * share : (k + 1) * share] + refs[:, cut].astype(jnp.float32)
        out[:, cut] = above / (both[body + k : body + k + 1] + 1.0)


def final_of(at, parts, refs):
    eigen, orient = refs.shape
    share = eigen // (2 * parts.shape[0])
    return pl.pallas_call(
        final_kernel,
        grid_spec=pltpu.PrefetchScalarGridSpec(
            num_scalar_prefetch=1,
            grid=(1,),
            in_specs=[
                pl.BlockSpec(parts.shape, lambda j, at: (0, 0, 0)),
                pl.BlockSpec((share, orient), lambda j, at: (at[6], 0)),
            ],
            out_specs=pl.BlockSpec((share, orient), lambda j, at: (0, 0)),
        ),
        out_shape=jax.ShapeDtypeStruct((share, orient), jnp.float32),
        compiler_params=SMALL,
        name="final",
    )(at, parts, refs)


def swapped(pair, axis):
    size = lax.axis_size(axis)
    with_a = [(i, i ^ 1) for i in range(size)]
    with_b = [(i, (i + (1 if i % 2 else -1)) % size) for i in range(size)]
    return tuple(lax.ppermute(x, axis, p) for x, p in zip(pair, (with_a, with_b)))


def shards(images, phantom, inject_rows, prior_blocks, basis, refs):
    rows = images.shape[1] * images.shape[2]
    flat = images[0].reshape(rows, basis.shape[0])
    p, q = lax.axis_index("yl"), lax.axis_index("zhl")
    at = jnp.stack(
        [
            (1 - p) * 2 + 1 - q,
            (1 - p) * 2 + q,
            p * 2 + 1 - q,
            p * 2 + q,
            lax.axis_index(MEM),
            lax.axis_index("core"),
            lax.axis_index(GRP),
        ]
    ).astype(jnp.int32)
    def block(which):
        return projected(which, inject_rows[0], flat, basis, phantom, 2)

    through = swapped(block(at[0:1]), RING)
    turned = relayed(block(at[2:3]), through)
    kept = block(at[3:4])
    low, high, after = lax.optimization_barrier((*turned, at[1:2]))
    others = swapped((low, high), TALL)
    came = swapped(block(after), RING)
    parts = joined(kept, came, others)
    parts = lax.all_to_all(parts, ALIKE, 0, 0, tiled=True)
    own = lax.all_to_all(summed_copies(parts), ALIKE, 0, 0, tiled=True)
    middle = own.shape[0] // 2
    low, high = swapped((own[:middle], own[middle:]), TALL)
    near = swapped((own[:, :8], own[:, 8:]), RING)
    far = swapped(peeled(low, high), RING)
    powers, rounded, sent = scores_of(
        at,
        (staged_of(at, (own, low, high, *near)), *far),
        prior_blocks[0].reshape(1, rows),
        refs.T,
        lax.axis_size(MEM),
    )
    stats = lax.all_to_all(sent, EVERY, 0, 0, tiled=True)
    sums = (stats, sent, powers, rounded, lax.axis_size(PEERS))
    came = lax.ppermute(totals_of(True, at, *sums), "core", [(0, 1), (1, 0)])
    parts = totals_of(False, at, *sums) + came
    parts = lax.all_to_all(parts, PEERS, 0, 0, tiled=True)
    return final_of(at, parts, refs)


def solution(mesh):
    fine = Mesh(mesh.devices.reshape(4, 2, 2, 4, 2, 2, 2), GRP + MEM)
    placed = (
        P(GRP, None, None, MEM),
        P(GRP, MEM),
        P(GRP, None, None),
        P(GRP, None, None),
        P(MEM, None),
        P(None, MEM),
    )
    return jax.shard_map(
        shards, mesh=fine, in_specs=placed, out_specs=P(GRP, MEM), check_vma=False
    )
```

```python
import functools

import jax
import jax.numpy as jnp
from jax import lax
from jax.experimental import pallas as pl
from jax.experimental.pallas import tpu as pltpu
from jax.sharding import Mesh, PartitionSpec as P

OBLOCK = 256
PRIOR_INCREMENT = 3.0
GRP = ("x", "zl", "core")
RING = ("yh", "yl")
TALL = ("zhh", "zhl")
MEM = RING + TALL
ALIKE = ("yh", "zhh")
EVERY = ("zhl", "zhh", "yl", "yh")
PEERS = ("zl", "x")
LANES = 128
BIG = pltpu.CompilerParams(vmem_limit_bytes=16 << 20)
SMALL = pltpu.CompilerParams(vmem_limit_bytes=8 << 20)
LAST = (((1,), (1,)), ((), ()))


def project_kernel(at, inject, images, basis, phantom, *rest):
    outs, (pixels_in, columns, ghost, sems) = rest[:-4], rest[-4:]
    which = pixels_in.shape[0]
    width = pixels_in.shape[1]
    count = columns.shape[1]
    first = pl.multiple_of(at[0] * count, count)
    loads = [
        pltpu.make_async_copy(basis.at[:, pl.ds(first, count)], columns, sems.at[which]),
        pltpu.make_async_copy(phantom, ghost, sems.at[which + 1]),
    ] + [
        pltpu.make_async_copy(images.at[pl.ds(k * width, width), :], pixels_in.at[k], sems.at[k])
        for k in range(which)
    ]
    for load in loads:
        load.start()
    per_batch = which // inject.shape[0]
    hits = []
    for k in range(which):
        position = (k % per_batch) * width + lax.broadcasted_iota(jnp.int32, (1, width), 1)
        hit = jnp.zeros((1, width), jnp.float32)
        for i in range(inject.shape[1]):
            hit = jnp.where(position == inject[k // per_batch, i], 1.0, hit)
        hits.append(hit)
    loads[0].wait()
    loads[1].wait()
    mine = columns[...].T
    spread = jnp.broadcast_to(ghost[...], (LANES, ghost.shape[1]))
    extra = lax.dot_general(mine, spread, LAST, preferred_element_type=jnp.float32)
    share = count // len(outs)
    for k in range(which):
        loads[2 + k].wait()
        plain = lax.dot_general(mine, pixels_in[k], LAST, preferred_element_type=jnp.float32)
        for c in range(width // LANES):
            cut = slice(c * LANES, (c + 1) * LANES)
            value = plain[:, cut] + extra * hits[k][:, cut]
            for j, out in enumerate(outs):
                out[:, k * width + c * LANES : k * width + (c + 1) * LANES] = value[
                    j * share : (j + 1) * share
                ]


def projected(block, inject, images, basis, phantom, pieces):
    rows, pixels = images.shape
    steps = 2 * inject.shape[0]
    count = basis.shape[1] // 4
    out = jax.ShapeDtypeStruct((count // pieces, rows), jnp.float32)
    inject, images, basis, phantom = (
        pltpu.with_memory_space_constraint(x, pltpu.HBM) for x in (inject, images, basis, phantom)
    )
    found = pl.pallas_call(
        project_kernel,
        grid_spec=pltpu.PrefetchScalarGridSpec(
            num_scalar_prefetch=2,
            grid=(1,),
            in_specs=[pl.BlockSpec(memory_space=pltpu.HBM)] * 3,
            out_specs=[pl.BlockSpec(out.shape, lambda j, at, s: (0, 0))] * pieces,
            scratch_shapes=[
                pltpu.VMEM((steps, rows // steps, pixels), images.dtype),
                pltpu.VMEM((pixels, count), basis.dtype),
                pltpu.VMEM((1, pixels), phantom.dtype),
                pltpu.SemaphoreType.DMA((steps + 2,)),
            ],
        ),
        out_shape=[out] * pieces,
        compiler_params=SMALL,
        name="project",
    )(block, inject, images, basis, phantom)
    return tuple(found)


def whole(kernel, name, operands, shapes, at=None, scratch=(), params=SMALL):
    lead = [] if at is None else [at]
    return pl.pallas_call(
        kernel,
        in_specs=[pl.BlockSpec(memory_space=pltpu.SMEM)] * len(lead)
        + [pl.BlockSpec(memory_space=pltpu.VMEM)] * len(operands),
        out_specs=[pl.BlockSpec(memory_space=pltpu.VMEM)] * len(shapes),
        out_shape=[jax.ShapeDtypeStruct(shape, dtype) for shape, dtype in shapes],
        scratch_shapes=list(scratch),
        compiler_params=params,
        name=name,
    )(*lead, *operands)


def relay_kernel(here_a, here_b, came_a, came_b, low, high):
    members = low.shape[0]
    for side, out in enumerate((low, high)):
        for q in range(members):
            cut = slice((side * members + q) * 8, (side * members + q + 1) * 8)
            out[q, :8, :] = here_a[cut, :] + came_a[cut, :]
            out[q, 8:, :] = here_b[cut, :] + came_b[cut, :]


def relayed(here, came):
    count, rows = here[0].shape
    shape = ((count // 16, 16, rows), jnp.float32)
    return whole(relay_kernel, "relay", (*here, *came), [shape, shape])


def join_kernel(here_a, here_b, came_a, came_b, low, high, out):
    members = low.shape[0]
    for side, other in enumerate((low, high)):
        for q in range(members):
            m = side * members + q
            cut = slice(m * 8, (m + 1) * 8)
            out[m, :8, :] = here_a[cut, :] + came_a[cut, :] + other[q, :8, :]
            out[m, 8:, :] = here_b[cut, :] + came_b[cut, :] + other[q, 8:, :]


def joined(here, came, others):
    count, rows = here[0].shape
    shape = ((count // 8, 16, rows), jnp.float32)
    return whole(join_kernel, "join", (*here, *came, *others), [shape])[0]


def spread_kernel(parts, out):
    width = 256

    def column(j, carry):
        cut = pl.ds(pl.multiple_of(j * width, width), width)
        total = parts[0, :, cut]
        for k in range(1, parts.shape[0]):
            total = total + parts[k, :, cut]
        for k in range(out.shape[0]):
            out[k, :, cut] = total
        return carry

    lax.fori_loop(0, parts.shape[2] // width, column, 0)


def summed_copies(parts):
    return whole(spread_kernel, "spread", (parts,), [(parts.shape, jnp.float32)])[0]


def peel_kernel(low, high, out_a, out_b):
    middle = low.shape[0]
    for offset, source in ((0, low), (middle, high)):
        out_a[offset : offset + middle] = source[:, :8, :]
        out_b[offset : offset + middle] = source[:, 8:, :]


def peeled(low, high):
    members, _, rows = low.shape
    shape = ((2 * members, 8, rows), jnp.float32)
    return whole(peel_kernel, "peel", (low, high), [shape, shape])


def put_block(at, rounded, cut, which, offset, block):
    count = block.shape[0] * block.shape[1]
    place = at[which] * (rounded.shape[0] // 4) + offset
    place = pl.multiple_of(place, rounded.shape[0] // 16)
    rounded[pl.ds(place, count), cut] = block.reshape(count, -1).astype(jnp.bfloat16)


def stage_kernel(at, own, low, high, near_a, near_b, staged):
    width = 256
    half = staged.shape[0] // 8
    quarter = half // 2

    def column(step, carry):
        cut = pl.ds(pl.multiple_of(step * width, width), width)
        put = functools.partial(put_block, at, staged, cut)
        put(0, 0, jnp.zeros((16, 8, width), jnp.float32))
        put(1, 0, near_a[:, :, cut])
        put(1, half, near_b[:, :, cut])
        for offset, source in ((0, low), (quarter, high)):
            put(2, offset, source[:, :8, cut])
            put(2, half + offset, source[:, 8:, cut])
        put(3, 0, own[:, :8, cut])
        put(3, half, own[:, 8:, cut])
        return carry

    lax.fori_loop(0, staged.shape[1] // width, column, 0)


def staged_of(at, held):
    members, high, rows = held[0].shape
    shape = ((members * high * 4, rows), jnp.bfloat16)
    return whole(stage_kernel, "stage", held, [shape], at=at)[0]


def score_kernel(at, staged, far_a, far_b, prior, refs_t, powers, rounded, stats):
    width = 256
    orient, eigen = refs_t.shape
    lines = stats.shape[1] // 2

    def column(step, carry):
        cut = pl.ds(pl.multiple_of(step * width, width), width)
        rounded[:, cut] = staged[:, cut]
        put_block(at, rounded, cut, 0, 0, far_a[:, :, cut])
        put_block(at, rounded, cut, 0, eigen // 8, far_b[:, :, cut])
        scores = jnp.dot(refs_t[...], rounded[:, cut], preferred_element_type=jnp.float32)
        block = prior[:, cut] - at[4] * (orient // OBLOCK)
        parts = [
            (scores[k * OBLOCK : (k + 1) * OBLOCK], jnp.where(block == k, PRIOR_INCREMENT, 0.0))
            for k in range(orient // OBLOCK)
        ]
        tops = [jnp.max(part, axis=0, keepdims=True) + bonus for part, bonus in parts]
        top = tops[0]
        for other in tops[1:]:
            top = jnp.maximum(top, other)
        total = jnp.zeros_like(top)
        for k, (part, bonus) in enumerate(parts):
            power = jnp.exp(part - (top - bonus))
            powers[k * OBLOCK : (k + 1) * OBLOCK, cut] = power
            total = total + jnp.sum(power, axis=0, keepdims=True)
        for h in range(width // LANES):
            line = step * (width // LANES) + h
            side = slice(h * LANES, (h + 1) * LANES)
            shape = (stats.shape[0], 1, LANES)
            stats[:, pl.ds(line, 1), :] = jnp.broadcast_to(top[None, :, side], shape)
            stats[:, pl.ds(lines + line, 1), :] = jnp.broadcast_to(total[None, :, side], shape)
        return carry

    lax.fori_loop(0, powers.shape[1] // width, column, 0, unroll=2)


def scores_of(at, held, prior, refs_t, members):
    rows = prior.shape[1]
    orient, eigen = refs_t.shape
    shapes = [
        ((orient, rows), jnp.float32),
        ((eigen, rows), jnp.bfloat16),
        ((members, 2 * rows // LANES, LANES), jnp.float32),
    ]
    return whole(score_kernel, "scores", (*held, prior, refs_t), shapes, at=at, params=BIG)


def total_kernel(other, outer, at, stats, own, powers, rounded, out, factor, mine):
    width = 256
    eigen, rows = rounded.shape
    peers = out.shape[0]
    share = eigen // (2 * peers)
    lines = rows // LANES
    body = out.shape[1] - out.shape[1] % share
    tops = stats[:, :lines, :]
    top = jnp.max(tops, axis=0)
    total = jnp.sum(stats[:, lines:, :] * jnp.exp(tops - top[None]), axis=0)
    scale = jnp.exp(own[0, :lines, :] - top) / total
    for k in range(lines):
        factor[:, k * LANES : (k + 1) * LANES] = scale[k : k + 1, :]
    core = 1 - at[5] if other else at[5]
    for q in range(peers):
        owner = q % (peers // outer) * outer + q // (peers // outer)
        place = pl.multiple_of((2 * owner + core) * share, share)
        mine[q * share : (q + 1) * share, :] = rounded[pl.ds(place, share), :]
    ones = jnp.ones((16, rows), jnp.bfloat16)

    def orients(step, carry):
        block = powers[pl.ds(pl.multiple_of(step * width, width), width), :]
        weights = (block * factor[...]).astype(jnp.bfloat16)
        totals = lax.dot_general(mine[...], weights, LAST, preferred_element_type=jnp.float32)
        masses = lax.dot_general(ones, weights, LAST, preferred_element_type=jnp.float32)
        for h in range(width // LANES):
            column = step * (width // LANES) + h
            cut = slice(h * LANES, (h + 1) * LANES)
            place = pl.ds(pl.multiple_of(column * share, share), share)
            for q in range(peers):
                out[q, place, :] = totals[q * share : (q + 1) * share, cut]
            mass = jnp.broadcast_to(masses[None, 0:1, cut], (peers, 1, LANES))
            out[:, pl.ds(body + column, 1), :] = mass
        return carry

    lax.fori_loop(0, powers.shape[0] // width, orients, 0, unroll=2)


def totals_of(other, at, stats, sent, powers, rounded, peers):
    eigen, rows = rounded.shape
    orient = powers.shape[0]
    deep = (eigen // (2 * peers) + 1) * (orient // LANES)
    return whole(
        functools.partial(total_kernel, other, lax.axis_size(PEERS[0])),
        "totals",
        (stats, sent, powers, rounded),
        [((peers, deep, LANES), jnp.float32)],
        at=at,
        scratch=[pltpu.VMEM((1, rows), jnp.float32), pltpu.VMEM((eigen // 2, rows), jnp.bfloat16)],
        params=BIG,
    )[0]


def final_kernel(at, parts, refs, out):
    share, orient = out.shape
    both = parts[0]
    for d in range(1, parts.shape[0]):
        both = both + parts[d]
    body = share * (orient // LANES)
    for k in range(orient // LANES):
        cut = slice(k * LANES, (k + 1) * LANES)
        above = both[k * share : (k + 1) * share] + refs[:, cut].astype(jnp.float32)
        out[:, cut] = above / (both[body + k : body + k + 1] + 1.0)


def final_of(at, parts, refs):
    eigen, orient = refs.shape
    share = eigen // (2 * parts.shape[0])
    return pl.pallas_call(
        final_kernel,
        grid_spec=pltpu.PrefetchScalarGridSpec(
            num_scalar_prefetch=1,
            grid=(1,),
            in_specs=[
                pl.BlockSpec(parts.shape, lambda j, at: (0, 0, 0)),
                pl.BlockSpec((share, orient), lambda j, at: (at[6], 0)),
            ],
            out_specs=pl.BlockSpec((share, orient), lambda j, at: (0, 0)),
        ),
        out_shape=jax.ShapeDtypeStruct((share, orient), jnp.float32),
        compiler_params=SMALL,
        name="final",
    )(at, parts, refs)


def swapped(pair, axis):
    size = lax.axis_size(axis)
    with_a = [(i, i ^ 1) for i in range(size)]
    with_b = [(i, (i + (1 if i % 2 else -1)) % size) for i in range(size)]
    return tuple(lax.ppermute(x, axis, p) for x, p in zip(pair, (with_a, with_b)))


def shards(images, phantom, inject_rows, prior_blocks, basis, refs):
    rows = images.shape[1] * images.shape[2]
    flat = images[0].reshape(rows, basis.shape[0])
    p, q = lax.axis_index("yl"), lax.axis_index("zhl")
    at = jnp.stack(
        [
            (1 - p) * 2 + 1 - q,
            (1 - p) * 2 + q,
            p * 2 + 1 - q,
            p * 2 + q,
            lax.axis_index(MEM),
            lax.axis_index("core"),
            lax.axis_index(GRP),
        ]
    ).astype(jnp.int32)
    def block(which):
        return projected(which, inject_rows[0], flat, basis, phantom, 2)

    through = swapped(block(at[0:1]), RING)
    turned = relayed(block(at[2:3]), through)
    kept = block(at[3:4])
    low, high, after = lax.optimization_barrier((*turned, at[1:2]))
    others = swapped((low, high), TALL)
    came = swapped(block(after), RING)
    parts = joined(kept, came, others)
    parts = lax.all_to_all(parts, ALIKE, 0, 0, tiled=True)
    own = lax.all_to_all(summed_copies(parts), ALIKE, 0, 0, tiled=True)
    middle = own.shape[0] // 2
    low, high = swapped((own[:middle], own[middle:]), TALL)
    near = swapped((own[:, :8], own[:, 8:]), RING)
    far = swapped(peeled(low, high), RING)
    powers, rounded, sent = scores_of(
        at,
        (staged_of(at, (own, low, high, *near)), *far),
        prior_blocks[0].reshape(1, rows),
        refs.T,
        lax.axis_size(MEM),
    )
    stats = lax.all_to_all(sent, EVERY, 0, 0, tiled=True)
    sums = (stats, sent, powers, rounded, lax.axis_size(PEERS))
    came = lax.ppermute(totals_of(True, at, *sums), "core", [(0, 1), (1, 0)])
    parts = totals_of(False, at, *sums) + came
    parts = lax.all_to_all(parts, PEERS, 0, 0, tiled=True)
    return final_of(at, parts, refs)


def solution(mesh):
    fine = Mesh(mesh.devices.reshape(4, 2, 2, 4, 2, 2, 2), GRP + MEM)
    placed = (
        P(GRP, None, None, MEM),
        P(GRP, MEM),
        P(GRP, None, None),
        P(GRP, None, None),
        P(MEM, None),
        P(None, MEM),
    )
    return jax.shard_map(
        shards, mesh=fine, in_specs=placed, out_specs=P(GRP, MEM), check_vma=False
    )
```

```python
import functools

import jax
import jax.numpy as jnp
from jax import lax
from jax.experimental import pallas as pl
from jax.experimental.pallas import tpu as pltpu
from jax.sharding import Mesh, PartitionSpec as P

OBLOCK = 256
PRIOR_INCREMENT = 3.0
GRP = ("x", "zl", "core")
RING = ("yh", "yl")
TALL = ("zhh", "zhl")
MEM = RING + TALL
ALIKE = ("yh", "zhh")
EVERY = ("zhl", "zhh", "yl", "yh")
PEERS = ("zl", "x")
LANES = 128
BIG = pltpu.CompilerParams(vmem_limit_bytes=16 << 20)
SMALL = pltpu.CompilerParams(vmem_limit_bytes=8 << 20)
LAST = (((1,), (1,)), ((), ()))


def project_kernel(at, inject, images, basis, phantom, *rest):
    outs, (pixels_in, columns, ghost, sems) = rest[:-4], rest[-4:]
    which = pixels_in.shape[0]
    width = pixels_in.shape[1]
    count = columns.shape[1]
    first = pl.multiple_of(at[0] * count, count)
    loads = [
        pltpu.make_async_copy(basis.at[:, pl.ds(first, count)], columns, sems.at[which]),
        pltpu.make_async_copy(phantom, ghost, sems.at[which + 1]),
    ] + [
        pltpu.make_async_copy(images.at[pl.ds(k * width, width), :], pixels_in.at[k], sems.at[k])
        for k in range(which)
    ]
    for load in loads:
        load.start()
    per_batch = which // inject.shape[0]
    hits = []
    for k in range(which):
        position = (k % per_batch) * width + lax.broadcasted_iota(jnp.int32, (1, width), 1)
        hit = jnp.zeros((1, width), jnp.float32)
        for i in range(inject.shape[1]):
            hit = jnp.where(position == inject[k // per_batch, i], 1.0, hit)
        hits.append(hit)
    loads[0].wait()
    loads[1].wait()
    mine = columns[...].T
    spread = jnp.broadcast_to(ghost[...], (LANES, ghost.shape[1]))
    extra = lax.dot_general(mine, spread, LAST, preferred_element_type=jnp.float32)
    share = count // len(outs)
    for k in range(which):
        loads[2 + k].wait()
        plain = lax.dot_general(mine, pixels_in[k], LAST, preferred_element_type=jnp.float32)
        for c in range(width // LANES):
            cut = slice(c * LANES, (c + 1) * LANES)
            value = plain[:, cut] + extra * hits[k][:, cut]
            for j, out in enumerate(outs):
                out[:, k * width + c * LANES : k * width + (c + 1) * LANES] = value[
                    j * share : (j + 1) * share
                ]


def projected(block, inject, images, basis, phantom, pieces):
    rows, pixels = images.shape
    steps = 2 * inject.shape[0]
    count = basis.shape[1] // 4
    out = jax.ShapeDtypeStruct((count // pieces, rows), jnp.float32)
    inject, images, basis, phantom = (
        pltpu.with_memory_space_constraint(x, pltpu.HBM) for x in (inject, images, basis, phantom)
    )
    found = pl.pallas_call(
        project_kernel,
        grid_spec=pltpu.PrefetchScalarGridSpec(
            num_scalar_prefetch=2,
            grid=(1,),
            in_specs=[pl.BlockSpec(memory_space=pltpu.HBM)] * 3,
            out_specs=[pl.BlockSpec(out.shape, lambda j, at, s: (0, 0))] * pieces,
            scratch_shapes=[
                pltpu.VMEM((steps, rows // steps, pixels), images.dtype),
                pltpu.VMEM((pixels, count), basis.dtype),
                pltpu.VMEM((1, pixels), phantom.dtype),
                pltpu.SemaphoreType.DMA((steps + 2,)),
            ],
        ),
        out_shape=[out] * pieces,
        compiler_params=SMALL,
        name="project",
    )(block, inject, images, basis, phantom)
    return tuple(found)


def whole(kernel, name, operands, shapes, at=None, scratch=(), params=SMALL):
    lead = [] if at is None else [at]
    return pl.pallas_call(
        kernel,
        in_specs=[pl.BlockSpec(memory_space=pltpu.SMEM)] * len(lead)
        + [pl.BlockSpec(memory_space=pltpu.VMEM)] * len(operands),
        out_specs=[pl.BlockSpec(memory_space=pltpu.VMEM)] * len(shapes),
        out_shape=[jax.ShapeDtypeStruct(shape, dtype) for shape, dtype in shapes],
        scratch_shapes=list(scratch),
        compiler_params=params,
        name=name,
    )(*lead, *operands)


def relay_kernel(here_a, here_b, came_a, came_b, low, high):
    members = low.shape[0]
    for side, out in enumerate((low, high)):
        for q in range(members):
            cut = slice((side * members + q) * 8, (side * members + q + 1) * 8)
            out[q, :8, :] = here_a[cut, :] + came_a[cut, :]
            out[q, 8:, :] = here_b[cut, :] + came_b[cut, :]


def relayed(here, came):
    count, rows = here[0].shape
    shape = ((count // 16, 16, rows), jnp.float32)
    return whole(relay_kernel, "relay", (*here, *came), [shape, shape])


def join_kernel(here_a, here_b, came_a, came_b, low, high, out):
    members = low.shape[0]
    for side, other in enumerate((low, high)):
        for q in range(members):
            m = side * members + q
            cut = slice(m * 8, (m + 1) * 8)
            out[m, :8, :] = here_a[cut, :] + came_a[cut, :] + other[q, :8, :]
            out[m, 8:, :] = here_b[cut, :] + came_b[cut, :] + other[q, 8:, :]


def joined(here, came, others):
    count, rows = here[0].shape
    shape = ((count // 8, 16, rows), jnp.float32)
    return whole(join_kernel, "join", (*here, *came, *others), [shape])[0]


def spread_kernel(parts, out):
    width = 256

    def column(j, carry):
        cut = pl.ds(pl.multiple_of(j * width, width), width)
        total = parts[0, :, cut]
        for k in range(1, parts.shape[0]):
            total = total + parts[k, :, cut]
        for k in range(out.shape[0]):
            out[k, :, cut] = total
        return carry

    lax.fori_loop(0, parts.shape[2] // width, column, 0)


def summed_copies(parts):
    return whole(spread_kernel, "spread", (parts,), [(parts.shape, jnp.float32)])[0]


def peel_kernel(low, high, out_a, out_b):
    middle = low.shape[0]
    for offset, source in ((0, low), (middle, high)):
        out_a[offset : offset + middle] = source[:, :8, :]
        out_b[offset : offset + middle] = source[:, 8:, :]


def peeled(low, high):
    members, _, rows = low.shape
    shape = ((2 * members, 8, rows), jnp.float32)
    return whole(peel_kernel, "peel", (low, high), [shape, shape])


def put_block(at, rounded, cut, which, offset, block):
    count = block.shape[0] * block.shape[1]
    place = at[which] * (rounded.shape[0] // 4) + offset
    place = pl.multiple_of(place, rounded.shape[0] // 16)
    rounded[pl.ds(place, count), cut] = block.reshape(count, -1).astype(jnp.bfloat16)


def stage_kernel(at, own, low, high, near_a, near_b, staged):
    width = 256
    half = staged.shape[0] // 8
    quarter = half // 2

    def column(step, carry):
        cut = pl.ds(pl.multiple_of(step * width, width), width)
        put = functools.partial(put_block, at, staged, cut)
        put(0, 0, jnp.zeros((16, 8, width), jnp.float32))
        put(1, 0, near_a[:, :, cut])
        put(1, half, near_b[:, :, cut])
        for offset, source in ((0, low), (quarter, high)):
            put(2, offset, source[:, :8, cut])
            put(2, half + offset, source[:, 8:, cut])
        put(3, 0, own[:, :8, cut])
        put(3, half, own[:, 8:, cut])
        return carry

    lax.fori_loop(0, staged.shape[1] // width, column, 0)


def staged_of(at, held):
    members, high, rows = held[0].shape
    shape = ((members * high * 4, rows), jnp.bfloat16)
    return whole(stage_kernel, "stage", held, [shape], at=at)[0]


def score_kernel(at, staged, far_a, far_b, prior, refs_t, powers, rounded, stats):
    width = 256
    orient, eigen = refs_t.shape
    lines = stats.shape[1] // 2

    def column(step, carry):
        cut = pl.ds(pl.multiple_of(step * width, width), width)
        rounded[:, cut] = staged[:, cut]
        put_block(at, rounded, cut, 0, 0, far_a[:, :, cut])
        put_block(at, rounded, cut, 0, eigen // 8, far_b[:, :, cut])
        scores = jnp.dot(refs_t[...], rounded[:, cut], preferred_element_type=jnp.float32)
        block = prior[:, cut] - at[4] * (orient // OBLOCK)
        parts = [
            (scores[k * OBLOCK : (k + 1) * OBLOCK], jnp.where(block == k, PRIOR_INCREMENT, 0.0))
            for k in range(orient // OBLOCK)
        ]
        tops = [jnp.max(part, axis=0, keepdims=True) + bonus for part, bonus in parts]
        top = tops[0]
        for other in tops[1:]:
            top = jnp.maximum(top, other)
        total = jnp.zeros_like(top)
        for k, (part, bonus) in enumerate(parts):
            power = jnp.exp(part - (top - bonus))
            powers[k * OBLOCK : (k + 1) * OBLOCK, cut] = power
            total = total + jnp.sum(power, axis=0, keepdims=True)
        for h in range(width // LANES):
            line = step * (width // LANES) + h
            side = slice(h * LANES, (h + 1) * LANES)
            shape = (stats.shape[0], 1, LANES)
            stats[:, pl.ds(line, 1), :] = jnp.broadcast_to(top[None, :, side], shape)
            stats[:, pl.ds(lines + line, 1), :] = jnp.broadcast_to(total[None, :, side], shape)
        return carry

    lax.fori_loop(0, powers.shape[1] // width, column, 0, unroll=True)


def scores_of(at, held, prior, refs_t, members):
    rows = prior.shape[1]
    orient, eigen = refs_t.shape
    shapes = [
        ((orient, rows), jnp.float32),
        ((eigen, rows), jnp.bfloat16),
        ((members, 2 * rows // LANES, LANES), jnp.float32),
    ]
    return whole(score_kernel, "scores", (*held, prior, refs_t), shapes, at=at, params=BIG)


def total_kernel(other, outer, at, stats, own, powers, rounded, out, factor, mine):
    width = 256
    eigen, rows = rounded.shape
    peers = out.shape[0]
    share = eigen // (2 * peers)
    lines = rows // LANES
    body = out.shape[1] - out.shape[1] % share
    tops = stats[:, :lines, :]
    top = jnp.max(tops, axis=0)
    total = jnp.sum(stats[:, lines:, :] * jnp.exp(tops - top[None]), axis=0)
    scale = jnp.exp(own[0, :lines, :] - top) / total
    for k in range(lines):
        factor[:, k * LANES : (k + 1) * LANES] = scale[k : k + 1, :]
    core = 1 - at[5] if other else at[5]
    for q in range(peers):
        owner = q % (peers // outer) * outer + q // (peers // outer)
        place = pl.multiple_of((2 * owner + core) * share, share)
        mine[q * share : (q + 1) * share, :] = rounded[pl.ds(place, share), :]
    ones = jnp.ones((16, rows), jnp.bfloat16)

    def orients(step, carry):
        block = powers[pl.ds(pl.multiple_of(step * width, width), width), :]
        weights = (block * factor[...]).astype(jnp.bfloat16)
        totals = lax.dot_general(mine[...], weights, LAST, preferred_element_type=jnp.float32)
        masses = lax.dot_general(ones, weights, LAST, preferred_element_type=jnp.float32)
        for h in range(width // LANES):
            column = step * (width // LANES) + h
            cut = slice(h * LANES, (h + 1) * LANES)
            place = pl.ds(pl.multiple_of(column * share, share), share)
            for q in range(peers):
                out[q, place, :] = totals[q * share : (q + 1) * share, cut]
            mass = jnp.broadcast_to(masses[None, 0:1, cut], (peers, 1, LANES))
            out[:, pl.ds(body + column, 1), :] = mass
        return carry

    lax.fori_loop(0, powers.shape[0] // width, orients, 0, unroll=True)


def totals_of(other, at, stats, sent, powers, rounded, peers):
    eigen, rows = rounded.shape
    orient = powers.shape[0]
    deep = (eigen // (2 * peers) + 1) * (orient // LANES)
    return whole(
        functools.partial(total_kernel, other, lax.axis_size(PEERS[0])),
        "totals",
        (stats, sent, powers, rounded),
        [((peers, deep, LANES), jnp.float32)],
        at=at,
        scratch=[pltpu.VMEM((1, rows), jnp.float32), pltpu.VMEM((eigen // 2, rows), jnp.bfloat16)],
        params=BIG,
    )[0]


def final_kernel(at, parts, refs, out):
    share, orient = out.shape
    both = parts[0]
    for d in range(1, parts.shape[0]):
        both = both + parts[d]
    body = share * (orient // LANES)
    for k in range(orient // LANES):
        cut = slice(k * LANES, (k + 1) * LANES)
        above = both[k * share : (k + 1) * share] + refs[:, cut].astype(jnp.float32)
        out[:, cut] = above / (both[body + k : body + k + 1] + 1.0)


def final_of(at, parts, refs):
    eigen, orient = refs.shape
    share = eigen // (2 * parts.shape[0])
    return pl.pallas_call(
        final_kernel,
        grid_spec=pltpu.PrefetchScalarGridSpec(
            num_scalar_prefetch=1,
            grid=(1,),
            in_specs=[
                pl.BlockSpec(parts.shape, lambda j, at: (0, 0, 0)),
                pl.BlockSpec((share, orient), lambda j, at: (at[6], 0)),
            ],
            out_specs=pl.BlockSpec((share, orient), lambda j, at: (0, 0)),
        ),
        out_shape=jax.ShapeDtypeStruct((share, orient), jnp.float32),
        compiler_params=SMALL,
        name="final",
    )(at, parts, refs)


def swapped(pair, axis):
    size = lax.axis_size(axis)
    with_a = [(i, i ^ 1) for i in range(size)]
    with_b = [(i, (i + (1 if i % 2 else -1)) % size) for i in range(size)]
    return tuple(lax.ppermute(x, axis, p) for x, p in zip(pair, (with_a, with_b)))


def shards(images, phantom, inject_rows, prior_blocks, basis, refs):
    rows = images.shape[1] * images.shape[2]
    flat = images[0].reshape(rows, basis.shape[0])
    p, q = lax.axis_index("yl"), lax.axis_index("zhl")
    at = jnp.stack(
        [
            (1 - p) * 2 + 1 - q,
            (1 - p) * 2 + q,
            p * 2 + 1 - q,
            p * 2 + q,
            lax.axis_index(MEM),
            lax.axis_index("core"),
            lax.axis_index(GRP),
        ]
    ).astype(jnp.int32)
    def block(which):
        return projected(which, inject_rows[0], flat, basis, phantom, 2)

    through = swapped(block(at[0:1]), RING)
    turned = relayed(block(at[2:3]), through)
    kept = block(at[3:4])
    low, high, after = lax.optimization_barrier((*turned, at[1:2]))
    others = swapped((low, high), TALL)
    came = swapped(block(after), RING)
    parts = joined(kept, came, others)
    parts = lax.all_to_all(parts, ALIKE, 0, 0, tiled=True)
    own = lax.all_to_all(summed_copies(parts), ALIKE, 0, 0, tiled=True)
    middle = own.shape[0] // 2
    low, high = swapped((own[:middle], own[middle:]), TALL)
    near = swapped((own[:, :8], own[:, 8:]), RING)
    far = swapped(peeled(low, high), RING)
    powers, rounded, sent = scores_of(
        at,
        (staged_of(at, (own, low, high, *near)), *far),
        prior_blocks[0].reshape(1, rows),
        refs.T,
        lax.axis_size(MEM),
    )
    stats = lax.all_to_all(sent, EVERY, 0, 0, tiled=True)
    sums = (stats, sent, powers, rounded, lax.axis_size(PEERS))
    came = lax.ppermute(totals_of(True, at, *sums), "core", [(0, 1), (1, 0)])
    parts = totals_of(False, at, *sums) + came
    parts = lax.all_to_all(parts, PEERS, 0, 0, tiled=True)
    return final_of(at, parts, refs)


def solution(mesh):
    fine = Mesh(mesh.devices.reshape(4, 2, 2, 4, 2, 2, 2), GRP + MEM)
    placed = (
        P(GRP, None, None, MEM),
        P(GRP, MEM),
        P(GRP, None, None),
        P(GRP, None, None),
        P(MEM, None),
        P(None, MEM),
    )
    return jax.shard_map(
        shards, mesh=fine, in_specs=placed, out_specs=P(GRP, MEM), check_vma=False
    )
```

```python
import functools

import jax
import jax.numpy as jnp
from jax import lax
from jax.experimental import pallas as pl
from jax.experimental.pallas import tpu as pltpu
from jax.sharding import Mesh, PartitionSpec as P

OBLOCK = 256
PRIOR_INCREMENT = 3.0
GRP = ("x", "zl", "core")
RING = ("yh", "yl")
TALL = ("zhh", "zhl")
MEM = RING + TALL
ALIKE = ("yh", "zhh")
EVERY = ("zhl", "zhh", "yl", "yh")
PEERS = ("zl", "x")
LANES = 128
BIG = pltpu.CompilerParams(vmem_limit_bytes=16 << 20)
SMALL = pltpu.CompilerParams(vmem_limit_bytes=8 << 20)
LAST = (((1,), (1,)), ((), ()))


def project_kernel(at, inject, images, basis, phantom, *rest):
    outs, (pixels_in, columns, ghost, sems) = rest[:-4], rest[-4:]
    which = pixels_in.shape[0]
    width = pixels_in.shape[1]
    count = columns.shape[1]
    first = pl.multiple_of(at[0] * count, count)
    loads = [
        pltpu.make_async_copy(basis.at[:, pl.ds(first, count)], columns, sems.at[which]),
        pltpu.make_async_copy(phantom, ghost, sems.at[which + 1]),
    ] + [
        pltpu.make_async_copy(images.at[pl.ds(k * width, width), :], pixels_in.at[k], sems.at[k])
        for k in range(which)
    ]
    for load in loads:
        load.start()
    per_batch = which // inject.shape[0]
    hits = []
    for k in range(which):
        position = (k % per_batch) * width + lax.broadcasted_iota(jnp.int32, (1, width), 1)
        hit = jnp.zeros((1, width), jnp.float32)
        for i in range(inject.shape[1]):
            hit = jnp.where(position == inject[k // per_batch, i], 1.0, hit)
        hits.append(hit)
    loads[0].wait()
    loads[1].wait()
    mine = columns[...].T
    spread = jnp.broadcast_to(ghost[...], (LANES, ghost.shape[1]))
    extra = lax.dot_general(mine, spread, LAST, preferred_element_type=jnp.float32)
    share = count // len(outs)
    for k in range(which):
        loads[2 + k].wait()
        plain = lax.dot_general(mine, pixels_in[k], LAST, preferred_element_type=jnp.float32)
        for c in range(width // LANES):
            cut = slice(c * LANES, (c + 1) * LANES)
            value = plain[:, cut] + extra * hits[k][:, cut]
            for j, out in enumerate(outs):
                out[:, k * width + c * LANES : k * width + (c + 1) * LANES] = value[
                    j * share : (j + 1) * share
                ]


def projected(block, inject, images, basis, phantom, pieces):
    rows, pixels = images.shape
    steps = 2 * inject.shape[0]
    count = basis.shape[1] // 4
    out = jax.ShapeDtypeStruct((count // pieces, rows), jnp.float32)
    inject, images, basis, phantom = (
        pltpu.with_memory_space_constraint(x, pltpu.HBM) for x in (inject, images, basis, phantom)
    )
    found = pl.pallas_call(
        project_kernel,
        grid_spec=pltpu.PrefetchScalarGridSpec(
            num_scalar_prefetch=2,
            grid=(1,),
            in_specs=[pl.BlockSpec(memory_space=pltpu.HBM)] * 3,
            out_specs=[pl.BlockSpec(out.shape, lambda j, at, s: (0, 0))] * pieces,
            scratch_shapes=[
                pltpu.VMEM((steps, rows // steps, pixels), images.dtype),
                pltpu.VMEM((pixels, count), basis.dtype),
                pltpu.VMEM((1, pixels), phantom.dtype),
                pltpu.SemaphoreType.DMA((steps + 2,)),
            ],
        ),
        out_shape=[out] * pieces,
        compiler_params=SMALL,
        name="project",
    )(block, inject, images, basis, phantom)
    return tuple(found)


def whole(kernel, name, operands, shapes, at=None, scratch=(), params=SMALL):
    lead = [] if at is None else [at]
    return pl.pallas_call(
        kernel,
        in_specs=[pl.BlockSpec(memory_space=pltpu.SMEM)] * len(lead)
        + [pl.BlockSpec(memory_space=pltpu.VMEM)] * len(operands),
        out_specs=[pl.BlockSpec(memory_space=pltpu.VMEM)] * len(shapes),
        out_shape=[jax.ShapeDtypeStruct(shape, dtype) for shape, dtype in shapes],
        scratch_shapes=list(scratch),
        compiler_params=params,
        name=name,
    )(*lead, *operands)


def relay_kernel(here_a, here_b, came_a, came_b, low, high):
    members = low.shape[0]
    for side, out in enumerate((low, high)):
        for q in range(members):
            cut = slice((side * members + q) * 8, (side * members + q + 1) * 8)
            out[q, :8, :] = here_a[cut, :] + came_a[cut, :]
            out[q, 8:, :] = here_b[cut, :] + came_b[cut, :]


def relayed(here, came):
    count, rows = here[0].shape
    shape = ((count // 16, 16, rows), jnp.float32)
    return whole(relay_kernel, "relay", (*here, *came), [shape, shape])


def join_kernel(here_a, here_b, came_a, came_b, low, high, out):
    members = low.shape[0]
    for side, other in enumerate((low, high)):
        for q in range(members):
            m = side * members + q
            cut = slice(m * 8, (m + 1) * 8)
            out[m, :8, :] = here_a[cut, :] + came_a[cut, :] + other[q, :8, :]
            out[m, 8:, :] = here_b[cut, :] + came_b[cut, :] + other[q, 8:, :]


def joined(here, came, others):
    count, rows = here[0].shape
    shape = ((count // 8, 16, rows), jnp.float32)
    return whole(join_kernel, "join", (*here, *came, *others), [shape])[0]


def spread_kernel(parts, out):
    width = 256

    def column(j, carry):
        cut = pl.ds(pl.multiple_of(j * width, width), width)
        total = parts[0, :, cut]
        for k in range(1, parts.shape[0]):
            total = total + parts[k, :, cut]
        for k in range(out.shape[0]):
            out[k, :, cut] = total
        return carry

    lax.fori_loop(0, parts.shape[2] // width, column, 0, unroll=True)


def summed_copies(parts):
    return whole(spread_kernel, "spread", (parts,), [(parts.shape, jnp.float32)])[0]


def peel_kernel(low, high, out_a, out_b):
    middle = low.shape[0]
    for offset, source in ((0, low), (middle, high)):
        out_a[offset : offset + middle] = source[:, :8, :]
        out_b[offset : offset + middle] = source[:, 8:, :]


def peeled(low, high):
    members, _, rows = low.shape
    shape = ((2 * members, 8, rows), jnp.float32)
    return whole(peel_kernel, "peel", (low, high), [shape, shape])


def put_block(at, rounded, cut, which, offset, block):
    count = block.shape[0] * block.shape[1]
    place = at[which] * (rounded.shape[0] // 4) + offset
    place = pl.multiple_of(place, rounded.shape[0] // 16)
    rounded[pl.ds(place, count), cut] = block.reshape(count, -1).astype(jnp.bfloat16)


def stage_kernel(at, own, low, high, near_a, near_b, staged):
    width = 256
    half = staged.shape[0] // 8
    quarter = half // 2

    def column(step, carry):
        cut = pl.ds(pl.multiple_of(step * width, width), width)
        put = functools.partial(put_block, at, staged, cut)
        put(0, 0, jnp.zeros((16, 8, width), jnp.float32))
        put(1, 0, near_a[:, :, cut])
        put(1, half, near_b[:, :, cut])
        for offset, source in ((0, low), (quarter, high)):
            put(2, offset, source[:, :8, cut])
            put(2, half + offset, source[:, 8:, cut])
        put(3, 0, own[:, :8, cut])
        put(3, half, own[:, 8:, cut])
        return carry

    lax.fori_loop(0, staged.shape[1] // width, column, 0, unroll=True)


def staged_of(at, held):
    members, high, rows = held[0].shape
    shape = ((members * high * 4, rows), jnp.bfloat16)
    return whole(stage_kernel, "stage", held, [shape], at=at)[0]


def score_kernel(at, staged, far_a, far_b, prior, refs_t, powers, rounded, stats):
    width = 256
    orient, eigen = refs_t.shape
    lines = stats.shape[1] // 2

    def column(step, carry):
        cut = pl.ds(pl.multiple_of(step * width, width), width)
        rounded[:, cut] = staged[:, cut]
        put_block(at, rounded, cut, 0, 0, far_a[:, :, cut])
        put_block(at, rounded, cut, 0, eigen // 8, far_b[:, :, cut])
        scores = jnp.dot(refs_t[...], rounded[:, cut], preferred_element_type=jnp.float32)
        block = prior[:, cut] - at[4] * (orient // OBLOCK)
        parts = [
            (scores[k * OBLOCK : (k + 1) * OBLOCK], jnp.where(block == k, PRIOR_INCREMENT, 0.0))
            for k in range(orient // OBLOCK)
        ]
        tops = [jnp.max(part, axis=0, keepdims=True) + bonus for part, bonus in parts]
        top = tops[0]
        for other in tops[1:]:
            top = jnp.maximum(top, other)
        total = jnp.zeros_like(top)
        for k, (part, bonus) in enumerate(parts):
            power = jnp.exp(part - (top - bonus))
            powers[k * OBLOCK : (k + 1) * OBLOCK, cut] = power
            total = total + jnp.sum(power, axis=0, keepdims=True)
        for h in range(width // LANES):
            line = step * (width // LANES) + h
            side = slice(h * LANES, (h + 1) * LANES)
            shape = (stats.shape[0], 1, LANES)
            stats[:, pl.ds(line, 1), :] = jnp.broadcast_to(top[None, :, side], shape)
            stats[:, pl.ds(lines + line, 1), :] = jnp.broadcast_to(total[None, :, side], shape)
        return carry

    lax.fori_loop(0, powers.shape[1] // width, column, 0, unroll=True)


def scores_of(at, held, prior, refs_t, members):
    rows = prior.shape[1]
    orient, eigen = refs_t.shape
    shapes = [
        ((orient, rows), jnp.float32),
        ((eigen, rows), jnp.bfloat16),
        ((members, 2 * rows // LANES, LANES), jnp.float32),
    ]
    return whole(score_kernel, "scores", (*held, prior, refs_t), shapes, at=at, params=BIG)


def total_kernel(other, outer, at, stats, own, powers, rounded, out, factor, mine):
    width = 256
    eigen, rows = rounded.shape
    peers = out.shape[0]
    share = eigen // (2 * peers)
    lines = rows // LANES
    body = out.shape[1] - out.shape[1] % share
    tops = stats[:, :lines, :]
    top = jnp.max(tops, axis=0)
    total = jnp.sum(stats[:, lines:, :] * jnp.exp(tops - top[None]), axis=0)
    scale = jnp.exp(own[0, :lines, :] - top) / total
    for k in range(lines):
        factor[:, k * LANES : (k + 1) * LANES] = scale[k : k + 1, :]
    core = 1 - at[5] if other else at[5]
    for q in range(peers):
        owner = q % (peers // outer) * outer + q // (peers // outer)
        place = pl.multiple_of((2 * owner + core) * share, share)
        mine[q * share : (q + 1) * share, :] = rounded[pl.ds(place, share), :]
    ones = jnp.ones((16, rows), jnp.bfloat16)

    def orients(step, carry):
        block = powers[pl.ds(pl.multiple_of(step * width, width), width), :]
        weights = (block * factor[...]).astype(jnp.bfloat16)
        totals = lax.dot_general(mine[...], weights, LAST, preferred_element_type=jnp.float32)
        masses = lax.dot_general(ones, weights, LAST, preferred_element_type=jnp.float32)
        for h in range(width // LANES):
            column = step * (width // LANES) + h
            cut = slice(h * LANES, (h + 1) * LANES)
            place = pl.ds(pl.multiple_of(column * share, share), share)
            for q in range(peers):
                out[q, place, :] = totals[q * share : (q + 1) * share, cut]
            mass = jnp.broadcast_to(masses[None, 0:1, cut], (peers, 1, LANES))
            out[:, pl.ds(body + column, 1), :] = mass
        return carry

    lax.fori_loop(0, powers.shape[0] // width, orients, 0, unroll=True)


def totals_of(other, at, stats, sent, powers, rounded, peers):
    eigen, rows = rounded.shape
    orient = powers.shape[0]
    deep = (eigen // (2 * peers) + 1) * (orient // LANES)
    return whole(
        functools.partial(total_kernel, other, lax.axis_size(PEERS[0])),
        "totals",
        (stats, sent, powers, rounded),
        [((peers, deep, LANES), jnp.float32)],
        at=at,
        scratch=[pltpu.VMEM((1, rows), jnp.float32), pltpu.VMEM((eigen // 2, rows), jnp.bfloat16)],
        params=BIG,
    )[0]


def final_kernel(at, parts, refs, out):
    share, orient = out.shape
    both = parts[0]
    for d in range(1, parts.shape[0]):
        both = both + parts[d]
    body = share * (orient // LANES)
    for k in range(orient // LANES):
        cut = slice(k * LANES, (k + 1) * LANES)
        above = both[k * share : (k + 1) * share] + refs[:, cut].astype(jnp.float32)
        out[:, cut] = above / (both[body + k : body + k + 1] + 1.0)


def final_of(at, parts, refs):
    eigen, orient = refs.shape
    share = eigen // (2 * parts.shape[0])
    return pl.pallas_call(
        final_kernel,
        grid_spec=pltpu.PrefetchScalarGridSpec(
            num_scalar_prefetch=1,
            grid=(1,),
            in_specs=[
                pl.BlockSpec(parts.shape, lambda j, at: (0, 0, 0)),
                pl.BlockSpec((share, orient), lambda j, at: (at[6], 0)),
            ],
            out_specs=pl.BlockSpec((share, orient), lambda j, at: (0, 0)),
        ),
        out_shape=jax.ShapeDtypeStruct((share, orient), jnp.float32),
        compiler_params=SMALL,
        name="final",
    )(at, parts, refs)


def swapped(pair, axis):
    size = lax.axis_size(axis)
    with_a = [(i, i ^ 1) for i in range(size)]
    with_b = [(i, (i + (1 if i % 2 else -1)) % size) for i in range(size)]
    return tuple(lax.ppermute(x, axis, p) for x, p in zip(pair, (with_a, with_b)))


def shards(images, phantom, inject_rows, prior_blocks, basis, refs):
    rows = images.shape[1] * images.shape[2]
    flat = images[0].reshape(rows, basis.shape[0])
    p, q = lax.axis_index("yl"), lax.axis_index("zhl")
    at = jnp.stack(
        [
            (1 - p) * 2 + 1 - q,
            (1 - p) * 2 + q,
            p * 2 + 1 - q,
            p * 2 + q,
            lax.axis_index(MEM),
            lax.axis_index("core"),
            lax.axis_index(GRP),
        ]
    ).astype(jnp.int32)
    def block(which):
        return projected(which, inject_rows[0], flat, basis, phantom, 2)

    through = swapped(block(at[0:1]), RING)
    turned = relayed(block(at[2:3]), through)
    kept = block(at[3:4])
    low, high, after = lax.optimization_barrier((*turned, at[1:2]))
    others = swapped((low, high), TALL)
    came = swapped(block(after), RING)
    parts = joined(kept, came, others)
    parts = lax.all_to_all(parts, ALIKE, 0, 0, tiled=True)
    own = lax.all_to_all(summed_copies(parts), ALIKE, 0, 0, tiled=True)
    middle = own.shape[0] // 2
    low, high = swapped((own[:middle], own[middle:]), TALL)
    near = swapped((own[:, :8], own[:, 8:]), RING)
    far = swapped(peeled(low, high), RING)
    powers, rounded, sent = scores_of(
        at,
        (staged_of(at, (own, low, high, *near)), *far),
        prior_blocks[0].reshape(1, rows),
        refs.T,
        lax.axis_size(MEM),
    )
    stats = lax.all_to_all(sent, EVERY, 0, 0, tiled=True)
    sums = (stats, sent, powers, rounded, lax.axis_size(PEERS))
    came = lax.ppermute(totals_of(True, at, *sums), "core", [(0, 1), (1, 0)])
    parts = totals_of(False, at, *sums) + came
    parts = lax.all_to_all(parts, PEERS, 0, 0, tiled=True)
    return final_of(at, parts, refs)


def solution(mesh):
    fine = Mesh(mesh.devices.reshape(4, 2, 2, 4, 2, 2, 2), GRP + MEM)
    placed = (
        P(GRP, None, None, MEM),
        P(GRP, MEM),
        P(GRP, None, None),
        P(GRP, None, None),
        P(MEM, None),
        P(None, MEM),
    )
    return jax.shard_map(
        shards, mesh=fine, in_specs=placed, out_specs=P(GRP, MEM), check_vma=False
    )
```
